256 devices in a mesh: patch: 64 (over y, x, z_hi), head: 4 (over z_lo, core).
Axes of the slice: x: 4, y: 4, z: 8 (z_hi: 4, z_lo: 2; z = z_hi * 2 + z_lo), core: 2. Of those that a mesh axis runs over, the one named last changes fastest.
Arguments:
- fresh_qkv: bfloat16 [32768, 3, 3072], P('patch', None, 'head'), may hold values from -12 to 12
- kv_cache: bfloat16 [32768, 2, 3072], P('patch', None, 'head'), may hold values from -8 to 8
- hidden: bfloat16 [32768, 3072], P('patch'), may hold values from -6 to 6
- refresh: int32 [4], replicated, may hold values from 0 to 63, as said below
- out_weight: bfloat16 [3072, 3072], P('head'), may hold values from -0.109375 to 0.109375
- final_weight: bfloat16 [3072, 64], replicated, may hold values from -0.109375 to 0.109375
- final_bias: float32 [64], replicated, may hold values from -3 to 3
- gate_scale: float32 [3072], replicated, may hold values from 0.1 to 1.9
- noise_level: float32 [1], replicated, may hold values from 0.15 to 0.35
- noisy_latent: bfloat16 [128, 16, 1024], P('patch'), may hold values from -6 to 6
- velocity_cache: bfloat16 [128, 16, 1024], P('patch'), may hold values from -6 to 6
- conv_weight: bfloat16 [512, 3, 3, 16], P('head'), may hold values from -0.5 to 0.5
- conv_bias: float32 [512], P('head'), may hold values from -3 to 3
Outputs:
- decoded: bfloat16 [128, 512, 1024], P('patch', 'head')
The draws below stay inside these ranges and needn't reach their ends.
Inputs may be any that keep to these rules, and one draw needn't show every extreme that they name: 4 distinct patch indices; refresh[1] is 63.
All inputs are finite; a program needn't handle non-finite values.
Results may differ from the reference program's by a relative error of at most 0.0044.
The reference program's roundings to bfloat16 on the way count: a program that leaves them out, or rounds other values in their place, can miss the bound.
Values may be sent and summed in bfloat16 or wider, within the bound.
No kernel may reach another device: no remote copies, remote signals or barrier semaphores. Data moves between devices by JAX's collectives and lax.ppermute only.
A program may use at most 128 MiB of HBM per device.

```python
import math
import jax
import jax.numpy as jnp
from jax import lax

D = 3072
HEADS = 24
HEAD_DIM = 128
LAT_CH = 16
CONV_CH = 512
GW = 512
ROWS_DEV = 1
REFRESH = 4
PATCH_VEC = 64
TOK_DEV = 512
PATCHES = 64
TOKENS = 32768
NQ = 2048
LROWS = 128
LW = 1024


def draw_fresh_qkv(key, part):
    first_key = jax.random.fold_in(key, 0)
    background = jnp.clip(2.0 * jax.random.normal(first_key, (TOKENS, 3, D), jnp.float32), -8.0, 8.0)
    return background.astype(jnp.bfloat16)


def draw_refresh(key, part):
    others = jax.random.permutation(key, PATCHES - 1)[:REFRESH - 1].astype(jnp.int32)
    last_patch = jnp.full((1,), PATCHES - 1, dtype=jnp.int32)
    return jnp.concatenate([others[:1], last_patch, others[1:]], axis=0)


def levels(rng, shape, cuts, low, high):
    def one(dim, shards_of):
        heights = jax.random.uniform(jax.random.fold_in(jax.random.fold_in(rng, 6), dim), (shards_of,), jnp.float32, low / len(cuts), high / len(cuts))
        return jnp.repeat(jnp.exp(heights), shape[dim] // shards_of).reshape((-1,) + (1,) * (len(shape) - dim - 1))

    gain = one(*cuts[0])
    for cut in cuts[1:]:
        gain = gain * one(*cut)
    return gain


def bell_draw(stream_key, dims, scale, limit, shards=(), held_as=jnp.bfloat16):
    gain = levels(stream_key, dims, shards, -0.22, 0.18) if shards else 1.0
    result = jax.random.normal(stream_key, dims, jnp.float32) * scale * gain
    return jnp.minimum(jnp.maximum(result, -limit), limit).astype(held_as)


def setup_inputs(seed: int = 0) -> dict:
    key_list = jax.random.split(jax.random.key(seed), 14)
    fresh_qkv = draw_fresh_qkv(jax.random.fold_in(key_list[13], 71), 0)
    kv_cache = bell_draw(key_list[1], (TOKENS, 2, D), 2.0, 8.0, ((0, 64), (2, 4)))
    hidden = bell_draw(key_list[2], (TOKENS, D), 1.0, 6.0, ((0, 64),))
    refresh = draw_refresh(jax.random.fold_in(key_list[13], 71), 0)
    out_weight = bell_draw(key_list[4], (D, D), D ** -0.5, 0.109375, ((0, 4),))
    final_weight = bell_draw(key_list[5], (D, PATCH_VEC), D ** -0.5, 0.109375)
    final_bias = bell_draw(key_list[6], (PATCH_VEC,), 0.5, 3.0, (), jnp.float32)
    gate_scale = jnp.clip(1.0 + 0.18 * jax.random.normal(key_list[7], (D,), jnp.float32), 0.1, 1.9)
    noise_level = jnp.clip(jax.random.uniform(key_list[8], (1,), jnp.float32, 0.15, 0.35), 0.15, 0.35)
    noisy_latent = bell_draw(key_list[9], (LROWS, LAT_CH, LW), 1.0, 6.0, ((0, 64),))
    velocity_cache = bell_draw(key_list[10], (LROWS, LAT_CH, LW), 1.0, 6.0, ((0, 64),))
    conv_weight = bell_draw(key_list[11], (CONV_CH, 3, 3, LAT_CH), (9 * LAT_CH) ** -0.5, 0.5, ((0, 4),))
    conv_bias = bell_draw(key_list[12], (CONV_CH,), 0.5, 3.0, ((0, 4),), jnp.float32)
    return dict(fresh_qkv=fresh_qkv, kv_cache=kv_cache, hidden=hidden, refresh=refresh, out_weight=out_weight, final_weight=final_weight, final_bias=final_bias, gate_scale=gate_scale, noise_level=noise_level, noisy_latent=noisy_latent, velocity_cache=velocity_cache, conv_weight=conv_weight, conv_bias=conv_bias)


def reference(fresh_qkv, kv_cache, hidden, refresh, out_weight, final_weight, final_bias, gate_scale, noise_level, noisy_latent, velocity_cache, conv_weight, conv_bias):
    patch_ids = jnp.arange(PATCHES, dtype=jnp.int32)
    chosen = jnp.any(patch_ids[:, None] == refresh[None, :], axis=1)
    token_chosen = jnp.repeat(chosen, TOK_DEV)
    key_rows = jnp.where(token_chosen[:, None], fresh_qkv[:, 1], kv_cache[:, 0])
    value_rows = jnp.where(token_chosen[:, None], fresh_qkv[:, 2], kv_cache[:, 1])
    queries = fresh_qkv.reshape(PATCHES, TOK_DEV, 3, D)[refresh][:, :, 0].reshape(NQ, D)
    block_rows = math.gcd(NQ, 512)
    score_scale = 1.0 / math.sqrt(HEAD_DIM)

    def one_head(head_number):
        head_start = (head_number * HEAD_DIM).astype(jnp.int32)
        head_queries = lax.dynamic_slice_in_dim(queries, head_start, HEAD_DIM, 1)
        head_keys = lax.dynamic_slice_in_dim(key_rows, head_start, HEAD_DIM, 1)
        head_values = lax.dynamic_slice_in_dim(value_rows, head_start, HEAD_DIM, 1)

        def one_block(block_number):
            row_start = (block_number * block_rows).astype(jnp.int32)
            row_block = lax.dynamic_slice_in_dim(head_queries, row_start, block_rows, 0)
            scores = jnp.dot(row_block, head_keys.T, preferred_element_type=jnp.float32) * score_scale
            row_max = lax.optimization_barrier(jnp.max(scores, axis=1, keepdims=True))
            exp_scores = jnp.exp(scores - row_max)
            denominator = lax.optimization_barrier(jnp.sum(exp_scores, axis=1, keepdims=True))
            numerator = jnp.dot(exp_scores.astype(jnp.bfloat16), head_values, preferred_element_type=jnp.float32)
            return numerator / denominator
        return lax.map(one_block, jnp.arange(NQ // block_rows, dtype=jnp.int32)).reshape(NQ, HEAD_DIM)
    attention = lax.map(one_head, jnp.arange(HEADS, dtype=jnp.int32))
    attention = jnp.transpose(attention, (1, 0, 2)).reshape(NQ, D)
    projected = jnp.dot(attention, out_weight.astype(jnp.float32), precision=lax.Precision.HIGHEST)
    hidden_rows = hidden.reshape(PATCHES, TOK_DEV, D)[refresh].reshape(NQ, D)
    velocity_fresh = jnp.dot(hidden_rows, final_weight, preferred_element_type=jnp.float32) + final_bias
    velocity_fresh = velocity_fresh + jnp.dot(gate_scale[None, :] * projected, final_weight.astype(jnp.float32), precision=lax.Precision.HIGHEST)
    fresh_field = velocity_fresh.reshape(REFRESH, ROWS_DEV, GW, LAT_CH, 2, 2)
    fresh_field = jnp.transpose(fresh_field, (0, 1, 4, 3, 2, 5)).reshape(REFRESH, 2 * ROWS_DEV, LAT_CH, LW)
    velocity_field = velocity_cache.astype(jnp.float32).reshape(PATCHES, 2 * ROWS_DEV, LAT_CH, LW)
    velocity_field = velocity_field.at[refresh].set(fresh_field).reshape(LROWS, LAT_CH, LW)
    latent = noisy_latent.astype(jnp.float32) - noise_level[0] * velocity_field
    decoder_in = (latent / 0.3611 + 0.1159).astype(jnp.bfloat16)
    padded = jnp.pad(decoder_in, ((1, 1), (0, 0), (1, 1)))
    stencil = jnp.stack([padded[row_shift:row_shift + LROWS, :, col_shift:col_shift + LW] for row_shift in range(3) for col_shift in range(3)], axis=1)
    stencil = stencil.reshape(LROWS, 9 * LAT_CH, LW)
    kernel = conv_weight.reshape(CONV_CH, 9 * LAT_CH)
    decoded = jnp.einsum('oc,rcw->row', kernel.astype(jnp.float32), stencil.astype(jnp.float32))
    decoded = decoded + conv_bias[None, :, None]
    return decoded.astype(jnp.bfloat16)
```

```python
import functools
import math

import jax
import jax.numpy as jnp
from jax import lax
from jax.experimental import pallas as pl
from jax.experimental.pallas import tpu as pltpu
from jax.sharding import PartitionSpec as P

HEAD_DIM = 128
LAT_CH = 16
PATCHES = 64
SLOTS = 4
HEADS_HERE = 6
HALF = 3
VEC = 64
ROWS = HALF * VEC
PACK = ROWS + 16
KEYS = 512
COLS = 1024
F32 = jnp.float32
BF16 = jnp.bfloat16
STRIDE = {"y": 16, "x": 4, "z": 1}


def coord(patch, axis):
    return (patch // STRIDE[axis]) % 4


def moved(patch, axis, step):
    here = coord(patch, axis)
    return patch + ((here + step) % 4 - here) * STRIDE[axis]


def shift(value, axis, step):
    if step == 0:
        return value
    return lax.ppermute(value, "patch", [(p, moved(p, axis, step)) for p in range(PATCHES)])


def pick(choices, which):
    out = choices[0]
    for k in range(1, 4):
        out = jnp.where(which == k, choices[k], out)
    return out


def cost(flops, moved_bytes, exps=0):
    return pl.CostEstimate(flops=flops, bytes_accessed=moved_bytes, transcendentals=exps)


def pack_lse(block, entries):
    row = lax.broadcasted_iota(jnp.int32, block.shape, 0)
    for h, lse in entries:
        high = lse.astype(BF16).astype(F32)
        rest = lse - high
        mid = rest.astype(BF16).astype(F32)
        low = rest - mid
        for part, value in enumerate((high, mid, low)):
            block = jnp.where(row == part * HALF + h, jnp.broadcast_to(value, block.shape), block)
    return block.astype(BF16)


def attend_kernel(qa_ref, qb_ref, ka_ref, kb_ref, va_ref, vb_ref, oa_ref, ob_ref):
    scale = math.log2(math.e) / math.sqrt(HEAD_DIM)
    h = pl.program_id(0)
    halves = ((qa_ref, ka_ref, va_ref, oa_ref), (qb_ref, kb_ref, vb_ref, ob_ref))
    for q_ref, k_ref, v_ref, o_ref in halves:
        dots = lax.dot_general(
            k_ref[...], q_ref[...], (((1,), (1,)), ((), ())), preferred_element_type=F32
        )
        top = jnp.max(dots, axis=0, keepdims=True)
        exps = jnp.exp2((dots - top) * scale)
        total = jnp.sum(exps, axis=0, keepdims=True)
        parts = jnp.dot(v_ref[0], exps.astype(BF16), preferred_element_type=F32)
        out = (parts[:VEC] + parts[VEC:]) / total
        o_ref[pl.ds(pl.multiple_of(h * VEC, VEC), VEC), :] = out.astype(BF16)
        lse = top * (1.0 / math.sqrt(HEAD_DIM)) + jnp.log(total)
        old = jnp.where(h == 0, 0.0, o_ref[ROWS:PACK, :].astype(F32))
        o_ref[ROWS:PACK, :] = pack_lse(old, [(h, lse)])


def attend(qa, qb, keys, values):
    n = qa.shape[0]
    out = jax.ShapeDtypeStruct((PACK, n), BF16)
    low, high = lambda h: (0, h), lambda h: (0, HALF + h)
    return pl.pallas_call(
        attend_kernel,
        grid=(HALF,),
        in_specs=[
            pl.BlockSpec((n, HEAD_DIM), low),
            pl.BlockSpec((n, HEAD_DIM), low),
            pl.BlockSpec((KEYS, HEAD_DIM), low),
            pl.BlockSpec((KEYS, HEAD_DIM), high),
            pl.BlockSpec((1, 2 * VEC, KEYS), lambda h: (h, 0, 0)),
            pl.BlockSpec((1, 2 * VEC, KEYS), lambda h: (HALF + h, 0, 0)),
        ],
        out_specs=[pl.BlockSpec((PACK, n), lambda h: (0, 0))] * 2,
        out_shape=(out, out),
        cost_estimate=cost(
            4 * n * KEYS * HEAD_DIM * HEADS_HERE, 4 * n * 768 + 4 * KEYS * 768, n * KEYS * HEADS_HERE
        ),
        name="attend",
    )(qa, qb, keys, keys, values, values)


def merge(refs, base):
    blocks = [r[base + ROWS : base + PACK, :].astype(F32) for r in refs]
    outs, lses = [], []
    for h in range(HALF):
        parts = [
            b[h : h + 1] + b[HALF + h : HALF + h + 1] + b[2 * HALF + h : 2 * HALF + h + 1] for b in blocks
        ]
        top = functools.reduce(jnp.maximum, parts)
        weights = [jnp.exp(p - top) for p in parts]
        total = sum(weights)
        inverse = 1.0 / total
        acc = 0.0
        for r, w in zip(refs, weights):
            acc = acc + r[base + h * VEC : base + (h + 1) * VEC, :].astype(F32) * (w * inverse)
        outs.append(acc)
        lses.append(top + jnp.log(total))
    return outs, lses


def merge_first_kernel(*refs):
    a_refs, b_refs, out_refs = refs[:4], refs[4:8], refs[8:]
    for half, ins in enumerate((a_refs, b_refs)):
        outs, lses = merge(ins, 0)
        packed = pack_lse(jnp.zeros((16, KEYS), F32), enumerate(lses))
        for k in range(4):
            o_ref = out_refs[half * 4 + k]
            for h in range(HALF):
                o_ref[h * VEC : (h + 1) * VEC, :] = outs[h][:, k * 128 : (k + 1) * 128].astype(BF16)
            o_ref[ROWS:PACK, :] = packed[:, k * 128 : (k + 1) * 128]


def merge_first(a_parts, b_parts):
    outs = pl.pallas_call(
        merge_first_kernel,
        out_shape=tuple(jax.ShapeDtypeStruct((PACK, 128), BF16) for _ in range(8)),
        cost_estimate=cost(8 * PACK * KEYS * 2, 10 * PACK * KEYS * 2),
        name="merge_first",
    )(*a_parts, *b_parts)
    return outs[:4], outs[4:]


def merge_second_kernel(*refs):
    o_ref = refs[8]
    for half in range(2):
        outs, lses = merge(refs[half * 4 : half * 4 + 4], 0)
        base = half * PACK
        for h in range(HALF):
            o_ref[base + h * VEC : base + (h + 1) * VEC, :] = outs[h].astype(BF16)
        o_ref[base + ROWS : base + PACK, :] = pack_lse(jnp.zeros((16, 128), F32), enumerate(lses))


def merge_second(a_parts, b_parts):
    return pl.pallas_call(
        merge_second_kernel,
        out_shape=jax.ShapeDtypeStruct((2 * PACK, 128), BF16),
        cost_estimate=cost(8 * PACK * 128 * 2, 10 * PACK * 128 * 2),
        name="merge_second",
    )(*a_parts, *b_parts)


def merge_last_kernel(*refs):
    outs = merge(refs[:4], 0)[0] + merge(refs[:4], PACK)[0]
    refs[4][...] = sum(outs[1:], outs[0])


def merge_last(parts):
    return pl.pallas_call(
        merge_last_kernel,
        out_shape=jax.ShapeDtypeStruct((VEC, 128), F32),
        cost_estimate=cost(8 * PACK * 128 * 2, 10 * PACK * 128),
        name="merge_last",
    )(*parts)


def decode_kernel(info, v0, v1, v2, v3, base_ref, up_ref, down_ref, level_ref, w_ref, b_ref, o_ref, all_ref):
    for kx, v_ref in enumerate((v0, v1, v2, v3)):
        all_ref[kx] = v_ref[...]
    level = level_ref[0]
    row = lax.broadcasted_iota(jnp.int32, (512, 128), 0)
    col = lax.broadcasted_iota(jnp.int32, (512, 128), 1)

    def attention_rows(which, first, count):
        slot, dy, dx, on = info[which, 0], info[which, 1], info[which, 2], info[which, 3]
        lane = row % 128
        target = (row // 256) * 64 + (lane % 32) * 2 + (row // 128) % 2
        choose = ((lane // 32 == slot) & (target == col)).astype(F32).astype(BF16)
        stacked = []
        for a in range(4):
            for pair in range(2):
                pieces = []
                for inner in range(2):
                    ky = (dy + 4 - a) % 4
                    kx = (dx + 4 - (pair * 2 + inner)) % 4
                    for b in range(2):
                        pieces.append(all_ref[kx, ky, b * 32 + first : b * 32 + first + count, :])
                stacked.append(jnp.concatenate(pieces, axis=1))
        left = jnp.concatenate(stacked, axis=0)
        high = left.astype(BF16)
        low = (left - high.astype(F32)).astype(BF16)
        spread = jnp.dot(high, choose, preferred_element_type=F32) + jnp.dot(
            low, choose, preferred_element_type=F32
        )
        spread = jnp.concatenate([spread[i * count : (i + 1) * count] for i in range(8)], axis=1)
        return jnp.where(on > 0, spread, 0.0)

    own = base_ref[...] - level * attention_rows(0, 0, 32)
    up = up_ref[...] - level * attention_rows(1, 16, 16)
    down = down_ref[...] - level * attention_rows(2, 0, 16)
    latent = jnp.concatenate([up, own, down], axis=0) / 0.3611 + 0.1159
    line = lax.broadcasted_iota(jnp.int32, latent.shape, 0)
    column = lax.broadcasted_iota(jnp.int32, latent.shape, 1)
    inside = ((line >= 16) | (info[1, 4] > 0)) & ((line < 48) | (info[2, 4] > 0))
    latent = jnp.where(inside, latent, 0.0)
    before = jnp.where(column == 0, 0.0, pltpu.roll(latent, 1, 1)).astype(BF16)
    after = jnp.where(column == COLS - 1, 0.0, pltpu.roll(latent, COLS - 1, 1)).astype(BF16)
    middle = latent.astype(BF16)
    for r in range(2):
        stencil = jnp.concatenate([s[r * 16 : r * 16 + 48] for s in (before, middle, after)], axis=0)
        out = jnp.dot(w_ref[...], stencil, preferred_element_type=F32) + b_ref[...]
        o_ref[r] = out.astype(BF16)


def decode(info, gathered, base, up, down, level, weight, bias):
    smem = pl.BlockSpec(memory_space=pltpu.SMEM)
    vmem = pl.BlockSpec(memory_space=pltpu.VMEM)
    return pl.pallas_call(
        decode_kernel,
        out_shape=jax.ShapeDtypeStruct((2, weight.shape[0], COLS), BF16),
        in_specs=[smem] + [vmem] * 7 + [smem] + [vmem] * 2,
        out_specs=vmem,
        scratch_shapes=[pltpu.VMEM((4, 4, VEC, 128), F32)],
        cost_estimate=cost(4 * 128 * 144 * 1024, 2 << 20),
        name="decode",
    )(info, *gathered, base, up, down, level, weight, bias)


def on_device(
    fresh_qkv,
    kv_cache,
    hidden,
    refresh,
    out_weight,
    final_weight,
    final_bias,
    gate_scale,
    noise_level,
    noisy_latent,
    velocity_cache,
    conv_weight,
    conv_bias,
):
    me = lax.axis_index("patch")
    my = {axis: coord(me, axis) for axis in STRIDE}
    offset = {axis: (my[axis] + 4 - coord(refresh, axis)) % 4 for axis in STRIDE}

    with jax.named_scope("queries"):
        own = fresh_qkv[:, 0]
        got = [shift(own[k * 128 : (k + 1) * 128], "y", k) for k in range(4)]
        held = jnp.stack([pick(got, offset["y"][s]) for s in range(SLOTS)])
        got = [shift(held[:, k * 32 : (k + 1) * 32], "x", k) for k in range(4)]
        held = jnp.stack([pick([g[s] for g in got], offset["x"][s]) for s in range(SLOTS)])
        got = [shift(held, "z", k) for k in range(4)]
        held = jnp.stack([pick([g[s] for g in got], offset["z"][s]) for s in range(SLOTS)])
        held = held.reshape(SLOTS * 32, HEADS_HERE * HEAD_DIM)
        first, second = held[:, : HALF * HEAD_DIM], held[:, HALF * HEAD_DIM :]
        qa = jnp.concatenate([shift(first, "y", k) for k in range(4)], axis=0)
        qb = jnp.concatenate([shift(second, "x", k) for k in range(4)], axis=0)
        qa = [shift(qa, "x", k) for k in range(4)]
        qb = [shift(qb, "y", k) for k in range(4)]

    with jax.named_scope("keys_values"):
        refreshed = jnp.any(refresh == me)
        keys = jnp.where(refreshed, fresh_qkv[:, 1], kv_cache[:, 0])
        value_rows = jnp.where(refreshed, fresh_qkv[:, 2], kv_cache[:, 1])
        final_wide = final_weight.astype(F32)
        gated = gate_scale[:, None] * final_wide
        gated = gated.reshape(-1, LAT_CH, 2, 2).transpose(0, 3, 2, 1).reshape(-1, VEC)
        mixed = jnp.dot(out_weight.astype(F32), gated, precision=lax.Precision.HIGH)
        values = jnp.einsum(
            "khd,hdn->hnk",
            value_rows.reshape(KEYS, HEADS_HERE, HEAD_DIM).astype(F32),
            mixed.reshape(HEADS_HERE, HEAD_DIM, VEC),
            precision=lax.Precision.HIGH,
        )
        high = lax.reduce_precision(values, 8, 7)
        values = jnp.concatenate([high.astype(BF16), (values - high).astype(BF16)], axis=1)

    with jax.named_scope("latent_base"):
        plain = jnp.dot(hidden, final_weight, preferred_element_type=F32) + final_bias
        plain = plain.reshape(1, KEYS, LAT_CH, 2, 2).transpose(0, 3, 2, 1, 4).reshape(2, LAT_CH, COLS)
        plain = jnp.where(refreshed, plain, velocity_cache.astype(F32))
        base = noisy_latent.astype(F32) - noise_level[0] * plain
        up = lax.ppermute(base[1], "patch", [(p, p + 1) for p in range(PATCHES - 1)])
        down = lax.ppermute(base[0], "patch", [(p + 1, p) for p in range(PATCHES - 1)])

    with jax.named_scope("attention"):
        back_a, back_b = [None] * 4, [None] * 4
        for k in (0, 1, 3, 2):
            out_a, out_b = attend(qa[k], qb[k], keys, values)
            back_a[k] = shift(out_a, "x", -k)
            back_b[k] = shift(out_b, "y", -k)
        parts_a, parts_b = merge_first(back_a, back_b)
        back_a = [shift(parts_a[k], "y", -k) for k in range(4)]
        back_b = [shift(parts_b[k], "x", -k) for k in range(4)]
        part = merge_second(back_a, back_b)
        term = merge_last([shift(part, "z", k) for k in range(4)])

    with jax.named_scope("velocity"):
        count = lax.axis_size("head")
        for k in range(1, count):
            arrived = lax.ppermute(term, "head", [(i, (i + k) % count) for i in range(count)])
            total = arrived if k == 1 else total + arrived
        term = term + total
        term = jnp.stack([shift(term, "y", k) for k in range(4)])
        gathered = [shift(term, "x", k) for k in range(4)]

    with jax.named_scope("decode"):
        rows = []
        for near in (0, -1, 1):
            match = refresh == me + near
            slot = jnp.sum(jnp.where(match, jnp.arange(SLOTS, dtype=jnp.int32), 0))
            chosen = lambda v: jnp.sum(jnp.where(match, v, 0))
            exists = (me + near >= 0) & (me + near < PATCHES)
            rows.append(
                jnp.stack(
                    [
                        slot,
                        chosen(offset["y"]),
                        chosen(offset["x"]),
                        jnp.any(match).astype(jnp.int32),
                        exists.astype(jnp.int32),
                    ]
                )
            )
        info = jnp.stack(rows).astype(jnp.int32)
        weight = conv_weight.transpose(0, 2, 1, 3).reshape(conv_weight.shape[0], -1)
        return decode(
            info, gathered, base.reshape(2 * LAT_CH, COLS), up, down, noise_level, weight, conv_bias[:, None]
        )


def solution(mesh):
    return jax.shard_map(
        on_device,
        mesh=mesh,
        in_specs=(
            P("patch", None, "head"),
            P("patch", None, "head"),
            P("patch", None),
            P(),
            P("head", None),
            P(),
            P(),
            P(),
            P(),
            P("patch", None, None),
            P("patch", None, None),
            P("head", None, None, None),
            P("head"),
        ),
        out_specs=P("patch", "head", None),
        check_vma=False,
    )
```

```python
import functools
import math

import jax
import jax.numpy as jnp
from jax import lax
from jax.experimental import pallas as pl
from jax.experimental.pallas import tpu as pltpu
from jax.sharding import PartitionSpec as P

HEAD_DIM = 128
LAT_CH = 16
PATCHES = 64
SLOTS = 4
HEADS_HERE = 6
HALF = 3
VEC = 64
ROWS = HALF * VEC
PACK = ROWS + 16
KEYS = 512
COLS = 1024
F32 = jnp.float32
BF16 = jnp.bfloat16
STRIDE = {"y": 16, "x": 4, "z": 1}
BITS = {"y": 4, "x": 2, "z": 0}


def coord(patch, axis):
    return (patch // STRIDE[axis]) % 4


def moved(patch, axis, step):
    here = coord(patch, axis)
    return patch + ((here + step) % 4 - here) * STRIDE[axis]


def shift(value, axis, step):
    if step == 0:
        return value
    return lax.ppermute(value, "patch", [(p, moved(p, axis, step)) for p in range(PATCHES)])


def cost(flops, moved_bytes, exps=0):
    return pl.CostEstimate(flops=flops, bytes_accessed=moved_bytes, transcendentals=exps)


def scalars_then(count):
    smem = pl.BlockSpec(memory_space=pltpu.SMEM)
    return [smem, smem] + [pl.BlockSpec(memory_space=pltpu.VMEM)] * count


def select_kernel(axis, pieces, refresh_ref, me_ref, *refs):
    got, outs = refs[:4], refs[4:]
    here = me_ref[0] >> BITS[axis]
    size = outs[0].shape[0] // SLOTS
    for slot in range(SLOTS):
        which = (here - (refresh_ref[slot] >> BITS[axis])) & 3
        first = 0 if got[0].shape[0] == pieces * size else slot * pieces * size
        for k in range(4):

            @pl.when(which == k)
            def _():
                for j in range(pieces):
                    start = first + j * size
                    outs[j][slot * size : (slot + 1) * size, :] = got[k][start : start + size, :]


def select(axis, pieces, size, refresh, me, got):
    width = got[0].shape[1]
    outs = pl.pallas_call(
        functools.partial(select_kernel, axis, pieces),
        in_specs=scalars_then(4),
        out_shape=tuple(jax.ShapeDtypeStruct((SLOTS * size, width), BF16) for _ in range(pieces)),
        cost_estimate=cost(0, 4 * SLOTS * size * pieces * width),
        name="select_" + axis,
    )(refresh, me, *got)
    return list(outs)


def assemble_kernel(me_ref, g0, g1, g2, g3, a_ref, b_ref):
    half = a_ref.shape[1]
    for k, ref in enumerate((g0, g1, g2, g3)):
        rows = pl.ds(pl.multiple_of(((me_ref[0] - k) & 3) * 32, 32), 32)
        a_ref[rows, :] = ref[:, :half]
        b_ref[rows, :] = ref[:, half:]


def assemble(me, got):
    half = HALF * HEAD_DIM
    return pl.pallas_call(
        assemble_kernel,
        in_specs=scalars_then(4)[1:],
        out_shape=(jax.ShapeDtypeStruct((128, half), BF16),) * 2,
        cost_estimate=cost(0, 8 * 128 * half),
        name="assemble",
    )(me, *got)


def pack_lse(block, entries):
    row = lax.broadcasted_iota(jnp.int32, block.shape, 0)
    for h, lse in entries:
        high = lse.astype(BF16).astype(F32)
        rest = lse - high
        mid = rest.astype(BF16).astype(F32)
        low = rest - mid
        for part, value in enumerate((high, mid, low)):
            block = jnp.where(row == part * HALF + h, jnp.broadcast_to(value, block.shape), block)
    return block.astype(BF16)


def attend_kernel(qa_ref, qb_ref, ka_ref, kb_ref, va_ref, vb_ref, oa_ref, ob_ref):
    scale = math.log2(math.e) / math.sqrt(HEAD_DIM)
    h = pl.program_id(0)
    halves = ((qa_ref, ka_ref, va_ref, oa_ref), (qb_ref, kb_ref, vb_ref, ob_ref))
    for q_ref, k_ref, v_ref, o_ref in halves:
        dots = lax.dot_general(
            k_ref[...], q_ref[...], (((1,), (1,)), ((), ())), preferred_element_type=F32
        )
        top = jnp.max(dots, axis=0, keepdims=True)
        exps = jnp.exp2((dots - top) * scale)
        total = jnp.sum(exps, axis=0, keepdims=True)
        parts = jnp.dot(v_ref[0], exps.astype(BF16), preferred_element_type=F32)
        out = (parts[:VEC] + parts[VEC:]) / total
        o_ref[pl.ds(pl.multiple_of(h * VEC, VEC), VEC), :] = out.astype(BF16)
        lse = top * (1.0 / math.sqrt(HEAD_DIM)) + jnp.log(total)
        old = jnp.where(h == 0, 0.0, o_ref[ROWS:PACK, :].astype(F32))
        o_ref[ROWS:PACK, :] = pack_lse(old, [(h, lse)])


def attend(qa, qb, keys, values):
    n = qa.shape[0]
    out = jax.ShapeDtypeStruct((PACK, n), BF16)
    low, high = lambda h: (0, h), lambda h: (0, HALF + h)
    return pl.pallas_call(
        attend_kernel,
        grid=(HALF,),
        in_specs=[
            pl.BlockSpec((n, HEAD_DIM), low),
            pl.BlockSpec((n, HEAD_DIM), low),
            pl.BlockSpec((KEYS, HEAD_DIM), low),
            pl.BlockSpec((KEYS, HEAD_DIM), high),
            pl.BlockSpec((1, 2 * VEC, KEYS), lambda h: (h, 0, 0)),
            pl.BlockSpec((1, 2 * VEC, KEYS), lambda h: (HALF + h, 0, 0)),
        ],
        out_specs=[pl.BlockSpec((PACK, n), lambda h: (0, 0))] * 2,
        out_shape=(out, out),
        cost_estimate=cost(
            4 * n * KEYS * HEAD_DIM * HEADS_HERE, 4 * n * 768 + 4 * KEYS * 768, n * KEYS * HEADS_HERE
        ),
        name="attend",
    )(qa, qb, keys, keys, values, values)


def merge(refs, base):
    blocks = [r[base + ROWS : base + PACK, :].astype(F32) for r in refs]
    outs, lses = [], []
    for h in range(HALF):
        parts = [
            b[h : h + 1] + b[HALF + h : HALF + h + 1] + b[2 * HALF + h : 2 * HALF + h + 1] for b in blocks
        ]
        top = functools.reduce(jnp.maximum, parts)
        weights = [jnp.exp(p - top) for p in parts]
        total = sum(weights)
        inverse = 1.0 / total
        acc = 0.0
        for r, w in zip(refs, weights):
            acc = acc + r[base + h * VEC : base + (h + 1) * VEC, :].astype(F32) * (w * inverse)
        outs.append(acc)
        lses.append(top + jnp.log(total))
    return outs, lses


def merge_first_kernel(*refs):
    a_refs, b_refs, out_refs = refs[:4], refs[4:8], refs[8:]
    for half, ins in enumerate((a_refs, b_refs)):
        outs, lses = merge(ins, 0)
        packed = pack_lse(jnp.zeros((16, KEYS), F32), enumerate(lses))
        for k in range(4):
            o_ref = out_refs[half * 4 + k]
            for h in range(HALF):
                o_ref[h * VEC : (h + 1) * VEC, :] = outs[h][:, k * 128 : (k + 1) * 128].astype(BF16)
            o_ref[ROWS:PACK, :] = packed[:, k * 128 : (k + 1) * 128]


def merge_first(a_parts, b_parts):
    outs = pl.pallas_call(
        merge_first_kernel,
        out_shape=tuple(jax.ShapeDtypeStruct((PACK, 128), BF16) for _ in range(8)),
        cost_estimate=cost(8 * PACK * KEYS * 2, 10 * PACK * KEYS * 2),
        name="merge_first",
    )(*a_parts, *b_parts)
    return outs[:4], outs[4:]


def merge_second_kernel(*refs):
    o_ref = refs[8]
    for half in range(2):
        outs, lses = merge(refs[half * 4 : half * 4 + 4], 0)
        base = half * PACK
        for h in range(HALF):
            o_ref[base + h * VEC : base + (h + 1) * VEC, :] = outs[h].astype(BF16)
        o_ref[base + ROWS : base + PACK, :] = pack_lse(jnp.zeros((16, 128), F32), enumerate(lses))


def merge_second(a_parts, b_parts):
    return pl.pallas_call(
        merge_second_kernel,
        out_shape=jax.ShapeDtypeStruct((2 * PACK, 128), BF16),
        cost_estimate=cost(8 * PACK * 128 * 2, 10 * PACK * 128 * 2),
        name="merge_second",
    )(*a_parts, *b_parts)


def merge_last_kernel(*refs):
    outs = merge(refs[:4], 0)[0] + merge(refs[:4], PACK)[0]
    refs[4][...] = sum(outs[1:], outs[0])


def merge_last(parts):
    return pl.pallas_call(
        merge_last_kernel,
        out_shape=jax.ShapeDtypeStruct((VEC, 128), F32),
        cost_estimate=cost(8 * PACK * 128 * 2, 10 * PACK * 128),
        name="merge_last",
    )(*parts)


def decode_kernel(
    refresh_ref, me_ref, v0, v1, v2, v3, base_ref, up_ref, down_ref, level_ref, w_ref, b_ref, o_ref, all_ref
):
    for kx, v_ref in enumerate((v0, v1, v2, v3)):
        all_ref[kx] = v_ref[...]
    level = level_ref[0]
    me = me_ref[0]
    row = lax.broadcasted_iota(jnp.int32, (512, 128), 0)
    col = lax.broadcasted_iota(jnp.int32, (512, 128), 1)
    lane = row % 128

    def attention_rows(near, kinds):
        patch, slot, on = me + near, 0, 0
        for s in range(SLOTS):
            hit = refresh_ref[s] == patch
            slot = jnp.where(hit, s, slot)
            on = jnp.where(hit, 1, on)
        dy = ((me >> BITS["y"]) - (patch >> BITS["y"])) & 3
        dx = ((me >> BITS["x"]) - (patch >> BITS["x"])) & 3
        token = (((lane // 32) - patch) & 3) * 8 + lane % 8
        target = (row // 256) * 64 + token * 2 + (row // 128) % 2
        choose = (((lane // 8) % 4 == slot) & (target == col)).astype(F32).astype(BF16)
        count = 16 * len(kinds)
        stacked = []
        for a in range(4):
            ky = (dy - a) & 3
            for pair in range(2):
                pieces = []
                for inner in range(2):
                    kx = (dx - (pair * 2 + inner)) & 3
                    for b in range(2):
                        parts = [all_ref[kx, ky, pl.ds(kind * 2 + b, 16, 4), :] for kind in kinds]
                        pieces.append(jnp.concatenate(parts, axis=0))
                stacked.append(jnp.concatenate(pieces, axis=1))
        left = jnp.concatenate(stacked, axis=0)
        high = left.astype(BF16)
        low = (left - high.astype(F32)).astype(BF16)
        spread = jnp.dot(high, choose, preferred_element_type=F32) + jnp.dot(
            low, choose, preferred_element_type=F32
        )
        spread = jnp.concatenate([spread[i * count : (i + 1) * count] for i in range(8)], axis=1)
        return jnp.where(on > 0, spread, 0.0)

    own = base_ref[...] - level * attention_rows(0, (0, 1))
    up = up_ref[...] - level * attention_rows(-1, (1,))
    down = down_ref[...] - level * attention_rows(1, (0,))
    latent = jnp.concatenate([up, own, down], axis=0) / 0.3611 + 0.1159
    line = lax.broadcasted_iota(jnp.int32, latent.shape, 0)
    column = lax.broadcasted_iota(jnp.int32, latent.shape, 1)
    inside = ((line >= 16) | (me > 0)) & ((line < 48) | (me < PATCHES - 1))
    latent = jnp.where(inside, latent, 0.0)
    before = jnp.where(column == 0, 0.0, pltpu.roll(latent, 1, 1)).astype(BF16)
    after = jnp.where(column == COLS - 1, 0.0, pltpu.roll(latent, COLS - 1, 1)).astype(BF16)
    middle = latent.astype(BF16)
    for r in range(2):
        stencil = jnp.concatenate([s[r * 16 : r * 16 + 48] for s in (before, middle, after)], axis=0)
        out = jnp.dot(w_ref[...], stencil, preferred_element_type=F32) + b_ref[...]
        o_ref[r] = out.astype(BF16)


def decode(refresh, me, gathered, base, up, down, level, weight, bias):
    smem = pl.BlockSpec(memory_space=pltpu.SMEM)
    vmem = pl.BlockSpec(memory_space=pltpu.VMEM)
    return pl.pallas_call(
        decode_kernel,
        out_shape=jax.ShapeDtypeStruct((2, weight.shape[0], COLS), BF16),
        in_specs=[smem, smem] + [vmem] * 7 + [smem] + [vmem] * 2,
        out_specs=vmem,
        scratch_shapes=[pltpu.VMEM((4, 4, VEC, 128), F32)],
        cost_estimate=cost(4 * 128 * 144 * 1024, 2 << 20),
        name="decode",
    )(refresh, me, *gathered, base, up, down, level, weight, bias)


def on_device(
    fresh_qkv,
    kv_cache,
    hidden,
    refresh,
    out_weight,
    final_weight,
    final_bias,
    gate_scale,
    noise_level,
    noisy_latent,
    velocity_cache,
    conv_weight,
    conv_bias,
):
    me = lax.axis_index("patch").astype(jnp.int32)
    here = me.reshape(1)
    together = lax.optimization_barrier

    with jax.named_scope("queries"):
        own = fresh_qkv[:, 0]
        got = [shift(own[k * 128 : (k + 1) * 128], "y", k) for k in range(4)]
        sent = select("y", 4, 32, refresh, here, got)
        got = [shift(sent[k], "x", k) for k in range(4)]

    with jax.named_scope("keys_values"):
        refreshed = jnp.any(refresh == me)
        keys = jnp.where(refreshed, fresh_qkv[:, 1], kv_cache[:, 0])
        value_rows = jnp.where(refreshed, fresh_qkv[:, 2], kv_cache[:, 1])
        gated = gate_scale[:, None] * final_weight.astype(F32)
        mixed = jnp.dot(out_weight.astype(F32), gated, precision=lax.Precision.HIGH)
        values = jnp.einsum(
            "khd,hdn->hnk",
            value_rows.reshape(KEYS, HEADS_HERE, HEAD_DIM).astype(F32),
            mixed.reshape(HEADS_HERE, HEAD_DIM, VEC),
            precision=lax.Precision.HIGH,
        )
        high = lax.reduce_precision(values, 8, 7)
        values = jnp.concatenate([high.astype(BF16), (values - high).astype(BF16)], axis=1)

    with jax.named_scope("latent_base"):
        plain = jnp.dot(hidden, final_weight, preferred_element_type=F32) + final_bias
        plain = plain.reshape(1, KEYS, LAT_CH, 2, 2).transpose(0, 3, 2, 1, 4).reshape(2, LAT_CH, COLS)
        plain = jnp.where(refreshed, plain, velocity_cache.astype(F32))
        base = noisy_latent.astype(F32) - noise_level[0] * plain
        up = lax.ppermute(base[1], "patch", [(p, p + 1) for p in range(PATCHES - 1)])
        down = lax.ppermute(base[0], "patch", [(p + 1, p) for p in range(PATCHES - 1)])
        base = base.reshape(2 * LAT_CH, COLS)
        weight = conv_weight.transpose(0, 2, 1, 3).reshape(conv_weight.shape[0], -1)
        bias = conv_bias[:, None]

    with jax.named_scope("queries"):
        got, mixed, keys = together((got, mixed, keys))
        sent = select("x", 4, 8, refresh, here, got)
        got = [shift(sent[k], "z", k) for k in range(4)]
        got, base, weight, bias = together((got, base, weight, bias))
        sent = select("z", 1, 8, refresh, here, got)[0]
        got = [shift(sent, "z", k) for k in range(4)]
        first, second = assemble(here, got)
        first, second, up, down = together((first, second, up, down))
        qa = [shift(first, "y", k) for k in range(4)]
        qb = [shift(second, "x", k) for k in range(4)]
        qa, qb, values = together((qa, qb, values))
        qa, qb = jnp.concatenate(qa, axis=0), jnp.concatenate(qb, axis=0)
        qa = [shift(qa, "x", k) for k in range(4)]
        qb = [shift(qb, "y", k) for k in range(4)]

    with jax.named_scope("attention"):
        back_a, back_b = [None] * 4, [None] * 4
        for k in (0, 1, 3, 2):
            out_a, out_b = attend(qa[k], qb[k], keys, values)
            keys, out_a, out_b = together((keys, out_a, out_b))
            back_a[k] = shift(out_a, "x", -k)
            back_b[k] = shift(out_b, "y", -k)
        parts_a, parts_b = merge_first(back_a, back_b)
        back_a = [shift(parts_a[k], "y", -k) for k in range(4)]
        back_b = [shift(parts_b[k], "x", -k) for k in range(4)]
        part = merge_second(back_a, back_b)
        term = merge_last([shift(part, "z", k) for k in range(4)])

    with jax.named_scope("velocity"):
        count = lax.axis_size("head")
        for k in range(1, count):
            arrived = lax.ppermute(term, "head", [(i, (i + k) % count) for i in range(count)])
            total = arrived if k == 1 else total + arrived
        term = term + total
        term = jnp.stack([shift(term, "y", k) for k in range(4)])
        gathered = [shift(term, "x", k) for k in range(4)]

    with jax.named_scope("decode"):
        return decode(refresh, here, gathered, base, up, down, noise_level, weight, bias)


def solution(mesh):
    return jax.shard_map(
        on_device,
        mesh=mesh,
        in_specs=(
            P("patch", None, "head"),
            P("patch", None, "head"),
            P("patch", None),
            P(),
            P("head", None),
            P(),
            P(),
            P(),
            P(),
            P("patch", None, None),
            P("patch", None, None),
            P("head", None, None, None),
            P("head"),
        ),
        out_specs=P("patch", "head", None),
        check_vma=False,
    )
```

```python
import functools
import math

import jax
import jax.numpy as jnp
from jax import lax
from jax.experimental import pallas as pl
from jax.experimental.pallas import tpu as pltpu
from jax.sharding import Mesh
from jax.sharding import PartitionSpec as P

HEAD_DIM = 128
LAT_CH = 16
PATCHES = 64
SLOTS = 4
HEADS_HERE = 6
HALF = 3
VEC = 64
ROWS = HALF * VEC
PACK = ROWS + 16
KEYS = 512
COLS = 1024
CHUNK = 8
F32 = jnp.float32
BF16 = jnp.bfloat16
PATCH = ("y", "x", "z")
HEAD = ("w", "c")
BITS = {"y": 4, "x": 2, "z": 0}


def shift(value, axis, step):
    if step == 0:
        return value
    return lax.ppermute(value, axis, [(i, (i + step) % 4) for i in range(4)])


def spread_out(value):
    return jnp.broadcast_to(value[None], (4,) + value.shape)


def exchange(value, axis):
    return lax.all_to_all(value, axis, 0, 0)


def cost(flops, moved_bytes, exps=0):
    return pl.CostEstimate(flops=flops, bytes_accessed=moved_bytes, transcendentals=exps)


SMEM = pl.BlockSpec(memory_space=pltpu.SMEM)
VMEM = pl.BlockSpec(memory_space=pltpu.VMEM)


def split(value):
    high = value.astype(BF16)
    return high, (value - high.astype(F32)).astype(BF16)


def select_kernel(refresh_ref, got_ref, o_ref):
    for slot in range(SLOTS):
        rows = got_ref[refresh_ref[slot]]
        for k in range(4):
            o_ref[k, slot * CHUNK : (slot + 1) * CHUNK, :] = rows


def select(refresh, got):
    width = got.shape[2]
    return pl.pallas_call(
        select_kernel,
        in_specs=[SMEM, VMEM],
        out_shape=jax.ShapeDtypeStruct((4, SLOTS * CHUNK, width), BF16),
        cost_estimate=cost(0, 5 * SLOTS * CHUNK * width * 2),
        name="select",
    )(refresh, got)


def values_kernel(v_ref, w_ref, o_ref):
    for h in range(HEADS_HERE):
        cols = slice(h * HEAD_DIM, (h + 1) * HEAD_DIM)
        left = jnp.concatenate(split(w_ref[:, cols]), axis=0)
        both = lax.dot_general(
            left, v_ref[:, cols], (((1,), (1,)), ((), ())), preferred_element_type=F32
        )
        high, low = split(both[:VEC] + both[VEC:])
        o_ref[h, :VEC, :] = high
        o_ref[h, VEC:, :] = low


def project_values(value_rows, mixed):
    return pl.pallas_call(
        values_kernel,
        out_shape=jax.ShapeDtypeStruct((HEADS_HERE, 2 * VEC, KEYS), BF16),
        cost_estimate=cost(4 * KEYS * VEC * HEAD_DIM * HEADS_HERE, 4 * KEYS * 768),
        name="values",
    )(value_rows, mixed)


def base_kernel(refresh_ref, me_ref, level_ref, plain_ref, noisy_ref, cache_ref, o_ref, *rest):
    first_ref, last_ref, block_ref = rest
    row = lax.broadcasted_iota(jnp.int32, (256, 256), 0)
    col = lax.broadcasted_iota(jnp.int32, (256, 256), 1)
    choose = ((row % 128) * 2 + row // 128 == col).astype(F32).astype(BF16)
    stacked = []
    for i in range(4):
        block_ref[i] = plain_ref[:, i * 128 : (i + 1) * 128]
        pieces = []
        for b in range(2):
            parts = [block_ref[i, pl.ds(a * 2 + b, LAT_CH, 4), :] for a in range(2)]
            pieces.append(jnp.concatenate(parts, axis=0))
        stacked.append(jnp.concatenate(pieces, axis=1))
    left = jnp.concatenate(stacked, axis=0)
    high, rest = left.astype(BF16), left - left.astype(BF16).astype(F32)
    mid, low = split(rest)
    field = sum(jnp.dot(part, choose, preferred_element_type=F32) for part in (high, mid, low))
    field = jnp.concatenate([field[i * 32 : (i + 1) * 32] for i in range(4)], axis=1)
    fresh = False
    for slot in range(SLOTS):
        fresh = fresh | (refresh_ref[slot] == me_ref[0])
    level = level_ref[0]
    for a in range(2):
        rows = slice(a * LAT_CH, (a + 1) * LAT_CH)
        velocity = jnp.where(fresh, field[rows], cache_ref[a].astype(F32))
        latent = noisy_ref[a].astype(F32) - level * velocity
        o_ref[rows, :] = latent
        (first_ref, last_ref)[a][...] = latent


def latent_base(refresh, me, level, plain, noisy, cache):
    edge = jax.ShapeDtypeStruct((LAT_CH, COLS), F32)
    return pl.pallas_call(
        base_kernel,
        in_specs=[SMEM] * 3 + [VMEM] * 3,
        out_shape=(jax.ShapeDtypeStruct((2 * LAT_CH, COLS), F32), edge, edge),
        scratch_shapes=[pltpu.VMEM((4, VEC, 128), F32)],
        cost_estimate=cost(6 * 128 * 256 * 256, 1 << 19),
        name="latent_base",
    )(refresh, me, level, plain, noisy, cache)


def pack_lse(entries, width):
    row = lax.broadcasted_iota(jnp.int32, (16, width), 0)
    block = jnp.zeros((16, width), F32)
    for h, lse in enumerate(entries):
        high = lse.astype(BF16).astype(F32)
        rest = lse - high
        mid = rest.astype(BF16).astype(F32)
        low = rest - mid
        for part, value in enumerate((high, mid, low)):
            block = jnp.where(row == part * HALF + h, jnp.broadcast_to(value, block.shape), block)
    return block.astype(BF16)


def attend_kernel(qa_ref, qb_ref, k_ref, v_ref, oa_ref, ob_ref):
    scale = math.log2(math.e) / math.sqrt(HEAD_DIM)
    halves = ((qa_ref, oa_ref), (qb_ref, ob_ref))

    def scores(head):
        half, h = divmod(head, HALF)
        return lax.dot_general(
            k_ref[:, head * HEAD_DIM : (head + 1) * HEAD_DIM],
            halves[half][0][:, h * HEAD_DIM : (h + 1) * HEAD_DIM],
            (((1,), (1,)), ((), ())),
            preferred_element_type=F32,
        )

    dots, lses = scores(0), []
    for head in range(HEADS_HERE):
        half, h = divmod(head, HALF)
        o_ref = halves[half][1]
        following = scores(head + 1) if head + 1 < HEADS_HERE else None
        top = jnp.max(dots, axis=0, keepdims=True)
        exps = jnp.exp2((dots - top) * scale)
        total = jnp.sum(exps, axis=0, keepdims=True)
        parts = jnp.dot(v_ref[head], exps.astype(BF16), preferred_element_type=F32)
        o_ref[h * VEC : (h + 1) * VEC, :] = ((parts[:VEC] + parts[VEC:]) * (1.0 / total)).astype(BF16)
        lses.append(top * (1.0 / math.sqrt(HEAD_DIM)) + jnp.log(total))
        if h == HALF - 1:
            o_ref[ROWS:PACK, :] = pack_lse(lses, o_ref.shape[1])
            lses = []
        dots = following


def attend(qa, qb, keys, values):
    n = qa.shape[0]
    out = jax.ShapeDtypeStruct((PACK, n), BF16)
    return pl.pallas_call(
        attend_kernel,
        out_shape=(out, out),
        cost_estimate=cost(
            4 * n * KEYS * HEAD_DIM * HEADS_HERE, 4 * n * 768 + 4 * KEYS * 768, n * KEYS * HEADS_HERE
        ),
        name="attend",
    )(qa, qb, keys, values)


def merge(parts_of):
    blocks = [p(ROWS, PACK).astype(F32) for p in parts_of]
    outs, lses = [], []
    for h in range(HALF):
        parts = [
            b[h : h + 1] + b[HALF + h : HALF + h + 1] + b[2 * HALF + h : 2 * HALF + h + 1] for b in blocks
        ]
        top = functools.reduce(jnp.maximum, parts)
        weights = [jnp.exp(p - top) for p in parts]
        total = sum(weights)
        inverse = 1.0 / total
        acc = 0.0
        for p, w in zip(parts_of, weights):
            acc = acc + p(h * VEC, (h + 1) * VEC).astype(F32) * (w * inverse)
        outs.append(acc)
        lses.append(top + jnp.log(total))
    return outs, lses


def merge_first_kernel(me_ref, *refs):
    for half, axis in enumerate(("y", "x")):
        ins, o_ref = refs[half * 4 : half * 4 + 4], refs[8 + half]
        outs, lses = merge([lambda a, b, r=r: r[a:b, :] for r in ins])
        packed = pack_lse(lses, KEYS)
        for k in range(4):
            target = ((me_ref[0] >> BITS[axis]) - k) & 3
            cols = slice(k * 128, (k + 1) * 128)
            for h in range(HALF):
                o_ref[target, h * VEC : (h + 1) * VEC, :] = outs[h][:, cols].astype(BF16)
            o_ref[target, ROWS:PACK, :] = packed[:, cols]


def merge_first(me, a_parts, b_parts):
    return pl.pallas_call(
        merge_first_kernel,
        in_specs=[SMEM] + [VMEM] * 8,
        out_shape=(jax.ShapeDtypeStruct((4, PACK, 128), BF16),) * 2,
        cost_estimate=cost(8 * PACK * KEYS * 2, 10 * PACK * KEYS * 2),
        name="merge_first",
    )(me, *a_parts, *b_parts)


def merge_second_kernel(a_ref, b_ref, o_ref):
    for half, ref in enumerate((a_ref, b_ref)):
        outs, lses = merge([lambda a, b, k=k: ref[k, a:b, :] for k in range(4)])
        base = half * PACK
        packed = pack_lse(lses, 128)
        for k in range(4):
            for h in range(HALF):
                o_ref[k, base + h * VEC : base + (h + 1) * VEC, :] = outs[h].astype(BF16)
            o_ref[k, base + ROWS : base + PACK, :] = packed


def merge_second(a_parts, b_parts):
    return pl.pallas_call(
        merge_second_kernel,
        out_shape=jax.ShapeDtypeStruct((4, 2 * PACK, 128), BF16),
        cost_estimate=cost(8 * PACK * 128 * 2, 16 * PACK * 128 * 2),
        name="merge_second",
    )(a_parts, b_parts)


def merge_last_kernel(p_ref, o_ref):
    outs = []
    for base in (0, PACK):
        outs += merge([lambda a, b, k=k: p_ref[k, base + a : base + b, :] for k in range(4)])[0]
    o_ref[...] = sum(outs[1:], outs[0])


def merge_last(parts):
    return pl.pallas_call(
        merge_last_kernel,
        out_shape=jax.ShapeDtypeStruct((VEC, 128), F32),
        cost_estimate=cost(8 * PACK * 128 * 2, 10 * PACK * 128),
        name="merge_last",
    )(parts)


def decode_kernel(refresh_ref, me_ref, level_ref, v_ref, base_ref, up_ref, down_ref, w_ref, b_ref, o_ref):
    level, me = level_ref[0], me_ref[0]
    row = lax.broadcasted_iota(jnp.int32, (512, 128), 0)
    col = lax.broadcasted_iota(jnp.int32, (512, 128), 1)
    lane = row % 128
    target = (row // 256) * 64 + ((lane // 32) * 8 + lane % 8) * 2 + (row // 128) % 2

    def attention_rows(near, kinds):
        slot, on = 0, 0
        for s in range(SLOTS):
            hit = refresh_ref[s] == me + near
            slot = jnp.where(hit, s, slot)
            on = jnp.where(hit, 1, on)
        choose = (((lane // 8) % 4 == slot) & (target == col)).astype(F32).astype(BF16)
        count = LAT_CH * len(kinds)
        stacked = []
        for ys in range(4):
            for pair in range(2):
                pieces = []
                for xs in (pair * 2, pair * 2 + 1):
                    for b in range(2):
                        parts = [v_ref[xs, ys, pl.ds(kind * 2 + b, LAT_CH, 4), :] for kind in kinds]
                        pieces.append(jnp.concatenate(parts, axis=0))
                stacked.append(jnp.concatenate(pieces, axis=1))
        high, low = split(jnp.concatenate(stacked, axis=0))
        field = jnp.dot(high, choose, preferred_element_type=F32) + jnp.dot(
            low, choose, preferred_element_type=F32
        )
        field = jnp.concatenate([field[i * count : (i + 1) * count] for i in range(8)], axis=1)
        return jnp.where(on > 0, field, 0.0)

    own = base_ref[...] - level * attention_rows(0, (0, 1))
    up = up_ref[...] - level * attention_rows(-1, (1,))
    down = down_ref[...] - level * attention_rows(1, (0,))
    latent = jnp.concatenate([up, own, down], axis=0) / 0.3611 + 0.1159
    line = lax.broadcasted_iota(jnp.int32, latent.shape, 0)
    column = lax.broadcasted_iota(jnp.int32, latent.shape, 1)
    inside = ((line >= 16) | (me > 0)) & ((line < 48) | (me < PATCHES - 1))
    latent = jnp.where(inside, latent, 0.0)
    before = jnp.where(column == 0, 0.0, pltpu.roll(latent, 1, 1)).astype(BF16)
    after = jnp.where(column == COLS - 1, 0.0, pltpu.roll(latent, COLS - 1, 1)).astype(BF16)
    middle = latent.astype(BF16)

    channels = w_ref.shape[3]
    line = lax.broadcasted_iota(jnp.int32, (16, channels), 0)
    bias = jnp.broadcast_to(b_ref[...], (16, channels))
    high = bias.astype(BF16).astype(F32)
    mid = (bias - high).astype(BF16).astype(F32)
    bias = jnp.where(line == 0, high, jnp.where(line == 1, mid, jnp.where(line == 2, bias - high - mid, 0.0)))
    weight = [w_ref[u, v] for v in range(3) for u in range(3)] + [bias.astype(BF16)]
    weight = jnp.concatenate(weight, axis=0)
    ones = jnp.ones((16, COLS), BF16)
    for r in range(2):
        stencil = [s[r * 16 : r * 16 + 48] for s in (before, middle, after)] + [ones]
        out = lax.dot_general(
            weight, jnp.concatenate(stencil, axis=0), (((0,), (0,)), ((), ())), preferred_element_type=F32
        )
        o_ref[r] = out.astype(BF16)


def decode(refresh, me, level, gathered, base, up, down, weight, bias):
    return pl.pallas_call(
        decode_kernel,
        out_shape=jax.ShapeDtypeStruct((2, weight.shape[3], COLS), BF16),
        in_specs=[SMEM] * 3 + [VMEM] * 6,
        out_specs=VMEM,
        cost_estimate=cost(4 * 128 * 160 * 1024, 2 << 20),
        name="decode",
    )(refresh, me, level, gathered, base, up, down, weight, bias)


def on_device(
    fresh_qkv,
    kv_cache,
    hidden,
    refresh,
    out_weight,
    final_weight,
    final_bias,
    gate_scale,
    noise_level,
    noisy_latent,
    velocity_cache,
    conv_weight,
    conv_bias,
):
    me = lax.axis_index(PATCH).astype(jnp.int32)
    here = me.reshape(1)
    together = lax.optimization_barrier

    with jax.named_scope("queries"):
        own = fresh_qkv[:, 0].reshape(PATCHES, CHUNK, -1)
        own, fresh_qkv = together((own, fresh_qkv))
        got = exchange(own, PATCH)

    with jax.named_scope("latent_base"):
        plain = lax.dot_general(
            final_weight, hidden, (((0,), (1,)), ((), ())), preferred_element_type=F32
        )
        plain = plain + final_bias[:, None]
        base, edge_first, edge_last = latent_base(
            refresh, here, noise_level, plain, noisy_latent, velocity_cache
        )
        up = lax.ppermute(edge_last, PATCH, [(p, p + 1) for p in range(PATCHES - 1)])
        down = lax.ppermute(edge_first, PATCH, [(p + 1, p) for p in range(PATCHES - 1)])

    with jax.named_scope("keys_values"):
        refreshed = jnp.any(refresh == me)
        keys = jnp.where(refreshed, fresh_qkv[:, 1], kv_cache[:, 0])
        value_rows = jnp.where(refreshed, fresh_qkv[:, 2], kv_cache[:, 1])
        gated = final_weight.T.astype(F32) * gate_scale[None, :]
        high = lax.reduce_precision(gated, 8, 7)
        both = jnp.concatenate([high, gated - high], axis=0).astype(BF16)

    with jax.named_scope("queries"):
        got, base, up, down, keys, value_rows, both = together((got, base, up, down, keys, value_rows, both))
        held = exchange(select(refresh, got), "z")

    with jax.named_scope("keys_values"):
        mixed = lax.dot_general(both, out_weight, (((1,), (1,)), ((), ())), preferred_element_type=F32)
        values = project_values(value_rows, mixed[:VEC] + mixed[VEC:])

    with jax.named_scope("queries"):
        held, mixed = together((held, mixed))
        held = held.reshape(SLOTS * 4 * CHUNK, HEADS_HERE * HEAD_DIM)
        first, second = held[:, : HALF * HEAD_DIM], held[:, HALF * HEAD_DIM :]
        qa = [shift(first, "y", k) for k in range(4)]
        qb = [shift(second, "x", k) for k in range(4)]
        qa, qb, values = together((qa, qb, values))
        qa, qb = jnp.concatenate(qa, axis=0), jnp.concatenate(qb, axis=0)

    with jax.named_scope("attention"):
        back_a, back_b = [None] * 4, [None] * 4
        got_a, got_b = [qa] + [None] * 3, [qb] + [None] * 3
        for k in (1, 3):
            got_a[k], got_b[k] = shift(qa, "x", k), shift(qb, "y", k)
        back_a[0], back_b[0] = attend(qa, qb, keys, values)
        qa, qb, back_a[0], back_b[0] = together((qa, qb, back_a[0], back_b[0]))
        got_a[2], got_b[2] = shift(qa, "x", 2), shift(qb, "y", 2)
        for k in (1, 3, 2):
            out_a, out_b = attend(got_a[k], got_b[k], keys, values)
            back_a[k], back_b[k] = shift(out_a, "x", -k), shift(out_b, "y", -k)
            if k == 1:
                got_a[3], got_b[3], _ = together((got_a[3], got_b[3], out_a))
            if k == 3:
                got_a[2], got_b[2], back_a[1], back_b[1], _ = together(
                    (got_a[2], got_b[2], back_a[1], back_b[1], out_a)
                )
        parts_a, parts_b = merge_first(here, back_a, back_b)
        part = merge_second(exchange(parts_a, "y"), exchange(parts_b, "x"))
        term = merge_last(exchange(part, "z"))

    with jax.named_scope("velocity"):
        term = jnp.sum(lax.all_gather(term, HEAD), axis=0)
        term = exchange(spread_out(term), "y")
        gathered = exchange(spread_out(term), "x")

    with jax.named_scope("decode"):
        weight = conv_weight.transpose(1, 2, 3, 0)
        return decode(
            refresh, here, noise_level, gathered, base, up, down, weight, conv_bias.reshape(1, -1)
        )


def solution(mesh):
    wide = Mesh(mesh.devices.reshape(4, 4, 4, 2, 2), PATCH + HEAD)
    return jax.shard_map(
        on_device,
        mesh=wide,
        in_specs=(
            P(PATCH, None, HEAD),
            P(PATCH, None, HEAD),
            P(PATCH, None),
            P(),
            P(HEAD, None),
            P(),
            P(),
            P(),
            P(),
            P(PATCH, None, None),
            P(PATCH, None, None),
            P(HEAD, None, None, None),
            P(HEAD),
        ),
        out_specs=P(PATCH, HEAD, None),
        check_vma=False,
    )
```

```python
import functools
import math

import jax
import jax.numpy as jnp
from jax import lax
from jax.experimental import pallas as pl
from jax.experimental.pallas import tpu as pltpu
from jax.sharding import Mesh
from jax.sharding import PartitionSpec as P

HEAD_DIM = 128
LAT_CH = 16
PATCHES = 64
SLOTS = 4
HEADS_HERE = 6
HALF = 3
VEC = 64
ROWS = HALF * VEC
PACK = ROWS + 16
KEYS = 512
COLS = 1024
CHUNK = 8
F32 = jnp.float32
BF16 = jnp.bfloat16
PATCH = ("y", "x", "z")
HEAD = ("w", "c")
BITS = {"y": 4, "x": 2, "z": 0}


def shift(value, axis, step):
    if step == 0:
        return value
    return lax.ppermute(value, axis, [(i, (i + step) % 4) for i in range(4)])


def spread_out(value, count):
    return jnp.broadcast_to(value[None], (count,) + value.shape)


def exchange(value, axis):
    return lax.all_to_all(value, axis, 0, 0)


def cost(flops, moved_bytes, exps=0):
    return pl.CostEstimate(flops=flops, bytes_accessed=moved_bytes, transcendentals=exps)


SMEM = pl.BlockSpec(memory_space=pltpu.SMEM)
VMEM = pl.BlockSpec(memory_space=pltpu.VMEM)


def split(value):
    high = value.astype(BF16)
    return high, (value - high.astype(F32)).astype(BF16)


def select_kernel(refresh_ref, got_ref, o_ref):
    for slot in range(SLOTS):
        rows = got_ref[refresh_ref[slot]]
        for k in range(o_ref.shape[0]):
            o_ref[k, slot * CHUNK : (slot + 1) * CHUNK, :] = rows


def select(refresh, got):
    width = got.shape[2]
    return pl.pallas_call(
        select_kernel,
        in_specs=[SMEM, VMEM],
        out_shape=jax.ShapeDtypeStruct((16, SLOTS * CHUNK, width), BF16),
        cost_estimate=cost(0, 17 * SLOTS * CHUNK * width * 2),
        name="select",
    )(refresh, got)


def values_kernel(v_ref, w_ref, o_ref):
    for h in range(HEADS_HERE):
        cols = slice(h * HEAD_DIM, (h + 1) * HEAD_DIM)
        left = jnp.concatenate(split(w_ref[:, cols]), axis=0)
        both = lax.dot_general(
            left, v_ref[:, cols], (((1,), (1,)), ((), ())), preferred_element_type=F32
        )
        high, low = split(both[:VEC] + both[VEC:])
        o_ref[h, :VEC, :] = high
        o_ref[h, VEC:, :] = low


def project_values(value_rows, mixed):
    return pl.pallas_call(
        values_kernel,
        out_shape=jax.ShapeDtypeStruct((HEADS_HERE, 2 * VEC, KEYS), BF16),
        cost_estimate=cost(4 * KEYS * VEC * HEAD_DIM * HEADS_HERE, 4 * KEYS * 768),
        name="values",
    )(value_rows, mixed)


def base_kernel(refresh_ref, me_ref, level_ref, plain_ref, noisy_ref, cache_ref, o_ref, *rest):
    first_ref, last_ref, block_ref = rest
    row = lax.broadcasted_iota(jnp.int32, (256, 256), 0)
    col = lax.broadcasted_iota(jnp.int32, (256, 256), 1)
    choose = ((row % 128) * 2 + row // 128 == col).astype(F32).astype(BF16)
    stacked = []
    for i in range(4):
        block_ref[i] = plain_ref[:, i * 128 : (i + 1) * 128]
        pieces = []
        for b in range(2):
            parts = [block_ref[i, pl.ds(a * 2 + b, LAT_CH, 4), :] for a in range(2)]
            pieces.append(jnp.concatenate(parts, axis=0))
        stacked.append(jnp.concatenate(pieces, axis=1))
    left = jnp.concatenate(stacked, axis=0)
    high, rest = left.astype(BF16), left - left.astype(BF16).astype(F32)
    mid, low = split(rest)
    field = sum(jnp.dot(part, choose, preferred_element_type=F32) for part in (high, mid, low))
    field = jnp.concatenate([field[i * 32 : (i + 1) * 32] for i in range(4)], axis=1)
    fresh = False
    for slot in range(SLOTS):
        fresh = fresh | (refresh_ref[slot] == me_ref[0])
    level = level_ref[0]
    for a in range(2):
        rows = slice(a * LAT_CH, (a + 1) * LAT_CH)
        velocity = jnp.where(fresh, field[rows], cache_ref[a].astype(F32))
        latent = noisy_ref[a].astype(F32) - level * velocity
        o_ref[rows, :] = latent
        (first_ref, last_ref)[a][...] = latent


def latent_base(refresh, me, level, plain, noisy, cache):
    edge = jax.ShapeDtypeStruct((LAT_CH, COLS), F32)
    return pl.pallas_call(
        base_kernel,
        in_specs=[SMEM] * 3 + [VMEM] * 3,
        out_shape=(jax.ShapeDtypeStruct((2 * LAT_CH, COLS), F32), edge, edge),
        scratch_shapes=[pltpu.VMEM((4, VEC, 128), F32)],
        cost_estimate=cost(6 * 128 * 256 * 256, 1 << 19),
        name="latent_base",
    )(refresh, me, level, plain, noisy, cache)


def pack_lse(entries, width):
    row = lax.broadcasted_iota(jnp.int32, (16, width), 0)
    block = jnp.zeros((16, width), F32)
    for h, lse in enumerate(entries):
        high = lse.astype(BF16).astype(F32)
        rest = lse - high
        mid = rest.astype(BF16).astype(F32)
        low = rest - mid
        for part, value in enumerate((high, mid, low)):
            block = jnp.where(row == part * HALF + h, jnp.broadcast_to(value, block.shape), block)
    return block.astype(BF16)


def attend_kernel(q_ref, k_ref, v_ref, o_ref):
    scale = math.log2(math.e) / math.sqrt(HEAD_DIM)

    def scores(head):
        cols = slice(head * HEAD_DIM, (head + 1) * HEAD_DIM)
        return lax.dot_general(
            k_ref[:, cols], q_ref[:, cols], (((1,), (1,)), ((), ())), preferred_element_type=F32
        )

    dots, lses = scores(0), []
    for head in range(HEADS_HERE):
        half, h = divmod(head, HALF)
        following = scores(head + 1) if head + 1 < HEADS_HERE else None
        top = jnp.max(dots, axis=0, keepdims=True)
        exps = jnp.exp2((dots - top) * scale)
        total = jnp.sum(exps, axis=0, keepdims=True)
        parts = jnp.dot(v_ref[head], exps.astype(BF16), preferred_element_type=F32)
        row = half * PACK + h * VEC
        o_ref[row : row + VEC, :] = ((parts[:VEC] + parts[VEC:]) * (1.0 / total)).astype(BF16)
        lses.append(top * (1.0 / math.sqrt(HEAD_DIM)) + jnp.log(total))
        if h == HALF - 1:
            o_ref[half * PACK + ROWS : (half + 1) * PACK, :] = pack_lse(lses, o_ref.shape[1])
            lses = []
        dots = following


def attend(queries, keys, values):
    n = queries.shape[0]
    return pl.pallas_call(
        attend_kernel,
        out_shape=jax.ShapeDtypeStruct((2 * PACK, n), BF16),
        cost_estimate=cost(
            4 * n * KEYS * HEAD_DIM * HEADS_HERE, 4 * n * 768 + 4 * KEYS * 768, n * KEYS * HEADS_HERE
        ),
        name="attend",
    )(queries, keys, values)


def merge(parts_of):
    blocks = [p(ROWS, PACK).astype(F32) for p in parts_of]
    outs, lses = [], []
    for h in range(HALF):
        parts = [
            b[h : h + 1] + b[HALF + h : HALF + h + 1] + b[2 * HALF + h : 2 * HALF + h + 1] for b in blocks
        ]
        top = functools.reduce(jnp.maximum, parts)
        weights = [jnp.exp(p - top) for p in parts]
        total = sum(weights)
        inverse = 1.0 / total
        acc = 0.0
        for p, w in zip(parts_of, weights):
            acc = acc + p(h * VEC, (h + 1) * VEC).astype(F32) * (w * inverse)
        outs.append(acc)
        lses.append(top + jnp.log(total))
    return outs, lses


def merge_first_kernel(*refs):
    o_ref = refs[4]
    for base in (0, PACK):
        outs, lses = merge([lambda a, b, r=r: r[base + a : base + b, :] for r in refs[:4]])
        packed = pack_lse(lses, KEYS)
        for k in range(4):
            cols = slice(k * 128, (k + 1) * 128)
            for h in range(HALF):
                o_ref[k, base + h * VEC : base + (h + 1) * VEC, :] = outs[h][:, cols].astype(BF16)
            o_ref[k, base + ROWS : base + PACK, :] = packed[:, cols]


def merge_first(parts):
    return pl.pallas_call(
        merge_first_kernel,
        out_shape=jax.ShapeDtypeStruct((4, 2 * PACK, 128), BF16),
        cost_estimate=cost(8 * PACK * KEYS * 2, 10 * PACK * KEYS * 2),
        name="merge_first",
    )(*parts)


def merge_second_kernel(p_ref, o_ref):
    for base in (0, PACK):
        outs, lses = merge([lambda a, b, k=k: p_ref[k, base + a : base + b, :] for k in range(4)])
        packed = pack_lse(lses, 128)
        for k in range(4):
            for h in range(HALF):
                o_ref[k, base + h * VEC : base + (h + 1) * VEC, :] = outs[h].astype(BF16)
            o_ref[k, base + ROWS : base + PACK, :] = packed


def merge_second(parts):
    return pl.pallas_call(
        merge_second_kernel,
        out_shape=jax.ShapeDtypeStruct((4, 2 * PACK, 128), BF16),
        cost_estimate=cost(8 * PACK * 128 * 2, 16 * PACK * 128 * 2),
        name="merge_second",
    )(parts)


def merge_last_kernel(p_ref, o_ref):
    outs = []
    for base in (0, PACK):
        outs += merge([lambda a, b, k=k: p_ref[k, base + a : base + b, :] for k in range(4)])[0]
    o_ref[...] = sum(outs[1:], outs[0])


def merge_last(parts):
    return pl.pallas_call(
        merge_last_kernel,
        out_shape=jax.ShapeDtypeStruct((VEC, 128), F32),
        cost_estimate=cost(8 * PACK * 128 * 2, 10 * PACK * 128),
        name="merge_last",
    )(parts)


def decode_kernel(refresh_ref, me_ref, level_ref, v_ref, base_ref, up_ref, down_ref, w_ref, b_ref, o_ref):
    level, me = level_ref[0], me_ref[0]
    row = lax.broadcasted_iota(jnp.int32, (512, 128), 0)
    col = lax.broadcasted_iota(jnp.int32, (512, 128), 1)
    lane = row % 128
    target = (row // 256) * 64 + ((lane // 32) * 8 + lane % 8) * 2 + (row // 128) % 2

    def attention_rows(near, kinds):
        slot, on = 0, 0
        for s in range(SLOTS):
            hit = refresh_ref[s] == me + near
            slot = jnp.where(hit, s, slot)
            on = jnp.where(hit, 1, on)
        choose = (((lane // 8) % 4 == slot) & (target == col)).astype(F32).astype(BF16)
        count = LAT_CH * len(kinds)
        stacked = []
        for ys in range(4):
            for pair in range(2):
                pieces = []
                for xs in (pair * 2, pair * 2 + 1):
                    for b in range(2):
                        parts = [v_ref[ys * 4 + xs, pl.ds(kind * 2 + b, LAT_CH, 4), :] for kind in kinds]
                        pieces.append(jnp.concatenate(parts, axis=0))
                stacked.append(jnp.concatenate(pieces, axis=1))
        high, low = split(jnp.concatenate(stacked, axis=0))
        field = jnp.dot(high, choose, preferred_element_type=F32) + jnp.dot(
            low, choose, preferred_element_type=F32
        )
        field = jnp.concatenate([field[i * count : (i + 1) * count] for i in range(8)], axis=1)
        return jnp.where(on > 0, field, 0.0)

    own = base_ref[...] - level * attention_rows(0, (0, 1))
    up = up_ref[...] - level * attention_rows(-1, (1,))
    down = down_ref[...] - level * attention_rows(1, (0,))
    latent = jnp.concatenate([up, own, down], axis=0) / 0.3611 + 0.1159
    line = lax.broadcasted_iota(jnp.int32, latent.shape, 0)
    column = lax.broadcasted_iota(jnp.int32, latent.shape, 1)
    inside = ((line >= 16) | (me > 0)) & ((line < 48) | (me < PATCHES - 1))
    latent = jnp.where(inside, latent, 0.0)
    before = jnp.where(column == 0, 0.0, pltpu.roll(latent, 1, 1)).astype(BF16)
    after = jnp.where(column == COLS - 1, 0.0, pltpu.roll(latent, COLS - 1, 1)).astype(BF16)
    middle = latent.astype(BF16)

    channels = w_ref.shape[3]
    line = lax.broadcasted_iota(jnp.int32, (16, channels), 0)
    bias = jnp.broadcast_to(b_ref[...], (16, channels))
    high = bias.astype(BF16).astype(F32)
    mid = (bias - high).astype(BF16).astype(F32)
    bias = jnp.where(line == 0, high, jnp.where(line == 1, mid, jnp.where(line == 2, bias - high - mid, 0.0)))
    weight = [w_ref[u, v] for v in range(3) for u in range(3)] + [bias.astype(BF16)]
    weight = jnp.concatenate(weight, axis=0)
    ones = jnp.ones((16, COLS), BF16)
    for r in range(2):
        stencil = [s[r * 16 : r * 16 + 48] for s in (before, middle, after)] + [ones]
        out = lax.dot_general(
            weight, jnp.concatenate(stencil, axis=0), (((0,), (0,)), ((), ())), preferred_element_type=F32
        )
        o_ref[r] = out.astype(BF16)


def decode(refresh, me, level, gathered, base, up, down, weight, bias):
    return pl.pallas_call(
        decode_kernel,
        out_shape=jax.ShapeDtypeStruct((2, weight.shape[3], COLS), BF16),
        in_specs=[SMEM] * 3 + [VMEM] * 6,
        out_specs=VMEM,
        cost_estimate=cost(4 * 128 * 160 * 1024, 2 << 20),
        name="decode",
    )(refresh, me, level, gathered, base, up, down, weight, bias)


def on_device(
    fresh_qkv,
    kv_cache,
    hidden,
    refresh,
    out_weight,
    final_weight,
    final_bias,
    gate_scale,
    noise_level,
    noisy_latent,
    velocity_cache,
    conv_weight,
    conv_bias,
):
    me = lax.axis_index(PATCH).astype(jnp.int32)
    here = me.reshape(1)
    together = lax.optimization_barrier

    with jax.named_scope("queries"):
        own = fresh_qkv[:, 0].reshape(PATCHES, CHUNK, -1)
        own, fresh_qkv = together((own, fresh_qkv))
        got = exchange(own, PATCH)

    with jax.named_scope("latent_base"):
        plain = lax.dot_general(
            final_weight, hidden, (((0,), (1,)), ((), ())), preferred_element_type=F32
        )
        plain = plain + final_bias[:, None]
        base, edge_first, edge_last = latent_base(
            refresh, here, noise_level, plain, noisy_latent, velocity_cache
        )

    with jax.named_scope("keys_values"):
        refreshed = jnp.any(refresh == me)
        keys = jnp.where(refreshed, fresh_qkv[:, 1], kv_cache[:, 0])
        value_rows = jnp.where(refreshed, fresh_qkv[:, 2], kv_cache[:, 1])
        gated = final_weight.T.astype(F32) * gate_scale[None, :]
        high = lax.reduce_precision(gated, 8, 7)
        both = jnp.concatenate([high, gated - high], axis=0).astype(BF16)

    with jax.named_scope("queries"):
        got, base, keys, value_rows, both = together((got, base, keys, value_rows, both))
        held = select(refresh, got)
        held, edge_first, edge_last = together((held, edge_first, edge_last))
        held = exchange(held, ("y", "z"))

    with jax.named_scope("keys_values"):
        mixed = lax.dot_general(both, out_weight, (((1,), (1,)), ((), ())), preferred_element_type=F32)
        values = project_values(value_rows, mixed[:VEC] + mixed[VEC:])

    with jax.named_scope("latent_base"):
        up = lax.ppermute(edge_last, PATCH, [(p, p + 1) for p in range(PATCHES - 1)])
        down = lax.ppermute(edge_first, PATCH, [(p + 1, p) for p in range(PATCHES - 1)])

    with jax.named_scope("attention"):
        held, values, up, down = together((held, values, up, down))
        queries = held.reshape(16 * SLOTS * CHUNK, HEADS_HERE * HEAD_DIM)
        got, back = [queries] + [None] * 3, [None] * 4
        for k in (1, 3, 2):
            got[k] = shift(queries, "x", k)
        for k in (0, 1, 3, 2):
            out = attend(got[k], keys, values)
            back[k] = shift(out, "x", -k)
            if k == 0:
                got[1], _ = together((got[1], out))
            if k == 1:
                got[3], _ = together((got[3], out))
            if k == 3:
                got[2], back[1], _ = together((got[2], back[1], out))
        part = merge_second(exchange(merge_first(back), "y"))
        term = merge_last(exchange(part, "z"))

    with jax.named_scope("velocity"):
        term = jnp.sum(lax.all_gather(term, HEAD), axis=0)
        gathered = exchange(spread_out(term, 16), ("y", "x"))

    with jax.named_scope("decode"):
        weight = conv_weight.transpose(1, 2, 3, 0)
        return decode(
            refresh, here, noise_level, gathered, base, up, down, weight, conv_bias.reshape(1, -1)
        )


def solution(mesh):
    wide = Mesh(mesh.devices.reshape(4, 4, 4, 2, 2), PATCH + HEAD)
    return jax.shard_map(
        on_device,
        mesh=wide,
        in_specs=(
            P(PATCH, None, HEAD),
            P(PATCH, None, HEAD),
            P(PATCH, None),
            P(),
            P(HEAD, None),
            P(),
            P(),
            P(),
            P(),
            P(PATCH, None, None),
            P(PATCH, None, None),
            P(HEAD, None, None, None),
            P(HEAD),
        ),
        out_specs=P(PATCH, HEAD, None),
        check_vma=False,
    )
```

```python
import functools
import math

import jax
import jax.numpy as jnp
from jax import lax
from jax.experimental import pallas as pl
from jax.experimental.pallas import tpu as pltpu
from jax.sharding import Mesh
from jax.sharding import PartitionSpec as P

HEAD_DIM = 128
LAT_CH = 16
PATCHES = 64
SLOTS = 4
HEADS_HERE = 6
HALF = 3
VEC = 64
ROWS = HALF * VEC
PACK = ROWS + 16
KEYS = 512
COLS = 1024
CHUNK = 8
F32 = jnp.float32
BF16 = jnp.bfloat16
PATCH = ("yh", "yl", "xh", "xl", "z")
HEAD = ("w", "c")


def mirror(value, flip_y, flip_x):
    pairs = []
    for p in range(PATCHES):
        y, x, z = p // 16, (p // 4) % 4, p % 4
        pairs.append((p, (3 - y if flip_y else y) * 16 + (3 - x if flip_x else x) * 4 + z))
    return lax.ppermute(value, PATCH, pairs)


def spread_out(value, count):
    return jnp.broadcast_to(value[None], (count,) + value.shape)


def exchange(value, axis):
    return lax.all_to_all(value, axis, 0, 0)


def cost(flops, moved_bytes, exps=0):
    return pl.CostEstimate(flops=flops, bytes_accessed=moved_bytes, transcendentals=exps)


SMEM = pl.BlockSpec(memory_space=pltpu.SMEM)
VMEM = pl.BlockSpec(memory_space=pltpu.VMEM)


def split(value):
    high = value.astype(BF16)
    return high, (value - high.astype(F32)).astype(BF16)


def select_kernel(refresh_ref, got_ref, o_ref):
    for slot in range(SLOTS):
        rows = got_ref[refresh_ref[slot]]
        for k in range(o_ref.shape[0]):
            o_ref[k, slot * CHUNK : (slot + 1) * CHUNK, :] = rows


def select(refresh, got):
    width = got.shape[2]
    return pl.pallas_call(
        select_kernel,
        in_specs=[SMEM, VMEM],
        out_shape=jax.ShapeDtypeStruct((16, SLOTS * CHUNK, width), BF16),
        cost_estimate=cost(0, 17 * SLOTS * CHUNK * width * 2),
        name="select",
    )(refresh, got)


def values_kernel(v_ref, w_ref, o_ref):
    for h in range(HEADS_HERE):
        cols = slice(h * HEAD_DIM, (h + 1) * HEAD_DIM)
        left = jnp.concatenate(split(w_ref[:, cols]), axis=0)
        both = lax.dot_general(
            left, v_ref[:, cols], (((1,), (1,)), ((), ())), preferred_element_type=F32
        )
        o_ref[h * VEC : (h + 1) * VEC, :] = (both[:VEC] + both[VEC:]).astype(BF16)


def project_values(value_rows, mixed):
    return pl.pallas_call(
        values_kernel,
        out_shape=jax.ShapeDtypeStruct((HEADS_HERE * VEC, KEYS), BF16),
        cost_estimate=cost(4 * KEYS * VEC * HEAD_DIM * HEADS_HERE, 4 * KEYS * 768),
        name="values",
    )(value_rows, mixed)


def base_kernel(refresh_ref, me_ref, level_ref, plain_ref, noisy_ref, cache_ref, o_ref, *rest):
    first_ref, last_ref, block_ref = rest
    row = lax.broadcasted_iota(jnp.int32, (256, 256), 0)
    col = lax.broadcasted_iota(jnp.int32, (256, 256), 1)
    choose = ((row % 128) * 2 + row // 128 == col).astype(F32).astype(BF16)
    stacked = []
    for i in range(4):
        block_ref[i] = plain_ref[:, i * 128 : (i + 1) * 128]
        pieces = []
        for b in range(2):
            parts = [block_ref[i, pl.ds(a * 2 + b, LAT_CH, 4), :] for a in range(2)]
            pieces.append(jnp.concatenate(parts, axis=0))
        stacked.append(jnp.concatenate(pieces, axis=1))
    left = jnp.concatenate(stacked, axis=0)
    high, rest = left.astype(BF16), left - left.astype(BF16).astype(F32)
    mid, low = split(rest)
    field = sum(jnp.dot(part, choose, preferred_element_type=F32) for part in (high, mid, low))
    field = jnp.concatenate([field[i * 32 : (i + 1) * 32] for i in range(4)], axis=1)
    fresh = False
    for slot in range(SLOTS):
        fresh = fresh | (refresh_ref[slot] == me_ref[0])
    level = level_ref[0]
    for a in range(2):
        rows = slice(a * LAT_CH, (a + 1) * LAT_CH)
        velocity = jnp.where(fresh, field[rows], cache_ref[a].astype(F32))
        latent = noisy_ref[a].astype(F32) - level * velocity
        o_ref[rows, :] = latent
        (first_ref, last_ref)[a][...] = latent


def latent_base(refresh, me, level, plain, noisy, cache):
    edge = jax.ShapeDtypeStruct((LAT_CH, COLS), F32)
    return pl.pallas_call(
        base_kernel,
        in_specs=[SMEM] * 3 + [VMEM] * 3,
        out_shape=(jax.ShapeDtypeStruct((2 * LAT_CH, COLS), F32), edge, edge),
        scratch_shapes=[pltpu.VMEM((4, VEC, 128), F32)],
        cost_estimate=cost(6 * 128 * 256 * 256, 1 << 19),
        name="latent_base",
    )(refresh, me, level, plain, noisy, cache)


def pack_lse(entries, width):
    row = lax.broadcasted_iota(jnp.int32, (16, width), 0)
    block = jnp.zeros((16, width), F32)
    for h, lse in enumerate(entries):
        high = lse.astype(BF16).astype(F32)
        rest = lse - high
        mid = rest.astype(BF16).astype(F32)
        low = rest - mid
        for part, value in enumerate((high, mid, low)):
            block = jnp.where(row == part * HALF + h, jnp.broadcast_to(value, block.shape), block)
    return block.astype(BF16)


def attend_kernel(first, last, *refs):
    q_ref, v_ref, state_in, outs = refs[0], refs[1], None, refs[2:]
    if not first:
        state_in, outs = outs[:3], outs[3:]
    k_refs, outs = outs[: 2 if last else 1], outs[2 if last else 1 :]
    scale = math.log2(math.e) / math.sqrt(HEAD_DIM)

    def scores(head):
        cols = slice(head * HEAD_DIM, (head + 1) * HEAD_DIM)
        keys = [k[:, cols] for k in k_refs]
        keys = keys[0] if len(keys) == 1 else jnp.concatenate(keys, axis=0)
        return lax.dot_general(
            keys, q_ref[:, cols], (((1,), (1,)), ((), ())), preferred_element_type=F32
        )

    dots, lses = scores(0), []
    for head in range(HEADS_HERE):
        half, h = divmod(head, HALF)
        following = scores(head + 1) if head + 1 < HEADS_HERE else None
        rows = slice(head * VEC, (head + 1) * VEC)
        top = jnp.max(dots, axis=0, keepdims=True)
        if not first:
            old_top = state_in[1][head : head + 1, :]
            top = jnp.maximum(top, old_top)
        exps = jnp.exp2((dots - top) * scale)
        total = jnp.sum(exps, axis=0, keepdims=True)
        acc = jnp.dot(v_ref[rows, :], exps.astype(BF16), preferred_element_type=F32)
        if not first:
            shrink = jnp.exp2((old_top - top) * scale)
            total = total + state_in[2][head : head + 1, :] * shrink
            acc = acc + state_in[0][rows, :] * shrink
        if not last:
            outs[0][rows, :] = acc
            outs[1][head : head + 1, :] = top
            outs[2][head : head + 1, :] = total
        else:
            out = (acc * (1.0 / total)).astype(BF16)
            row = half * PACK + h * VEC
            for k in range(4):
                outs[0][k, row : row + VEC, :] = out[:, k * 128 : (k + 1) * 128]
            lses.append(top * (1.0 / math.sqrt(HEAD_DIM)) + jnp.log(total))
            if h == HALF - 1:
                packed = pack_lse(lses, out.shape[1])
                for k in range(4):
                    outs[0][k, half * PACK + ROWS : (half + 1) * PACK, :] = packed[:, k * 128 : (k + 1) * 128]
                lses = []
        dots = following


def attend(queries, values, state, keys):
    n = queries.shape[0]
    first, last = state is None, len(keys) == 2
    if last:
        out = jax.ShapeDtypeStruct((4, 2 * PACK, n // 4), BF16)
    else:
        rows = jax.ShapeDtypeStruct((8, n), F32)
        out = (jax.ShapeDtypeStruct((2 * ROWS, n), F32), rows, rows)
    return pl.pallas_call(
        functools.partial(attend_kernel, first, last),
        out_shape=out,
        cost_estimate=cost(
            4 * n * KEYS * HEAD_DIM * HEADS_HERE, 4 * n * 768 + 4 * KEYS * 768, n * KEYS * HEADS_HERE
        ),
        name="attend",
    )(queries, values, *(() if first else state), *keys)


def merge(parts_of):
    blocks = [p(ROWS, PACK).astype(F32) for p in parts_of]
    outs, lses = [], []
    for h in range(HALF):
        parts = [
            b[h : h + 1] + b[HALF + h : HALF + h + 1] + b[2 * HALF + h : 2 * HALF + h + 1] for b in blocks
        ]
        top = functools.reduce(jnp.maximum, parts)
        weights = [jnp.exp(p - top) for p in parts]
        total = sum(weights)
        inverse = 1.0 / total
        acc = 0.0
        for p, w in zip(parts_of, weights):
            acc = acc + p(h * VEC, (h + 1) * VEC).astype(F32) * (w * inverse)
        outs.append(acc)
        lses.append(top + jnp.log(total))
    return outs, lses


def merge_second_kernel(p_ref, o_ref):
    for base in (0, PACK):
        outs, lses = merge([lambda a, b, k=k: p_ref[k, base + a : base + b, :] for k in range(4)])
        packed = pack_lse(lses, 128)
        for k in range(4):
            for h in range(HALF):
                o_ref[k, base + h * VEC : base + (h + 1) * VEC, :] = outs[h].astype(BF16)
            o_ref[k, base + ROWS : base + PACK, :] = packed


def merge_second(parts):
    return pl.pallas_call(
        merge_second_kernel,
        out_shape=jax.ShapeDtypeStruct((4, 2 * PACK, 128), BF16),
        cost_estimate=cost(8 * PACK * 128 * 2, 16 * PACK * 128 * 2),
        name="merge_second",
    )(parts)


def merge_last_kernel(p_ref, o_ref):
    outs = []
    for base in (0, PACK):
        outs += merge([lambda a, b, k=k: p_ref[k, base + a : base + b, :] for k in range(4)])[0]
    o_ref[...] = sum(outs[1:], outs[0])


def merge_last(parts):
    return pl.pallas_call(
        merge_last_kernel,
        out_shape=jax.ShapeDtypeStruct((VEC, 128), F32),
        cost_estimate=cost(8 * PACK * 128 * 2, 10 * PACK * 128),
        name="merge_last",
    )(parts)


def decode_kernel(refresh_ref, me_ref, level_ref, v_ref, base_ref, up_ref, down_ref, w_ref, b_ref, o_ref):
    level, me = level_ref[0], me_ref[0]
    row = lax.broadcasted_iota(jnp.int32, (512, 128), 0)
    col = lax.broadcasted_iota(jnp.int32, (512, 128), 1)
    lane = row % 128
    target = (row // 256) * 64 + ((lane // 32) * 8 + lane % 8) * 2 + (row // 128) % 2

    def attention_rows(near, kinds):
        slot, on = 0, 0
        for s in range(SLOTS):
            hit = refresh_ref[s] == me + near
            slot = jnp.where(hit, s, slot)
            on = jnp.where(hit, 1, on)
        choose = (((lane // 8) % 4 == slot) & (target == col)).astype(F32).astype(BF16)
        count = LAT_CH * len(kinds)
        stacked = []
        for ys in range(4):
            for pair in range(2):
                pieces = []
                for xs in (pair * 2, pair * 2 + 1):
                    for b in range(2):
                        parts = [v_ref[ys * 4 + xs, pl.ds(kind * 2 + b, LAT_CH, 4), :] for kind in kinds]
                        pieces.append(jnp.concatenate(parts, axis=0))
                stacked.append(jnp.concatenate(pieces, axis=1))
        high, low = split(jnp.concatenate(stacked, axis=0))
        field = jnp.dot(high, choose, preferred_element_type=F32) + jnp.dot(
            low, choose, preferred_element_type=F32
        )
        field = jnp.concatenate([field[i * count : (i + 1) * count] for i in range(8)], axis=1)
        return jnp.where(on > 0, field, 0.0)

    own = base_ref[...] - level * attention_rows(0, (0, 1))
    up = up_ref[...] - level * attention_rows(-1, (1,))
    down = down_ref[...] - level * attention_rows(1, (0,))
    latent = jnp.concatenate([up, own, down], axis=0) / 0.3611 + 0.1159
    line = lax.broadcasted_iota(jnp.int32, latent.shape, 0)
    column = lax.broadcasted_iota(jnp.int32, latent.shape, 1)
    inside = ((line >= 16) | (me > 0)) & ((line < 48) | (me < PATCHES - 1))
    latent = jnp.where(inside, latent, 0.0)
    before = jnp.where(column == 0, 0.0, pltpu.roll(latent, 1, 1)).astype(BF16)
    after = jnp.where(column == COLS - 1, 0.0, pltpu.roll(latent, COLS - 1, 1)).astype(BF16)
    middle = latent.astype(BF16)

    channels = w_ref.shape[3]
    line = lax.broadcasted_iota(jnp.int32, (16, channels), 0)
    bias = jnp.broadcast_to(b_ref[...], (16, channels))
    high = bias.astype(BF16).astype(F32)
    mid = (bias - high).astype(BF16).astype(F32)
    bias = jnp.where(line == 0, high, jnp.where(line == 1, mid, jnp.where(line == 2, bias - high - mid, 0.0)))
    weight = [w_ref[u, v] for v in range(3) for u in range(3)] + [bias.astype(BF16)]
    weight = jnp.concatenate(weight, axis=0)
    ones = jnp.ones((16, COLS), BF16)
    for r in range(2):
        stencil = [s[r * 16 : r * 16 + 48] for s in (before, middle, after)] + [ones]
        out = lax.dot_general(
            weight, jnp.concatenate(stencil, axis=0), (((0,), (0,)), ((), ())), preferred_element_type=F32
        )
        o_ref[r] = out.astype(BF16)


def decode(refresh, me, level, gathered, base, up, down, weight, bias):
    return pl.pallas_call(
        decode_kernel,
        out_shape=jax.ShapeDtypeStruct((2, weight.shape[3], COLS), BF16),
        in_specs=[SMEM] * 3 + [VMEM] * 6,
        out_specs=VMEM,
        cost_estimate=cost(4 * 128 * 160 * 1024, 2 << 20),
        name="decode",
    )(refresh, me, level, gathered, base, up, down, weight, bias)


def on_device(
    fresh_qkv,
    kv_cache,
    hidden,
    refresh,
    out_weight,
    final_weight,
    final_bias,
    gate_scale,
    noise_level,
    noisy_latent,
    velocity_cache,
    conv_weight,
    conv_bias,
):
    me = lax.axis_index(PATCH).astype(jnp.int32)
    here = me.reshape(1)
    together = lax.optimization_barrier

    with jax.named_scope("queries"):
        own = fresh_qkv[:, 0].reshape(PATCHES, CHUNK, -1)
        own, fresh_qkv = together((own, fresh_qkv))
        got = exchange(own, PATCH)

    with jax.named_scope("keys_values"):
        refreshed = jnp.any(refresh == me)
        keys = jnp.where(refreshed, fresh_qkv[:, 1], kv_cache[:, 0])
        value_rows = jnp.where(refreshed, fresh_qkv[:, 2], kv_cache[:, 1])
        keys_x, keys_y = mirror(keys, 0, 1), mirror(keys, 1, 0)

    with jax.named_scope("latent_base"):
        plain = lax.dot_general(
            final_weight, hidden, (((0,), (1,)), ((), ())), preferred_element_type=F32
        )
        plain = plain + final_bias[:, None]
        base, edge_first, edge_last = latent_base(
            refresh, here, noise_level, plain, noisy_latent, velocity_cache
        )
        up = lax.ppermute(edge_last, PATCH, [(p, p + 1) for p in range(PATCHES - 1)])
        down = lax.ppermute(edge_first, PATCH, [(p + 1, p) for p in range(PATCHES - 1)])

    with jax.named_scope("queries"):
        got, base, up, down, keys_x, keys_y = together((got, base, up, down, keys_x, keys_y))
        held = exchange(select(refresh, got), ("yl", "xl", "z"))

    with jax.named_scope("keys_values"):
        gated = final_weight.T.astype(F32) * gate_scale[None, :]
        high = lax.reduce_precision(gated, 8, 7)
        both = jnp.concatenate([high, gated - high], axis=0).astype(BF16)
        mixed = lax.dot_general(both, out_weight, (((1,), (1,)), ((), ())), preferred_element_type=F32)
        values = project_values(value_rows, mixed[:VEC] + mixed[VEC:])
        half = KEYS // 2
        keys_far = mirror(keys_x[:half], 1, 0), mirror(keys_y[half:], 0, 1)
        blocks = [
            (values, (keys,)),
            (mirror(values, 0, 1), (keys_x,)),
            (mirror(values, 1, 0), (keys_y,)),
            (mirror(values, 1, 1), keys_far),
        ]

    with jax.named_scope("attention"):
        held, values = together((held, values))
        queries = held.reshape(16 * SLOTS * CHUNK, HEADS_HERE * HEAD_DIM)
        state = None
        for k, (values, keys) in enumerate(blocks):
            if k:
                values, keys, state = together((values, keys, state))
            state = attend(queries, values, state, keys)
        part = merge_second(exchange(state, ("yl", "xl")))
        term = merge_last(exchange(part, "z"))

    with jax.named_scope("velocity"):
        term = jnp.sum(lax.all_gather(term, HEAD), axis=0)
        gathered = exchange(spread_out(term, 16), ("yh", "yl", "xh", "xl"))

    with jax.named_scope("decode"):
        weight = conv_weight.transpose(1, 2, 3, 0)
        return decode(
            refresh, here, noise_level, gathered, base, up, down, weight, conv_bias.reshape(1, -1)
        )


def solution(mesh):
    wide = Mesh(mesh.devices.reshape(2, 2, 2, 2, 4, 2, 2), PATCH + HEAD)
    return jax.shard_map(
        on_device,
        mesh=wide,
        in_specs=(
            P(PATCH, None, HEAD),
            P(PATCH, None, HEAD),
            P(PATCH, None),
            P(),
            P(HEAD, None),
            P(),
            P(),
            P(),
            P(),
            P(PATCH, None, None),
            P(PATCH, None, None),
            P(HEAD, None, None, None),
            P(HEAD),
        ),
        out_specs=P(PATCH, HEAD, None),
        check_vma=False,
    )
```

```python
import functools
import math

import jax
import jax.numpy as jnp
from jax import lax
from jax.experimental import pallas as pl
from jax.experimental.pallas import tpu as pltpu
from jax.sharding import Mesh
from jax.sharding import PartitionSpec as P

HEAD_DIM = 128
LAT_CH = 16
PATCHES = 64
SLOTS = 4
HEADS_HERE = 6
HALF = 3
VEC = 64
ROWS = HALF * VEC
PACK = ROWS + 16
KEYS = 512
COLS = 1024
CHUNK = 8
F32 = jnp.float32
BF16 = jnp.bfloat16
PATCH = ("yh", "yl", "xh", "xl", "z")
HEAD = ("w", "c")


def mirror(value, flip_y, flip_x):
    pairs = []
    for p in range(PATCHES):
        y, x, z = p // 16, (p // 4) % 4, p % 4
        pairs.append((p, (3 - y if flip_y else y) * 16 + (3 - x if flip_x else x) * 4 + z))
    return lax.ppermute(value, PATCH, pairs)


def spread_out(value, count):
    return jnp.broadcast_to(value[None], (count,) + value.shape)


def exchange(value, axis):
    return lax.all_to_all(value, axis, 0, 0)


def cost(flops, moved_bytes, exps=0):
    return pl.CostEstimate(flops=flops, bytes_accessed=moved_bytes, transcendentals=exps)


SMEM = pl.BlockSpec(memory_space=pltpu.SMEM)
VMEM = pl.BlockSpec(memory_space=pltpu.VMEM)


def split(value):
    high = value.astype(BF16)
    return high, (value - high.astype(F32)).astype(BF16)


def select_kernel(refresh_ref, got_ref, o_ref):
    for slot in range(SLOTS):
        rows = got_ref[refresh_ref[slot]]
        for k in range(o_ref.shape[0]):
            o_ref[k, slot * CHUNK : (slot + 1) * CHUNK, :] = rows


def select(refresh, got):
    width = got.shape[2]
    return pl.pallas_call(
        select_kernel,
        in_specs=[SMEM, VMEM],
        out_shape=jax.ShapeDtypeStruct((16, SLOTS * CHUNK, width), BF16),
        cost_estimate=cost(0, 17 * SLOTS * CHUNK * width * 2),
        name="select",
    )(refresh, got)


def values_kernel(v_ref, w_ref, o_ref):
    for h in range(HEADS_HERE):
        cols = slice(h * HEAD_DIM, (h + 1) * HEAD_DIM)
        left = jnp.concatenate(split(w_ref[:, cols]), axis=0)
        both = lax.dot_general(
            left, v_ref[:, cols], (((1,), (1,)), ((), ())), preferred_element_type=F32
        )
        o_ref[h * VEC : (h + 1) * VEC, :] = (both[:VEC] + both[VEC:]).astype(BF16)


def project_values(value_rows, mixed):
    return pl.pallas_call(
        values_kernel,
        out_shape=jax.ShapeDtypeStruct((HEADS_HERE * VEC, KEYS), BF16),
        cost_estimate=cost(4 * KEYS * VEC * HEAD_DIM * HEADS_HERE, 4 * KEYS * 768),
        name="values",
    )(value_rows, mixed)


def halves_kernel(x_ref, y_ref, a_ref, b_ref, sems):
    half = KEYS // 2
    copies = [
        pltpu.make_async_copy(x_ref.at[:half], a_ref, sems.at[0]),
        pltpu.make_async_copy(y_ref.at[half:], b_ref, sems.at[1]),
    ]
    for copy in copies:
        copy.start()
    for copy in copies:
        copy.wait()


def halves(keys_x, keys_y):
    anywhere = pl.BlockSpec(memory_space=pl.ANY)
    half = jax.ShapeDtypeStruct((KEYS // 2, keys_x.shape[1]), BF16)
    return pl.pallas_call(
        halves_kernel,
        in_specs=[anywhere] * 2,
        out_specs=(anywhere, anywhere),
        out_shape=(half, half),
        scratch_shapes=[pltpu.SemaphoreType.DMA((2,))],
        cost_estimate=cost(0, 2 * KEYS * keys_x.shape[1] * 2),
        name="halves",
    )(keys_x, keys_y)


def base_kernel(refresh_ref, me_ref, level_ref, plain_ref, noisy_ref, cache_ref, o_ref, *rest):
    first_ref, last_ref, block_ref = rest
    row = lax.broadcasted_iota(jnp.int32, (256, 256), 0)
    col = lax.broadcasted_iota(jnp.int32, (256, 256), 1)
    choose = ((row % 128) * 2 + row // 128 == col).astype(F32).astype(BF16)
    stacked = []
    for i in range(4):
        block_ref[i] = plain_ref[:, i * 128 : (i + 1) * 128]
        pieces = []
        for b in range(2):
            parts = [block_ref[i, pl.ds(a * 2 + b, LAT_CH, 4), :] for a in range(2)]
            pieces.append(jnp.concatenate(parts, axis=0))
        stacked.append(jnp.concatenate(pieces, axis=1))
    left = jnp.concatenate(stacked, axis=0)
    high, rest = left.astype(BF16), left - left.astype(BF16).astype(F32)
    mid, low = split(rest)
    field = sum(jnp.dot(part, choose, preferred_element_type=F32) for part in (high, mid, low))
    field = jnp.concatenate([field[i * 32 : (i + 1) * 32] for i in range(4)], axis=1)
    fresh = False
    for slot in range(SLOTS):
        fresh = fresh | (refresh_ref[slot] == me_ref[0])
    level = level_ref[0]
    for a in range(2):
        rows = slice(a * LAT_CH, (a + 1) * LAT_CH)
        velocity = jnp.where(fresh, field[rows], cache_ref[a].astype(F32))
        latent = noisy_ref[a].astype(F32) - level * velocity
        o_ref[rows, :] = latent
        (first_ref, last_ref)[a][...] = latent


def latent_base(refresh, me, level, plain, noisy, cache):
    edge = jax.ShapeDtypeStruct((LAT_CH, COLS), F32)
    return pl.pallas_call(
        base_kernel,
        in_specs=[SMEM] * 3 + [VMEM] * 3,
        out_shape=(jax.ShapeDtypeStruct((2 * LAT_CH, COLS), F32), edge, edge),
        scratch_shapes=[pltpu.VMEM((4, VEC, 128), F32)],
        cost_estimate=cost(6 * 128 * 256 * 256, 1 << 19),
        name="latent_base",
    )(refresh, me, level, plain, noisy, cache)


def pack_lse(entries, width):
    row = lax.broadcasted_iota(jnp.int32, (16, width), 0)
    block = jnp.zeros((16, width), F32)
    for h, lse in enumerate(entries):
        high = lse.astype(BF16).astype(F32)
        rest = lse - high
        mid = rest.astype(BF16).astype(F32)
        low = rest - mid
        for part, value in enumerate((high, mid, low)):
            block = jnp.where(row == part * HALF + h, jnp.broadcast_to(value, block.shape), block)
    return block.astype(BF16)


def attend_kernel(first, last, *refs):
    q_ref, v_ref, state_in, outs = refs[0], refs[1], None, refs[2:]
    if not first:
        state_in, outs = outs[:3], outs[3:]
    k_refs, outs = outs[: 2 if last else 1], outs[2 if last else 1 :]
    scale = math.log2(math.e) / math.sqrt(HEAD_DIM)

    def scores(head):
        cols = slice(head * HEAD_DIM, (head + 1) * HEAD_DIM)
        keys = [k[:, cols] for k in k_refs]
        keys = keys[0] if len(keys) == 1 else jnp.concatenate(keys, axis=0)
        return lax.dot_general(
            keys, q_ref[:, cols], (((1,), (1,)), ((), ())), preferred_element_type=F32
        )

    dots, lses = scores(0), []
    for head in range(HEADS_HERE):
        half, h = divmod(head, HALF)
        following = scores(head + 1) if head + 1 < HEADS_HERE else None
        rows = slice(head * VEC, (head + 1) * VEC)
        top = jnp.max(dots, axis=0, keepdims=True)
        if not first:
            old_top = state_in[1][head : head + 1, :]
            top = jnp.maximum(top, old_top)
        exps = jnp.exp2((dots - top) * scale)
        total = jnp.sum(exps, axis=0, keepdims=True)
        acc = jnp.dot(v_ref[rows, :], exps.astype(BF16), preferred_element_type=F32)
        if not first:
            shrink = jnp.exp2((old_top - top) * scale)
            total = total + state_in[2][head : head + 1, :] * shrink
            acc = acc + state_in[0][rows, :] * shrink
        if not last:
            outs[0][rows, :] = acc
            outs[1][head : head + 1, :] = top
            outs[2][head : head + 1, :] = total
        else:
            out = (acc * (1.0 / total)).astype(BF16)
            row = half * PACK + h * VEC
            for k in range(4):
                outs[0][k, row : row + VEC, :] = out[:, k * 128 : (k + 1) * 128]
            lses.append(top * (1.0 / math.sqrt(HEAD_DIM)) + jnp.log(total))
            if h == HALF - 1:
                packed = pack_lse(lses, out.shape[1])
                for k in range(4):
                    outs[0][k, half * PACK + ROWS : (half + 1) * PACK, :] = packed[:, k * 128 : (k + 1) * 128]
                lses = []
        dots = following


def attend(queries, values, state, keys):
    n = queries.shape[0]
    first, last = state is None, len(keys) == 2
    if last:
        out = jax.ShapeDtypeStruct((4, 2 * PACK, n // 4), BF16)
    else:
        rows = jax.ShapeDtypeStruct((8, n), F32)
        out = (jax.ShapeDtypeStruct((2 * ROWS, n), F32), rows, rows)
    return pl.pallas_call(
        functools.partial(attend_kernel, first, last),
        out_shape=out,
        cost_estimate=cost(
            4 * n * KEYS * HEAD_DIM * HEADS_HERE, 4 * n * 768 + 4 * KEYS * 768, n * KEYS * HEADS_HERE
        ),
        name="attend",
    )(queries, values, *(() if first else state), *keys)


def merge(parts_of):
    blocks = [p(ROWS, PACK).astype(F32) for p in parts_of]
    outs, lses = [], []
    for h in range(HALF):
        parts = [
            b[h : h + 1] + b[HALF + h : HALF + h + 1] + b[2 * HALF + h : 2 * HALF + h + 1] for b in blocks
        ]
        top = functools.reduce(jnp.maximum, parts)
        weights = [jnp.exp(p - top) for p in parts]
        total = sum(weights)
        inverse = 1.0 / total
        acc = 0.0
        for p, w in zip(parts_of, weights):
            acc = acc + p(h * VEC, (h + 1) * VEC).astype(F32) * (w * inverse)
        outs.append(acc)
        lses.append(top + jnp.log(total))
    return outs, lses


def merge_second_kernel(p_ref, o_ref):
    for base in (0, PACK):
        outs, lses = merge([lambda a, b, k=k: p_ref[k, base + a : base + b, :] for k in range(4)])
        packed = pack_lse(lses, 128)
        for k in range(4):
            for h in range(HALF):
                o_ref[k, base + h * VEC : base + (h + 1) * VEC, :] = outs[h].astype(BF16)
            o_ref[k, base + ROWS : base + PACK, :] = packed


def merge_second(parts):
    return pl.pallas_call(
        merge_second_kernel,
        out_shape=jax.ShapeDtypeStruct((4, 2 * PACK, 128), BF16),
        cost_estimate=cost(8 * PACK * 128 * 2, 16 * PACK * 128 * 2),
        name="merge_second",
    )(parts)


def merge_last_kernel(p_ref, o_ref):
    outs = []
    for base in (0, PACK):
        outs += merge([lambda a, b, k=k: p_ref[k, base + a : base + b, :] for k in range(4)])[0]
    o_ref[...] = sum(outs[1:], outs[0])


def merge_last(parts):
    return pl.pallas_call(
        merge_last_kernel,
        out_shape=jax.ShapeDtypeStruct((VEC, 128), F32),
        cost_estimate=cost(8 * PACK * 128 * 2, 10 * PACK * 128),
        name="merge_last",
    )(parts)


def decode_kernel(refresh_ref, me_ref, level_ref, v_ref, base_ref, up_ref, down_ref, w_ref, b_ref, o_ref):
    level, me = level_ref[0], me_ref[0]
    row = lax.broadcasted_iota(jnp.int32, (512, 128), 0)
    col = lax.broadcasted_iota(jnp.int32, (512, 128), 1)
    lane = row % 128
    target = (row // 256) * 64 + ((lane // 32) * 8 + lane % 8) * 2 + (row // 128) % 2

    def attention_rows(near, kinds):
        slot, on = 0, 0
        for s in range(SLOTS):
            hit = refresh_ref[s] == me + near
            slot = jnp.where(hit, s, slot)
            on = jnp.where(hit, 1, on)
        choose = (((lane // 8) % 4 == slot) & (target == col)).astype(F32).astype(BF16)
        count = LAT_CH * len(kinds)
        stacked = []
        for ys in range(4):
            for pair in range(2):
                pieces = []
                for xs in (pair * 2, pair * 2 + 1):
                    for b in range(2):
                        parts = [v_ref[ys * 4 + xs, pl.ds(kind * 2 + b, LAT_CH, 4), :] for kind in kinds]
                        pieces.append(jnp.concatenate(parts, axis=0))
                stacked.append(jnp.concatenate(pieces, axis=1))
        high, low = split(jnp.concatenate(stacked, axis=0))
        field = jnp.dot(high, choose, preferred_element_type=F32) + jnp.dot(
            low, choose, preferred_element_type=F32
        )
        field = jnp.concatenate([field[i * count : (i + 1) * count] for i in range(8)], axis=1)
        return jnp.where(on > 0, field, 0.0)

    own = base_ref[...] - level * attention_rows(0, (0, 1))
    up = up_ref[...] - level * attention_rows(-1, (1,))
    down = down_ref[...] - level * attention_rows(1, (0,))
    latent = jnp.concatenate([up, own, down], axis=0) / 0.3611 + 0.1159
    line = lax.broadcasted_iota(jnp.int32, latent.shape, 0)
    column = lax.broadcasted_iota(jnp.int32, latent.shape, 1)
    inside = ((line >= 16) | (me > 0)) & ((line < 48) | (me < PATCHES - 1))
    latent = jnp.where(inside, latent, 0.0)
    before = jnp.where(column == 0, 0.0, pltpu.roll(latent, 1, 1)).astype(BF16)
    after = jnp.where(column == COLS - 1, 0.0, pltpu.roll(latent, COLS - 1, 1)).astype(BF16)
    middle = latent.astype(BF16)

    channels = w_ref.shape[3]
    line = lax.broadcasted_iota(jnp.int32, (16, channels), 0)
    bias = jnp.broadcast_to(b_ref[...], (16, channels))
    high = bias.astype(BF16).astype(F32)
    mid = (bias - high).astype(BF16).astype(F32)
    bias = jnp.where(line == 0, high, jnp.where(line == 1, mid, jnp.where(line == 2, bias - high - mid, 0.0)))
    weight = [w_ref[u, v] for v in range(3) for u in range(3)] + [bias.astype(BF16)]
    weight = jnp.concatenate(weight, axis=0)
    ones = jnp.ones((16, COLS), BF16)
    for r in range(2):
        stencil = [s[r * 16 : r * 16 + 48] for s in (before, middle, after)] + [ones]
        out = lax.dot_general(
            weight, jnp.concatenate(stencil, axis=0), (((0,), (0,)), ((), ())), preferred_element_type=F32
        )
        o_ref[r] = out.astype(BF16)


def decode(refresh, me, level, gathered, base, up, down, weight, bias):
    return pl.pallas_call(
        decode_kernel,
        out_shape=jax.ShapeDtypeStruct((2, weight.shape[3], COLS), BF16),
        in_specs=[SMEM] * 3 + [VMEM] * 6,
        out_specs=VMEM,
        cost_estimate=cost(4 * 128 * 160 * 1024, 2 << 20),
        name="decode",
    )(refresh, me, level, gathered, base, up, down, weight, bias)


def on_device(
    fresh_qkv,
    kv_cache,
    hidden,
    refresh,
    out_weight,
    final_weight,
    final_bias,
    gate_scale,
    noise_level,
    noisy_latent,
    velocity_cache,
    conv_weight,
    conv_bias,
):
    me = lax.axis_index(PATCH).astype(jnp.int32)
    here = me.reshape(1)
    together = lax.optimization_barrier

    with jax.named_scope("queries"):
        own = fresh_qkv[:, 0].reshape(PATCHES, CHUNK, -1)
        own, fresh_qkv = together((own, fresh_qkv))
        got = exchange(own, PATCH)

    with jax.named_scope("keys_values"):
        refreshed = jnp.any(refresh == me)
        keys = jnp.where(refreshed, fresh_qkv[:, 1], kv_cache[:, 0])
        value_rows = jnp.where(refreshed, fresh_qkv[:, 2], kv_cache[:, 1])
        keys_x, keys_y = mirror(keys, 0, 1), mirror(keys, 1, 0)

    with jax.named_scope("latent_base"):
        plain = lax.dot_general(
            final_weight, hidden, (((0,), (1,)), ((), ())), preferred_element_type=F32
        )
        plain = plain + final_bias[:, None]
        base, edge_first, edge_last = latent_base(
            refresh, here, noise_level, plain, noisy_latent, velocity_cache
        )
        up = lax.ppermute(edge_last, PATCH, [(p, p + 1) for p in range(PATCHES - 1)])
        down = lax.ppermute(edge_first, PATCH, [(p + 1, p) for p in range(PATCHES - 1)])

    with jax.named_scope("queries"):
        got, base, up, down, _ = together((got, base, up, down, keys))
        held = exchange(select(refresh, got), ("yl", "xl", "z"))

    with jax.named_scope("keys_values"):
        gated = final_weight.T.astype(F32) * gate_scale[None, :]
        high = lax.reduce_precision(gated, 8, 7)
        both = jnp.concatenate([high, gated - high], axis=0).astype(BF16)
        mixed = lax.dot_general(both, out_weight, (((1,), (1,)), ((), ())), preferred_element_type=F32)
        values = project_values(value_rows, mixed[:VEC] + mixed[VEC:])
        values_x, values_y, values_far = mirror(values, 0, 1), mirror(values, 1, 0), mirror(values, 1, 1)

    with jax.named_scope("attention"):
        held, values = together((held, values))
        queries = held.reshape(16 * SLOTS * CHUNK, HEADS_HERE * HEAD_DIM)
        state = attend(queries, values, None, (keys,))
        keys_x, keys_y, state = together((keys_x, keys_y, state))
        far_a, far_b = halves(keys_x, keys_y)
        far_a, far_b = mirror(far_a, 1, 0), mirror(far_b, 0, 1)
        state = attend(queries, values_x, state, (keys_x,))
        values_y, state = together((values_y, state))
        state = attend(queries, values_y, state, (keys_y,))
        values_far, far_a, far_b, state = together((values_far, far_a, far_b, state))
        state = attend(queries, values_far, state, (far_a, far_b))
        part = merge_second(exchange(state, ("yl", "xl")))
        term = merge_last(exchange(part, "z"))

    with jax.named_scope("velocity"):
        term = jnp.sum(lax.all_gather(term, HEAD), axis=0)
        gathered = exchange(spread_out(term, 16), ("yh", "yl", "xh", "xl"))

    with jax.named_scope("decode"):
        weight = conv_weight.transpose(1, 2, 3, 0)
        return decode(
            refresh, here, noise_level, gathered, base, up, down, weight, conv_bias.reshape(1, -1)
        )


def solution(mesh):
    wide = Mesh(mesh.devices.reshape(2, 2, 2, 2, 4, 2, 2), PATCH + HEAD)
    return jax.shard_map(
        on_device,
        mesh=wide,
        in_specs=(
            P(PATCH, None, HEAD),
            P(PATCH, None, HEAD),
            P(PATCH, None),
            P(),
            P(HEAD, None),
            P(),
            P(),
            P(),
            P(),
            P(PATCH, None, None),
            P(PATCH, None, None),
            P(HEAD, None, None, None),
            P(HEAD),
        ),
        out_specs=P(PATCH, HEAD, None),
        check_vma=False,
    )
```

```python
import functools
import math

import jax
import jax.numpy as jnp
from jax import lax
from jax.experimental import pallas as pl
from jax.experimental.pallas import tpu as pltpu
from jax.sharding import Mesh
from jax.sharding import PartitionSpec as P

HEAD_DIM = 128
LAT_CH = 16
PATCHES = 64
SLOTS = 4
HEADS_HERE = 6
VEC = 64
KEYS = 512
COLS = 1024
CHUNK = 8
F32 = jnp.float32
BF16 = jnp.bfloat16
PATCH = ("yh", "yl", "xh", "xl", "z")
HEAD = ("w", "c")


def mirror(value, flip_y, flip_x):
    pairs = []
    for p in range(PATCHES):
        y, x, z = p // 16, (p // 4) % 4, p % 4
        pairs.append((p, (3 - y if flip_y else y) * 16 + (3 - x if flip_x else x) * 4 + z))
    return lax.ppermute(value, PATCH, pairs)


def spread_out(value, count):
    return jnp.broadcast_to(value[None], (count,) + value.shape)


def exchange(value, axis):
    return lax.all_to_all(value, axis, 0, 0)


def cost(flops, moved_bytes, exps=0):
    return pl.CostEstimate(flops=flops, bytes_accessed=moved_bytes, transcendentals=exps)


SMEM = pl.BlockSpec(memory_space=pltpu.SMEM)
VMEM = pl.BlockSpec(memory_space=pltpu.VMEM)


def split(value):
    high = value.astype(BF16)
    return high, (value - high.astype(F32)).astype(BF16)


def select_kernel(refresh_ref, got_ref, o_ref):
    for slot in range(SLOTS):
        rows = got_ref[refresh_ref[slot]]
        for k in range(o_ref.shape[0]):
            o_ref[k, slot * CHUNK : (slot + 1) * CHUNK, :] = rows


def select(refresh, got):
    width = got.shape[2]
    return pl.pallas_call(
        select_kernel,
        in_specs=[SMEM, VMEM],
        out_shape=jax.ShapeDtypeStruct((16, SLOTS * CHUNK, width), BF16),
        cost_estimate=cost(0, 17 * SLOTS * CHUNK * width * 2),
        name="select",
    )(refresh, got)


def values_kernel(v_ref, w_ref, o_ref):
    for h in range(HEADS_HERE):
        cols = slice(h * HEAD_DIM, (h + 1) * HEAD_DIM)
        left = jnp.concatenate(split(w_ref[:, cols]), axis=0)
        both = lax.dot_general(
            left, v_ref[:, cols], (((1,), (1,)), ((), ())), preferred_element_type=F32
        )
        o_ref[h * VEC : (h + 1) * VEC, :] = (both[:VEC] + both[VEC:]).astype(BF16)


def project_values(value_rows, mixed):
    return pl.pallas_call(
        values_kernel,
        out_shape=jax.ShapeDtypeStruct((HEADS_HERE * VEC, KEYS), BF16),
        cost_estimate=cost(4 * KEYS * VEC * HEAD_DIM * HEADS_HERE, 4 * KEYS * 768),
        name="values",
    )(value_rows, mixed)


def halves_kernel(x_ref, y_ref, a_ref, b_ref):
    a_ref[...] = x_ref[...]
    b_ref[...] = y_ref[...]


def halves(keys_x, keys_y):
    block = (KEYS // 2, keys_x.shape[1])
    whole = pl.BlockSpec(block, lambda i: (0, 0))
    return pl.pallas_call(
        halves_kernel,
        grid=(1,),
        in_specs=[whole, pl.BlockSpec(block, lambda i: (1, 0))],
        out_specs=(whole, whole),
        out_shape=(jax.ShapeDtypeStruct(block, BF16),) * 2,
        cost_estimate=cost(0, 2 * KEYS * keys_x.shape[1] * 2),
        name="halves",
    )(keys_x, keys_y)


def base_kernel(refresh_ref, me_ref, level_ref, plain_ref, noisy_ref, cache_ref, o_ref, *rest):
    first_ref, last_ref, block_ref = rest
    row = lax.broadcasted_iota(jnp.int32, (256, 256), 0)
    col = lax.broadcasted_iota(jnp.int32, (256, 256), 1)
    choose = ((row % 128) * 2 + row // 128 == col).astype(F32).astype(BF16)
    stacked = []
    for i in range(4):
        block_ref[i] = plain_ref[:, i * 128 : (i + 1) * 128]
        pieces = []
        for b in range(2):
            parts = [block_ref[i, pl.ds(a * 2 + b, LAT_CH, 4), :] for a in range(2)]
            pieces.append(jnp.concatenate(parts, axis=0))
        stacked.append(jnp.concatenate(pieces, axis=1))
    left = jnp.concatenate(stacked, axis=0)
    high, rest = left.astype(BF16), left - left.astype(BF16).astype(F32)
    mid, low = split(rest)
    field = sum(jnp.dot(part, choose, preferred_element_type=F32) for part in (high, mid, low))
    field = jnp.concatenate([field[i * 32 : (i + 1) * 32] for i in range(4)], axis=1)
    fresh = False
    for slot in range(SLOTS):
        fresh = fresh | (refresh_ref[slot] == me_ref[0])
    level = level_ref[0]
    for a in range(2):
        rows = slice(a * LAT_CH, (a + 1) * LAT_CH)
        velocity = jnp.where(fresh, field[rows], cache_ref[a].astype(F32))
        latent = noisy_ref[a].astype(F32) - level * velocity
        o_ref[rows, :] = latent
        (first_ref, last_ref)[a][...] = latent


def latent_base(refresh, me, level, plain, noisy, cache):
    edge = jax.ShapeDtypeStruct((LAT_CH, COLS), F32)
    return pl.pallas_call(
        base_kernel,
        in_specs=[SMEM] * 3 + [VMEM] * 3,
        out_shape=(jax.ShapeDtypeStruct((2 * LAT_CH, COLS), F32), edge, edge),
        scratch_shapes=[pltpu.VMEM((4, VEC, 128), F32)],
        cost_estimate=cost(6 * 128 * 256 * 256, 1 << 19),
        name="latent_base",
    )(refresh, me, level, plain, noisy, cache)


def lse_rows(lses, width):
    row = lax.broadcasted_iota(jnp.int32, (128, width), 0)
    block = jnp.zeros((128, width), F32)
    for h, lse in enumerate(lses):
        high = lse.astype(BF16).astype(F32)
        mid = (lse - high).astype(BF16).astype(F32)
        for part, value in enumerate((high, mid, lse - high - mid)):
            block = jnp.where(row == part * HEADS_HERE + h, jnp.broadcast_to(value, block.shape), block)
    return block


def attend_kernel(first, last, *refs):
    q_ref, v_ref, state_in, outs = refs[0], refs[1], None, refs[2:]
    if not first:
        state_in, outs = outs[:3], outs[3:]
    k_refs, outs = outs[: 2 if last else 1], outs[2 if last else 1 :]
    scale = math.log2(math.e) / math.sqrt(HEAD_DIM)

    def scores(head):
        cols = slice(head * HEAD_DIM, (head + 1) * HEAD_DIM)
        keys = [k[:, cols] for k in k_refs]
        keys = keys[0] if len(keys) == 1 else jnp.concatenate(keys, axis=0)
        return lax.dot_general(
            keys, q_ref[:, cols], (((1,), (1,)), ((), ())), preferred_element_type=F32
        )

    def store(place, block):
        flat = jnp.transpose(block).astype(BF16)
        outs[0][:, :, place * 128 : (place + 1) * 128] = flat.reshape(outs[0].shape[:2] + (128,))

    dots, lses, pair = scores(0), [], []
    dots_width = dots.shape[1]
    for head in range(HEADS_HERE):
        following = scores(head + 1) if head + 1 < HEADS_HERE else None
        rows = slice(head * VEC, (head + 1) * VEC)
        top = jnp.max(dots, axis=0, keepdims=True)
        if not first:
            old_top = state_in[1][head : head + 1, :]
            top = jnp.maximum(top, old_top)
        exps = jnp.exp2((dots - top) * scale)
        total = jnp.sum(exps, axis=0, keepdims=True)
        acc = jnp.dot(v_ref[rows, :], exps.astype(BF16), preferred_element_type=F32)
        if not first:
            shrink = jnp.exp2((old_top - top) * scale)
            total = total + state_in[2][head : head + 1, :] * shrink
            acc = acc + state_in[0][rows, :] * shrink
        if not last:
            outs[0][rows, :] = acc
            outs[1][head : head + 1, :] = top
            outs[2][head : head + 1, :] = total
        else:
            pair.append(acc * (1.0 / total))
            lses.append(top * (1.0 / math.sqrt(HEAD_DIM)) + jnp.log(total))
            if head % 2:
                store(head // 2, jnp.concatenate(pair, axis=0))
                pair = []
        dots = following
    if last:
        store(HEADS_HERE // 2, lse_rows(lses, dots_width))


def attend(queries, values, state, keys):
    n = queries.shape[0]
    first, last = state is None, len(keys) == 2
    if last:
        out = jax.ShapeDtypeStruct((16, n // 16, 512), BF16)
    else:
        rows = jax.ShapeDtypeStruct((8, n), F32)
        out = (jax.ShapeDtypeStruct((HEADS_HERE * VEC, n), F32), rows, rows)
    return pl.pallas_call(
        functools.partial(attend_kernel, first, last),
        out_shape=out,
        cost_estimate=cost(
            4 * n * KEYS * HEAD_DIM * HEADS_HERE, 4 * n * 768 + 4 * KEYS * 768, n * KEYS * HEADS_HERE
        ),
        name="attend",
    )(queries, values, *(() if first else state), *keys)


def merge_kernel(p_ref, o_ref):
    parts, rows = p_ref.shape[:2]
    width = HEADS_HERE * VEC
    lse = p_ref[:, :, width:].astype(F32).reshape(parts * rows, 128)
    lse = lse + pltpu.roll(lse, 128 - HEADS_HERE, 1) + pltpu.roll(lse, 128 - 2 * HEADS_HERE, 1)
    lse = lse.reshape(parts, rows, 128)
    weights = jnp.exp(lse - jnp.max(lse, axis=0, keepdims=True))
    weights = weights * (1.0 / jnp.sum(weights, axis=0, keepdims=True))
    lane = lax.broadcasted_iota(jnp.int32, (128, width), 0)
    col = lax.broadcasted_iota(jnp.int32, (128, width), 1)
    wide = (col // VEC == lane).astype(F32).astype(BF16)
    high, low = split(weights.reshape(parts * rows, 128))
    weights = jnp.dot(high, wide, preferred_element_type=F32) + jnp.dot(low, wide, preferred_element_type=F32)
    weights = weights.reshape(parts, rows, width)
    acc = jnp.sum(p_ref[:, :, :width].astype(F32) * weights, axis=0)
    acc = acc[:, :128] + acc[:, 128:256] + acc[:, 256:]
    acc = acc + pltpu.roll(acc, VEC, 1)
    even = lax.broadcasted_iota(jnp.int32, (CHUNK, 128), 1) < VEC
    for pair in range(SLOTS // 2):
        first = acc[pair * 2 * CHUNK : (pair * 2 + 1) * CHUNK]
        second = acc[(pair * 2 + 1) * CHUNK : (pair * 2 + 2) * CHUNK]
        o_ref[pair * CHUNK : (pair + 1) * CHUNK, :] = jnp.where(even, first, second)


def merge(parts):
    return pl.pallas_call(
        merge_kernel,
        out_shape=jax.ShapeDtypeStruct((SLOTS // 2 * CHUNK, 128), F32),
        cost_estimate=cost(1 << 25, parts.size * 2),
        name="merge",
    )(parts)


def decode_kernel(refresh_ref, me_ref, level_ref, v_ref, base_ref, up_ref, down_ref, w_ref, b_ref, o_ref, block_ref):
    level, me = level_ref[0], me_ref[0]
    row = lax.broadcasted_iota(jnp.int32, (256, 256), 0)
    col = lax.broadcasted_iota(jnp.int32, (256, 256), 1)
    choose = ((row % 128) * 2 + row // 128 == col).astype(F32).astype(BF16)

    def attention_rows(which, near, kinds):
        slot, on = 0, 0
        for s in range(SLOTS):
            hit = refresh_ref[s] == me + near
            slot = jnp.where(hit, s, slot)
            on = jnp.where(hit, 1, on)
        tokens = v_ref[:, pl.ds(pl.multiple_of((slot >> 1) * CHUNK, CHUNK), CHUNK), :].reshape(KEYS, 128)
        tokens = jnp.transpose(tokens)
        tokens = jnp.where((slot & 1) == 0, tokens[:VEC], tokens[VEC:])
        stacked = []
        for i in range(4):
            block_ref[which, i] = tokens[:, i * 128 : (i + 1) * 128]
            pieces = []
            for b in range(2):
                parts = [block_ref[which, i, pl.ds(kind * 2 + b, LAT_CH, 4), :] for kind in kinds]
                pieces.append(jnp.concatenate(parts, axis=0))
            stacked.append(jnp.concatenate(pieces, axis=1))
        high, low = split(jnp.concatenate(stacked, axis=0))
        field = jnp.dot(high, choose, preferred_element_type=F32) + jnp.dot(
            low, choose, preferred_element_type=F32
        )
        count = LAT_CH * len(kinds)
        field = jnp.concatenate([field[i * count : (i + 1) * count] for i in range(4)], axis=1)
        return jnp.where(on > 0, field, 0.0)

    own = base_ref[...] - level * attention_rows(0, 0, (0, 1))
    up = up_ref[...] - level * attention_rows(1, -1, (1,))
    down = down_ref[...] - level * attention_rows(2, 1, (0,))
    latent = jnp.concatenate([up, own, down], axis=0) / 0.3611 + 0.1159
    line = lax.broadcasted_iota(jnp.int32, latent.shape, 0)
    column = lax.broadcasted_iota(jnp.int32, latent.shape, 1)
    inside = ((line >= 16) | (me > 0)) & ((line < 48) | (me < PATCHES - 1))
    latent = jnp.where(inside, latent, 0.0)
    before = jnp.where(column == 0, 0.0, pltpu.roll(latent, 1, 1)).astype(BF16)
    after = jnp.where(column == COLS - 1, 0.0, pltpu.roll(latent, COLS - 1, 1)).astype(BF16)
    middle = latent.astype(BF16)

    channels = w_ref.shape[3]
    line = lax.broadcasted_iota(jnp.int32, (16, channels), 0)
    bias = jnp.broadcast_to(b_ref[...], (16, channels))
    high = bias.astype(BF16).astype(F32)
    mid = (bias - high).astype(BF16).astype(F32)
    bias = jnp.where(line == 0, high, jnp.where(line == 1, mid, jnp.where(line == 2, bias - high - mid, 0.0)))
    weight = [w_ref[u, v] for v in range(3) for u in range(3)] + [bias.astype(BF16)]
    weight = jnp.concatenate(weight, axis=0)
    ones = jnp.ones((16, COLS), BF16)
    for r in range(2):
        stencil = [s[r * 16 : r * 16 + 48] for s in (before, middle, after)] + [ones]
        out = lax.dot_general(
            weight, jnp.concatenate(stencil, axis=0), (((0,), (0,)), ((), ())), preferred_element_type=F32
        )
        o_ref[r] = out.astype(BF16)


def decode(refresh, me, level, gathered, base, up, down, weight, bias):
    return pl.pallas_call(
        decode_kernel,
        out_shape=jax.ShapeDtypeStruct((2, weight.shape[3], COLS), BF16),
        in_specs=[SMEM] * 3 + [VMEM] * 6,
        out_specs=VMEM,
        scratch_shapes=[pltpu.VMEM((3, 4, VEC, 128), F32)],
        cost_estimate=cost(4 * 128 * 160 * 1024, 2 << 20),
        name="decode",
    )(refresh, me, level, gathered, base, up, down, weight, bias)


def on_device(
    fresh_qkv,
    kv_cache,
    hidden,
    refresh,
    out_weight,
    final_weight,
    final_bias,
    gate_scale,
    noise_level,
    noisy_latent,
    velocity_cache,
    conv_weight,
    conv_bias,
):
    me = lax.axis_index(PATCH).astype(jnp.int32)
    here = me.reshape(1)
    together = lax.optimization_barrier

    with jax.named_scope("queries"):
        own = fresh_qkv[:, 0].reshape(PATCHES, CHUNK, -1)
        own, fresh_qkv = together((own, fresh_qkv))
        got = exchange(own, PATCH)

    with jax.named_scope("keys_values"):
        refreshed = jnp.any(refresh == me)
        keys = jnp.where(refreshed, fresh_qkv[:, 1], kv_cache[:, 0])
        value_rows = jnp.where(refreshed, fresh_qkv[:, 2], kv_cache[:, 1])
        keys_x, keys_y = mirror(keys, 0, 1), mirror(keys, 1, 0)

    with jax.named_scope("latent_base"):
        plain = lax.dot_general(
            final_weight, hidden, (((0,), (1,)), ((), ())), preferred_element_type=F32
        )
        plain = plain + final_bias[:, None]
        base, edge_first, edge_last = latent_base(
            refresh, here, noise_level, plain, noisy_latent, velocity_cache
        )
        up = lax.ppermute(edge_last, PATCH, [(p, p + 1) for p in range(PATCHES - 1)])
        down = lax.ppermute(edge_first, PATCH, [(p + 1, p) for p in range(PATCHES - 1)])

    with jax.named_scope("queries"):
        got, base, up, down, _ = together((got, base, up, down, keys))
        held = exchange(select(refresh, got), ("yl", "xl", "z"))

    with jax.named_scope("keys_values"):
        gated = final_weight.T.astype(F32) * gate_scale[None, :]
        high = lax.reduce_precision(gated, 8, 7)
        both = jnp.concatenate([high, gated - high], axis=0).astype(BF16)
        mixed = lax.dot_general(both, out_weight, (((1,), (1,)), ((), ())), preferred_element_type=F32)
        values = project_values(value_rows, mixed[:VEC] + mixed[VEC:])
        values_x, values_y, values_far = mirror(values, 0, 1), mirror(values, 1, 0), mirror(values, 1, 1)

    with jax.named_scope("attention"):
        held, values = together((held, values))
        queries = held.reshape(16 * SLOTS * CHUNK, HEADS_HERE * HEAD_DIM)
        state = attend(queries, values, None, (keys,))
        keys_x, keys_y, state = together((keys_x, keys_y, state))
        far_a, far_b = halves(keys_x, keys_y)
        far_a, far_b = mirror(far_a, 1, 0), mirror(far_b, 0, 1)
        state = attend(queries, values_x, state, (keys_x,))
        values_y, state = together((values_y, state))
        state = attend(queries, values_y, state, (keys_y,))
        values_far, far_a, far_b, state = together((values_far, far_a, far_b, state))
        state = attend(queries, values_far, state, (far_a, far_b))
        term = merge(exchange(state, ("yl", "xl", "z")))

    with jax.named_scope("velocity"):
        term = jnp.sum(lax.all_gather(term, HEAD), axis=0)
        gathered = exchange(spread_out(term, PATCHES), PATCH)

    with jax.named_scope("decode"):
        weight = conv_weight.transpose(1, 2, 3, 0)
        return decode(
            refresh, here, noise_level, gathered, base, up, down, weight, conv_bias.reshape(1, -1)
        )


def solution(mesh):
    wide = Mesh(mesh.devices.reshape(2, 2, 2, 2, 4, 2, 2), PATCH + HEAD)
    return jax.shard_map(
        on_device,
        mesh=wide,
        in_specs=(
            P(PATCH, None, HEAD),
            P(PATCH, None, HEAD),
            P(PATCH, None),
            P(),
            P(HEAD, None),
            P(),
            P(),
            P(),
            P(),
            P(PATCH, None, None),
            P(PATCH, None, None),
            P(HEAD, None, None, None),
            P(HEAD),
        ),
        out_specs=P(PATCH, HEAD, None),
        check_vma=False,
    )
```

```python
import functools
import math

import jax
import jax.numpy as jnp
from jax import lax
from jax.experimental import pallas as pl
from jax.experimental.pallas import tpu as pltpu
from jax.sharding import Mesh
from jax.sharding import PartitionSpec as P

HEAD_DIM = 128
LAT_CH = 16
PATCHES = 64
SLOTS = 4
HEADS_HERE = 6
HALF = 3
VEC = 64
ROWS = HALF * VEC
PACK = ROWS + 16
KEYS = 512
COLS = 1024
CHUNK = 8
F32 = jnp.float32
BF16 = jnp.bfloat16
PATCH = ("yh", "yl", "xh", "xl", "z")
HEAD = ("w", "c")


def mirror(value, flip_y, flip_x):
    pairs = []
    for p in range(PATCHES):
        y, x, z = p // 16, (p // 4) % 4, p % 4
        pairs.append((p, (3 - y if flip_y else y) * 16 + (3 - x if flip_x else x) * 4 + z))
    return lax.ppermute(value, PATCH, pairs)


def spread_out(value, count):
    return jnp.broadcast_to(value[None], (count,) + value.shape)


def exchange(value, axis):
    return lax.all_to_all(value, axis, 0, 0)


def cost(flops, moved_bytes, exps=0):
    return pl.CostEstimate(flops=flops, bytes_accessed=moved_bytes, transcendentals=exps)


SMEM = pl.BlockSpec(memory_space=pltpu.SMEM)
VMEM = pl.BlockSpec(memory_space=pltpu.VMEM)


def split(value):
    high = value.astype(BF16)
    return high, (value - high.astype(F32)).astype(BF16)


def select_kernel(refresh_ref, got_ref, o_ref):
    for slot in range(SLOTS):
        rows = got_ref[refresh_ref[slot]]
        for k in range(o_ref.shape[0]):
            o_ref[k, slot * CHUNK : (slot + 1) * CHUNK, :] = rows


def select(refresh, got):
    width = got.shape[2]
    return pl.pallas_call(
        select_kernel,
        in_specs=[SMEM, VMEM],
        out_shape=jax.ShapeDtypeStruct((16, SLOTS * CHUNK, width), BF16),
        cost_estimate=cost(0, 17 * SLOTS * CHUNK * width * 2),
        name="select",
    )(refresh, got)


def values_kernel(v_ref, w_ref, o_ref):
    for h in range(HEADS_HERE):
        cols = slice(h * HEAD_DIM, (h + 1) * HEAD_DIM)
        left = jnp.concatenate(split(w_ref[:, cols]), axis=0)
        both = lax.dot_general(
            left, v_ref[:, cols], (((1,), (1,)), ((), ())), preferred_element_type=F32
        )
        o_ref[h * VEC : (h + 1) * VEC, :] = (both[:VEC] + both[VEC:]).astype(BF16)


def project_values(value_rows, mixed):
    return pl.pallas_call(
        values_kernel,
        out_shape=jax.ShapeDtypeStruct((HEADS_HERE * VEC, KEYS), BF16),
        cost_estimate=cost(4 * KEYS * VEC * HEAD_DIM * HEADS_HERE, 4 * KEYS * 768),
        name="values",
    )(value_rows, mixed)


def halves_kernel(x_ref, y_ref, a_ref, b_ref):
    a_ref[...] = x_ref[...]
    b_ref[...] = y_ref[...]


def halves(keys_x, keys_y):
    block = (KEYS // 2, keys_x.shape[1])
    whole = pl.BlockSpec(block, lambda i: (0, 0))
    return pl.pallas_call(
        halves_kernel,
        grid=(1,),
        in_specs=[whole, pl.BlockSpec(block, lambda i: (1, 0))],
        out_specs=(whole, whole),
        out_shape=(jax.ShapeDtypeStruct(block, BF16),) * 2,
        cost_estimate=cost(0, 2 * KEYS * keys_x.shape[1] * 2),
        name="halves",
    )(keys_x, keys_y)


def base_kernel(refresh_ref, me_ref, level_ref, plain_ref, noisy_ref, cache_ref, o_ref, *rest):
    first_ref, last_ref, block_ref = rest
    row = lax.broadcasted_iota(jnp.int32, (256, 256), 0)
    col = lax.broadcasted_iota(jnp.int32, (256, 256), 1)
    choose = ((row % 128) * 2 + row // 128 == col).astype(F32).astype(BF16)
    stacked = []
    for i in range(4):
        block_ref[i] = plain_ref[:, i * 128 : (i + 1) * 128]
        pieces = []
        for b in range(2):
            parts = [block_ref[i, pl.ds(a * 2 + b, LAT_CH, 4), :] for a in range(2)]
            pieces.append(jnp.concatenate(parts, axis=0))
        stacked.append(jnp.concatenate(pieces, axis=1))
    left = jnp.concatenate(stacked, axis=0)
    high, rest = left.astype(BF16), left - left.astype(BF16).astype(F32)
    mid, low = split(rest)
    field = sum(jnp.dot(part, choose, preferred_element_type=F32) for part in (high, mid, low))
    field = jnp.concatenate([field[i * 32 : (i + 1) * 32] for i in range(4)], axis=1)
    fresh = False
    for slot in range(SLOTS):
        fresh = fresh | (refresh_ref[slot] == me_ref[0])
    level = level_ref[0]
    for a in range(2):
        rows = slice(a * LAT_CH, (a + 1) * LAT_CH)
        velocity = jnp.where(fresh, field[rows], cache_ref[a].astype(F32))
        latent = noisy_ref[a].astype(F32) - level * velocity
        o_ref[rows, :] = latent
        (first_ref, last_ref)[a][...] = latent


def latent_base(refresh, me, level, plain, noisy, cache):
    edge = jax.ShapeDtypeStruct((LAT_CH, COLS), F32)
    return pl.pallas_call(
        base_kernel,
        in_specs=[SMEM] * 3 + [VMEM] * 3,
        out_shape=(jax.ShapeDtypeStruct((2 * LAT_CH, COLS), F32), edge, edge),
        scratch_shapes=[pltpu.VMEM((4, VEC, 128), F32)],
        cost_estimate=cost(6 * 128 * 256 * 256, 1 << 19),
        name="latent_base",
    )(refresh, me, level, plain, noisy, cache)


def pack_lse(entries, width):
    row = lax.broadcasted_iota(jnp.int32, (16, width), 0)
    block = jnp.zeros((16, width), F32)
    for h, lse in enumerate(entries):
        high = lse.astype(BF16).astype(F32)
        rest = lse - high
        mid = rest.astype(BF16).astype(F32)
        low = rest - mid
        for part, value in enumerate((high, mid, low)):
            block = jnp.where(row == part * HALF + h, jnp.broadcast_to(value, block.shape), block)
    return block.astype(BF16)


def attend_kernel(first, last, *refs):
    q_ref, v_ref, state_in, outs = refs[0], refs[1], None, refs[2:]
    if not first:
        state_in, outs = outs[:3], outs[3:]
    k_refs, outs = outs[: 2 if last else 1], outs[2 if last else 1 :]
    scale = math.log2(math.e) / math.sqrt(HEAD_DIM)

    def scores(head):
        cols = slice(head * HEAD_DIM, (head + 1) * HEAD_DIM)
        keys = [k[:, cols] for k in k_refs]
        keys = keys[0] if len(keys) == 1 else jnp.concatenate(keys, axis=0)
        return lax.dot_general(
            keys, q_ref[:, cols], (((1,), (1,)), ((), ())), preferred_element_type=F32
        )

    dots, lses = scores(0), []
    for head in range(HEADS_HERE):
        half, h = divmod(head, HALF)
        following = scores(head + 1) if head + 1 < HEADS_HERE else None
        rows = slice(head * VEC, (head + 1) * VEC)
        top = jnp.max(dots, axis=0, keepdims=True)
        if not first:
            old_top = state_in[1][head : head + 1, :]
            top = jnp.maximum(top, old_top)
        exps = jnp.exp2((dots - top) * scale)
        total = jnp.sum(exps, axis=0, keepdims=True)
        acc = jnp.dot(v_ref[rows, :], exps.astype(BF16), preferred_element_type=F32)
        if not first:
            shrink = jnp.exp2((old_top - top) * scale)
            total = total + state_in[2][head : head + 1, :] * shrink
            acc = acc + state_in[0][rows, :] * shrink
        if not last:
            outs[0][rows, :] = acc
            outs[1][head : head + 1, :] = top
            outs[2][head : head + 1, :] = total
        else:
            out = (acc * (1.0 / total)).astype(BF16)
            row = half * PACK + h * VEC
            for k in range(4):
                outs[0][k, row : row + VEC, :] = out[:, k * 128 : (k + 1) * 128]
            lses.append(top * (1.0 / math.sqrt(HEAD_DIM)) + jnp.log(total))
            if h == HALF - 1:
                packed = pack_lse(lses, out.shape[1])
                for k in range(4):
                    outs[0][k, half * PACK + ROWS : (half + 1) * PACK, :] = packed[:, k * 128 : (k + 1) * 128]
                lses = []
        dots = following


def attend(queries, values, state, keys):
    n = queries.shape[0]
    first, last = state is None, len(keys) == 2
    if last:
        out = jax.ShapeDtypeStruct((4, 2 * PACK, n // 4), BF16)
    else:
        rows = jax.ShapeDtypeStruct((8, n), F32)
        out = (jax.ShapeDtypeStruct((2 * ROWS, n), F32), rows, rows)
    return pl.pallas_call(
        functools.partial(attend_kernel, first, last),
        out_shape=out,
        cost_estimate=cost(
            4 * n * KEYS * HEAD_DIM * HEADS_HERE, 4 * n * 768 + 4 * KEYS * 768, n * KEYS * HEADS_HERE
        ),
        name="attend",
    )(queries, values, *(() if first else state), *keys)


def merge(parts_of):
    blocks = [p(ROWS, PACK).astype(F32) for p in parts_of]
    outs, lses = [], []
    for h in range(HALF):
        parts = [
            b[h : h + 1] + b[HALF + h : HALF + h + 1] + b[2 * HALF + h : 2 * HALF + h + 1] for b in blocks
        ]
        top = functools.reduce(jnp.maximum, parts)
        weights = [jnp.exp(p - top) for p in parts]
        total = sum(weights)
        inverse = 1.0 / total
        acc = 0.0
        for p, w in zip(parts_of, weights):
            acc = acc + p(h * VEC, (h + 1) * VEC).astype(F32) * (w * inverse)
        outs.append(acc)
        lses.append(top + jnp.log(total))
    return outs, lses


def merge_second_kernel(p_ref, o_ref):
    for base in (0, PACK):
        outs, lses = merge([lambda a, b, k=k: p_ref[k, base + a : base + b, :] for k in range(4)])
        packed = pack_lse(lses, 128)
        for k in range(4):
            for h in range(HALF):
                o_ref[k, base + h * VEC : base + (h + 1) * VEC, :] = outs[h].astype(BF16)
            o_ref[k, base + ROWS : base + PACK, :] = packed


def merge_second(parts):
    return pl.pallas_call(
        merge_second_kernel,
        out_shape=jax.ShapeDtypeStruct((4, 2 * PACK, 128), BF16),
        cost_estimate=cost(8 * PACK * 128 * 2, 16 * PACK * 128 * 2),
        name="merge_second",
    )(parts)


def merge_last_kernel(p_ref, o_ref):
    outs = []
    for base in (0, PACK):
        outs += merge([lambda a, b, k=k: p_ref[k, base + a : base + b, :] for k in range(4)])[0]
    o_ref[...] = sum(outs[1:], outs[0])


def merge_last(parts):
    return pl.pallas_call(
        merge_last_kernel,
        out_shape=jax.ShapeDtypeStruct((VEC, 128), F32),
        cost_estimate=cost(8 * PACK * 128 * 2, 10 * PACK * 128),
        name="merge_last",
    )(parts)


def decode_kernel(refresh_ref, me_ref, level_ref, v_ref, base_ref, up_ref, down_ref, w_ref, b_ref, o_ref, all_ref):
    level, me = level_ref[0], me_ref[0]
    all_ref[...] = v_ref[...].astype(F32)
    row = lax.broadcasted_iota(jnp.int32, (512, 128), 0)
    col = lax.broadcasted_iota(jnp.int32, (512, 128), 1)
    lane = row % 128
    target = (row // 256) * 64 + ((lane // 32) * 8 + lane % 8) * 2 + (row // 128) % 2

    def attention_rows(near, kinds):
        slot, on = 0, 0
        for s in range(SLOTS):
            hit = refresh_ref[s] == me + near
            slot = jnp.where(hit, s, slot)
            on = jnp.where(hit, 1, on)
        choose = (((lane // 8) % 4 == slot) & (target == col)).astype(F32).astype(BF16)
        count = LAT_CH * len(kinds)
        stacked = []
        for ys in range(4):
            for pair in range(2):
                pieces = []
                for xs in (pair * 2, pair * 2 + 1):
                    for b in range(2):
                        parts = [all_ref[ys * 4 + xs, pl.ds(kind * 2 + b, LAT_CH, 4), :] for kind in kinds]
                        pieces.append(jnp.concatenate(parts, axis=0))
                stacked.append(jnp.concatenate(pieces, axis=1))
        left = jnp.concatenate(stacked, axis=0).astype(BF16)
        field = jnp.dot(left, choose, preferred_element_type=F32)
        field = jnp.concatenate([field[i * count : (i + 1) * count] for i in range(8)], axis=1)
        return jnp.where(on > 0, field, 0.0)

    own = base_ref[...] - level * attention_rows(0, (0, 1))
    up = up_ref[...] - level * attention_rows(-1, (1,))
    down = down_ref[...] - level * attention_rows(1, (0,))
    latent = jnp.concatenate([up, own, down], axis=0) / 0.3611 + 0.1159
    line = lax.broadcasted_iota(jnp.int32, latent.shape, 0)
    column = lax.broadcasted_iota(jnp.int32, latent.shape, 1)
    inside = ((line >= 16) | (me > 0)) & ((line < 48) | (me < PATCHES - 1))
    latent = jnp.where(inside, latent, 0.0)
    before = jnp.where(column == 0, 0.0, pltpu.roll(latent, 1, 1)).astype(BF16)
    after = jnp.where(column == COLS - 1, 0.0, pltpu.roll(latent, COLS - 1, 1)).astype(BF16)
    middle = latent.astype(BF16)

    channels = w_ref.shape[3]
    line = lax.broadcasted_iota(jnp.int32, (16, channels), 0)
    bias = jnp.broadcast_to(b_ref[...], (16, channels))
    high = bias.astype(BF16).astype(F32)
    mid = (bias - high).astype(BF16).astype(F32)
    bias = jnp.where(line == 0, high, jnp.where(line == 1, mid, jnp.where(line == 2, bias - high - mid, 0.0)))
    weight = [w_ref[u, v] for v in range(3) for u in range(3)] + [bias.astype(BF16)]
    weight = jnp.concatenate(weight, axis=0)
    ones = jnp.ones((16, COLS), BF16)
    for r in range(2):
        stencil = [s[r * 16 : r * 16 + 48] for s in (before, middle, after)] + [ones]
        out = lax.dot_general(
            weight, jnp.concatenate(stencil, axis=0), (((0,), (0,)), ((), ())), preferred_element_type=F32
        )
        o_ref[r] = out.astype(BF16)


def decode(refresh, me, level, gathered, base, up, down, weight, bias):
    return pl.pallas_call(
        decode_kernel,
        out_shape=jax.ShapeDtypeStruct((2, weight.shape[3], COLS), BF16),
        in_specs=[SMEM] * 3 + [VMEM] * 6,
        out_specs=VMEM,
        scratch_shapes=[pltpu.VMEM((16, VEC, 128), F32)],
        cost_estimate=cost(4 * 128 * 160 * 1024, 2 << 20),
        name="decode",
    )(refresh, me, level, gathered, base, up, down, weight, bias)


def on_device(
    fresh_qkv,
    kv_cache,
    hidden,
    refresh,
    out_weight,
    final_weight,
    final_bias,
    gate_scale,
    noise_level,
    noisy_latent,
    velocity_cache,
    conv_weight,
    conv_bias,
):
    me = lax.axis_index(PATCH).astype(jnp.int32)
    here = me.reshape(1)
    together = lax.optimization_barrier

    with jax.named_scope("queries"):
        own = fresh_qkv[:, 0].reshape(PATCHES, CHUNK, -1)
        own, fresh_qkv = together((own, fresh_qkv))
        got = exchange(own, PATCH)

    with jax.named_scope("keys_values"):
        refreshed = jnp.any(refresh == me)
        keys = jnp.where(refreshed, fresh_qkv[:, 1], kv_cache[:, 0])
        value_rows = jnp.where(refreshed, fresh_qkv[:, 2], kv_cache[:, 1])
        gated = final_weight.T.astype(F32) * gate_scale[None, :]
        high = lax.reduce_precision(gated, 8, 7)
        both = jnp.concatenate([high, gated - high], axis=0).astype(BF16)
        mixed = lax.dot_general(both, out_weight, (((1,), (1,)), ((), ())), preferred_element_type=F32)
        values = project_values(value_rows, mixed[:VEC] + mixed[VEC:])

    with jax.named_scope("queries"):
        got, keys, values = together((got, keys, values))
        held = exchange(select(refresh, got), ("yl", "xl", "z"))

    with jax.named_scope("keys_values"):
        keys_x, keys_y = mirror(keys, 0, 1), mirror(keys, 1, 0)
        values_x, values_y, values_far = mirror(values, 0, 1), mirror(values, 1, 0), mirror(values, 1, 1)

    with jax.named_scope("attention"):
        queries = held.reshape(16 * SLOTS * CHUNK, HEADS_HERE * HEAD_DIM)
        state = attend(queries, values, None, (keys,))
        keys_x, keys_y, state = together((keys_x, keys_y, state))
        far_a, far_b = halves(keys_x, keys_y)
        far_a, far_b = mirror(far_a, 1, 0), mirror(far_b, 0, 1)
        state = attend(queries, values_x, state, (keys_x,))
        values_y, state = together((values_y, state))
        state = attend(queries, values_y, state, (keys_y,))
        values_far, far_a, far_b, state = together((values_far, far_a, far_b, state))
        state = attend(queries, values_far, state, (far_a, far_b))
        part = merge_second(exchange(state, ("yl", "xl")))
        part, hidden = together((part, hidden))
        parts = exchange(part, "z")

    with jax.named_scope("latent_base"):
        plain = lax.dot_general(
            final_weight, hidden, (((0,), (1,)), ((), ())), preferred_element_type=F32
        )
        plain = plain + final_bias[:, None]
        base, edge_first, edge_last = latent_base(
            refresh, here, noise_level, plain, noisy_latent, velocity_cache
        )
        up = lax.ppermute(edge_last, PATCH, [(p, p + 1) for p in range(PATCHES - 1)])
        down = lax.ppermute(edge_first, PATCH, [(p + 1, p) for p in range(PATCHES - 1)])

    with jax.named_scope("velocity"):
        parts, up, down = together((parts, up, down))
        term = merge_last(parts)
        term = jnp.sum(lax.all_gather(term, HEAD), axis=0).astype(BF16)
        gathered = exchange(spread_out(term, 16), ("yh", "yl", "xh", "xl"))

    with jax.named_scope("decode"):
        weight = conv_weight.transpose(1, 2, 3, 0)
        return decode(
            refresh, here, noise_level, gathered, base, up, down, weight, conv_bias.reshape(1, -1)
        )


def solution(mesh):
    wide = Mesh(mesh.devices.reshape(2, 2, 2, 2, 4, 2, 2), PATCH + HEAD)
    return jax.shard_map(
        on_device,
        mesh=wide,
        in_specs=(
            P(PATCH, None, HEAD),
            P(PATCH, None, HEAD),
            P(PATCH, None),
            P(),
            P(HEAD, None),
            P(),
            P(),
            P(),
            P(),
            P(PATCH, None, None),
            P(PATCH, None, None),
            P(HEAD, None, None, None),
            P(HEAD),
        ),
        out_specs=P(PATCH, HEAD, None),
        check_vma=False,
    )
```

```python
import functools
import math

import jax
import jax.numpy as jnp
from jax import lax
from jax.experimental import pallas as pl
from jax.experimental.pallas import tpu as pltpu
from jax.sharding import Mesh
from jax.sharding import PartitionSpec as P

HEAD_DIM = 128
LAT_CH = 16
PATCHES = 64
SLOTS = 4
HEADS_HERE = 6
HALF = 3
VEC = 64
ROWS = HALF * VEC
PACK = ROWS + 16
KEYS = 512
COLS = 1024
CHUNK = 8
F32 = jnp.float32
BF16 = jnp.bfloat16
PATCH = ("yh", "yl", "xh", "xl", "z")
HEAD = ("w", "c")


def mirror(value, flip_y, flip_x):
    pairs = []
    for p in range(PATCHES):
        y, x, z = p // 16, (p // 4) % 4, p % 4
        pairs.append((p, (3 - y if flip_y else y) * 16 + (3 - x if flip_x else x) * 4 + z))
    return lax.ppermute(value, PATCH, pairs)


def spread_out(value, count):
    return jnp.broadcast_to(value[None], (count,) + value.shape)


def exchange(value, axis):
    return lax.all_to_all(value, axis, 0, 0)


def cost(flops, moved_bytes, exps=0):
    return pl.CostEstimate(flops=flops, bytes_accessed=moved_bytes, transcendentals=exps)


SMEM = pl.BlockSpec(memory_space=pltpu.SMEM)
VMEM = pl.BlockSpec(memory_space=pltpu.VMEM)


def split(value):
    high = value.astype(BF16)
    return high, (value - high.astype(F32)).astype(BF16)


def select_kernel(refresh_ref, got_ref, o_ref):
    for slot in range(SLOTS):
        rows = got_ref[refresh_ref[slot]]
        for k in range(o_ref.shape[0]):
            o_ref[k, slot * CHUNK : (slot + 1) * CHUNK, :] = rows


def select(refresh, got):
    width = got.shape[2]
    return pl.pallas_call(
        select_kernel,
        in_specs=[SMEM, VMEM],
        out_shape=jax.ShapeDtypeStruct((16, SLOTS * CHUNK, width), BF16),
        cost_estimate=cost(0, 17 * SLOTS * CHUNK * width * 2),
        name="select",
    )(refresh, got)


def values_kernel(v_ref, w_ref, o_ref):
    for h in range(HEADS_HERE):
        cols = slice(h * HEAD_DIM, (h + 1) * HEAD_DIM)
        left = jnp.concatenate(split(w_ref[:, cols]), axis=0)
        both = lax.dot_general(
            left, v_ref[:, cols], (((1,), (1,)), ((), ())), preferred_element_type=F32
        )
        o_ref[h * VEC : (h + 1) * VEC, :] = (both[:VEC] + both[VEC:]).astype(BF16)


def project_values(value_rows, mixed):
    return pl.pallas_call(
        values_kernel,
        out_shape=jax.ShapeDtypeStruct((HEADS_HERE * VEC, KEYS), BF16),
        cost_estimate=cost(4 * KEYS * VEC * HEAD_DIM * HEADS_HERE, 4 * KEYS * 768),
        name="values",
    )(value_rows, mixed)


def halves_kernel(x_ref, y_ref, a_ref, b_ref):
    a_ref[...] = x_ref[...]
    b_ref[...] = y_ref[...]


def halves(keys_x, keys_y):
    block = (KEYS // 2, keys_x.shape[1])
    whole = pl.BlockSpec(block, lambda i: (0, 0))
    return pl.pallas_call(
        halves_kernel,
        grid=(1,),
        in_specs=[whole, pl.BlockSpec(block, lambda i: (1, 0))],
        out_specs=(whole, whole),
        out_shape=(jax.ShapeDtypeStruct(block, BF16),) * 2,
        cost_estimate=cost(0, 2 * KEYS * keys_x.shape[1] * 2),
        name="halves",
    )(keys_x, keys_y)


def base_kernel(refresh_ref, me_ref, level_ref, plain_ref, noisy_ref, cache_ref, o_ref, *rest):
    first_ref, last_ref, block_ref = rest
    row = lax.broadcasted_iota(jnp.int32, (256, 256), 0)
    col = lax.broadcasted_iota(jnp.int32, (256, 256), 1)
    choose = ((row % 128) * 2 + row // 128 == col).astype(F32).astype(BF16)
    stacked = []
    for i in range(4):
        block_ref[i] = plain_ref[:, i * 128 : (i + 1) * 128]
        pieces = []
        for b in range(2):
            parts = [block_ref[i, pl.ds(a * 2 + b, LAT_CH, 4), :] for a in range(2)]
            pieces.append(jnp.concatenate(parts, axis=0))
        stacked.append(jnp.concatenate(pieces, axis=1))
    left = jnp.concatenate(stacked, axis=0)
    high, rest = left.astype(BF16), left - left.astype(BF16).astype(F32)
    mid, low = split(rest)
    field = sum(jnp.dot(part, choose, preferred_element_type=F32) for part in (high, mid, low))
    field = jnp.concatenate([field[i * 32 : (i + 1) * 32] for i in range(4)], axis=1)
    fresh = False
    for slot in range(SLOTS):
        fresh = fresh | (refresh_ref[slot] == me_ref[0])
    level = level_ref[0]
    for a in range(2):
        rows = slice(a * LAT_CH, (a + 1) * LAT_CH)
        velocity = jnp.where(fresh, field[rows], cache_ref[a].astype(F32))
        latent = noisy_ref[a].astype(F32) - level * velocity
        o_ref[rows, :] = latent
        (first_ref, last_ref)[a][...] = latent


def latent_base(refresh, me, level, plain, noisy, cache):
    edge = jax.ShapeDtypeStruct((LAT_CH, COLS), F32)
    return pl.pallas_call(
        base_kernel,
        in_specs=[SMEM] * 3 + [VMEM] * 3,
        out_shape=(jax.ShapeDtypeStruct((2 * LAT_CH, COLS), F32), edge, edge),
        scratch_shapes=[pltpu.VMEM((4, VEC, 128), F32)],
        cost_estimate=cost(6 * 128 * 256 * 256, 1 << 19),
        name="latent_base",
    )(refresh, me, level, plain, noisy, cache)


def pack_lse(entries, width):
    row = lax.broadcasted_iota(jnp.int32, (16, width), 0)
    block = jnp.zeros((16, width), F32)
    for h, lse in enumerate(entries):
        high = lse.astype(BF16).astype(F32)
        rest = lse - high
        mid = rest.astype(BF16).astype(F32)
        low = rest - mid
        for part, value in enumerate((high, mid, low)):
            block = jnp.where(row == part * HALF + h, jnp.broadcast_to(value, block.shape), block)
    return block.astype(BF16)


def attend_kernel(first, last, *refs):
    q_ref, v_ref, state_in, outs = refs[0], refs[1], None, refs[2:]
    if not first:
        state_in, outs = outs[:3], outs[3:]
    k_refs, outs = outs[: 2 if last else 1], outs[2 if last else 1 :]
    scale = math.log2(math.e) / math.sqrt(HEAD_DIM)

    def scores(head):
        cols = slice(head * HEAD_DIM, (head + 1) * HEAD_DIM)
        keys = [k[:, cols] for k in k_refs]
        keys = keys[0] if len(keys) == 1 else jnp.concatenate(keys, axis=0)
        return lax.dot_general(
            keys, q_ref[:, cols], (((1,), (1,)), ((), ())), preferred_element_type=F32
        )

    dots, lses = scores(0), []
    for head in range(HEADS_HERE):
        half, h = divmod(head, HALF)
        following = scores(head + 1) if head + 1 < HEADS_HERE else None
        rows = slice(head * VEC, (head + 1) * VEC)
        top = jnp.max(dots, axis=0, keepdims=True)
        if not first:
            old_top = state_in[1][head : head + 1, :]
            top = jnp.maximum(top, old_top)
        exps = jnp.exp2((dots - top) * scale)
        total = jnp.sum(exps, axis=0, keepdims=True)
        acc = jnp.dot(v_ref[rows, :], exps.astype(BF16), preferred_element_type=F32)
        if not first:
            shrink = jnp.exp2((old_top - top) * scale)
            total = total + state_in[2][head : head + 1, :] * shrink
            acc = acc + state_in[0][rows, :] * shrink
        if not last:
            outs[0][rows, :] = acc
            outs[1][head : head + 1, :] = top
            outs[2][head : head + 1, :] = total
        else:
            out = (acc * (1.0 / total)).astype(BF16)
            row = half * PACK + h * VEC
            for k in range(4):
                outs[0][k, row : row + VEC, :] = out[:, k * 128 : (k + 1) * 128]
            lses.append(top * (1.0 / math.sqrt(HEAD_DIM)) + jnp.log(total))
            if h == HALF - 1:
                packed = pack_lse(lses, out.shape[1])
                for k in range(4):
                    outs[0][k, half * PACK + ROWS : (half + 1) * PACK, :] = packed[:, k * 128 : (k + 1) * 128]
                lses = []
        dots = following


def attend(queries, values, state, keys):
    n = queries.shape[0]
    first, last = state is None, len(keys) == 2
    if last:
        out = jax.ShapeDtypeStruct((4, 2 * PACK, n // 4), BF16)
    else:
        rows = jax.ShapeDtypeStruct((8, n), F32)
        out = (jax.ShapeDtypeStruct((2 * ROWS, n), F32), rows, rows)
    return pl.pallas_call(
        functools.partial(attend_kernel, first, last),
        out_shape=out,
        cost_estimate=cost(
            4 * n * KEYS * HEAD_DIM * HEADS_HERE, 4 * n * 768 + 4 * KEYS * 768, n * KEYS * HEADS_HERE
        ),
        name="attend",
    )(queries, values, *(() if first else state), *keys)


def merge(parts_of):
    blocks = [p(ROWS, PACK).astype(F32) for p in parts_of]
    outs, lses = [], []
    for h in range(HALF):
        parts = [
            b[h : h + 1] + b[HALF + h : HALF + h + 1] + b[2 * HALF + h : 2 * HALF + h + 1] for b in blocks
        ]
        top = functools.reduce(jnp.maximum, parts)
        weights = [jnp.exp(p - top) for p in parts]
        total = sum(weights)
        inverse = 1.0 / total
        acc = 0.0
        for p, w in zip(parts_of, weights):
            acc = acc + p(h * VEC, (h + 1) * VEC).astype(F32) * (w * inverse)
        outs.append(acc)
        lses.append(top + jnp.log(total))
    return outs, lses


def merge_second_kernel(p_ref, o_ref):
    for base in (0, PACK):
        outs, lses = merge([lambda a, b, k=k: p_ref[k, base + a : base + b, :] for k in range(4)])
        packed = pack_lse(lses, 128)
        for k in range(4):
            for h in range(HALF):
                o_ref[k, base + h * VEC : base + (h + 1) * VEC, :] = outs[h].astype(BF16)
            o_ref[k, base + ROWS : base + PACK, :] = packed


def merge_second(parts):
    return pl.pallas_call(
        merge_second_kernel,
        out_shape=jax.ShapeDtypeStruct((4, 2 * PACK, 128), BF16),
        cost_estimate=cost(8 * PACK * 128 * 2, 16 * PACK * 128 * 2),
        name="merge_second",
    )(parts)


def merge_last_kernel(p_ref, o_ref):
    outs = []
    for base in (0, PACK):
        outs += merge([lambda a, b, k=k: p_ref[k, base + a : base + b, :] for k in range(4)])[0]
    o_ref[...] = sum(outs[1:], outs[0])


def merge_last(parts):
    return pl.pallas_call(
        merge_last_kernel,
        out_shape=jax.ShapeDtypeStruct((VEC, 128), F32),
        cost_estimate=cost(8 * PACK * 128 * 2, 10 * PACK * 128),
        name="merge_last",
    )(parts)


def decode_kernel(refresh_ref, me_ref, level_ref, v_ref, base_ref, up_ref, down_ref, w_ref, b_ref, o_ref, all_ref):
    level, me = level_ref[0], me_ref[0]
    all_ref[...] = v_ref[...].astype(F32)
    row = lax.broadcasted_iota(jnp.int32, (512, 128), 0)
    col = lax.broadcasted_iota(jnp.int32, (512, 128), 1)
    lane = row % 128
    target = (row // 256) * 64 + ((lane // 32) * 8 + lane % 8) * 2 + (row // 128) % 2

    def attention_rows(near, kinds):
        slot, on = 0, 0
        for s in range(SLOTS):
            hit = refresh_ref[s] == me + near
            slot = jnp.where(hit, s, slot)
            on = jnp.where(hit, 1, on)
        choose = (((lane // 8) % 4 == slot) & (target == col)).astype(F32).astype(BF16)
        count = LAT_CH * len(kinds)
        stacked = []
        for ys in range(4):
            for pair in range(2):
                pieces = []
                for xs in (pair * 2, pair * 2 + 1):
                    for b in range(2):
                        parts = [all_ref[ys * 4 + xs, pl.ds(kind * 2 + b, LAT_CH, 4), :] for kind in kinds]
                        pieces.append(jnp.concatenate(parts, axis=0))
                stacked.append(jnp.concatenate(pieces, axis=1))
        left = jnp.concatenate(stacked, axis=0).astype(BF16)
        field = jnp.dot(left, choose, preferred_element_type=F32)
        field = jnp.concatenate([field[i * count : (i + 1) * count] for i in range(8)], axis=1)
        return jnp.where(on > 0, field, 0.0)

    own = base_ref[...] - level * attention_rows(0, (0, 1))
    up = up_ref[...] - level * attention_rows(-1, (1,))
    down = down_ref[...] - level * attention_rows(1, (0,))
    latent = jnp.concatenate([up, own, down], axis=0) / 0.3611 + 0.1159
    line = lax.broadcasted_iota(jnp.int32, latent.shape, 0)
    column = lax.broadcasted_iota(jnp.int32, latent.shape, 1)
    inside = ((line >= 16) | (me > 0)) & ((line < 48) | (me < PATCHES - 1))
    latent = jnp.where(inside, latent, 0.0)
    before = jnp.where(column == 0, 0.0, pltpu.roll(latent, 1, 1)).astype(BF16)
    after = jnp.where(column == COLS - 1, 0.0, pltpu.roll(latent, COLS - 1, 1)).astype(BF16)
    middle = latent.astype(BF16)

    channels = w_ref.shape[3]
    line = lax.broadcasted_iota(jnp.int32, (16, channels), 0)
    bias = jnp.broadcast_to(b_ref[...], (16, channels))
    high = bias.astype(BF16).astype(F32)
    mid = (bias - high).astype(BF16).astype(F32)
    bias = jnp.where(line == 0, high, jnp.where(line == 1, mid, jnp.where(line == 2, bias - high - mid, 0.0)))
    weight = [w_ref[u, v] for v in range(3) for u in range(3)] + [bias.astype(BF16)]
    weight = jnp.concatenate(weight, axis=0)
    ones = jnp.ones((16, COLS), BF16)
    for r in range(2):
        stencil = [s[r * 16 : r * 16 + 48] for s in (before, middle, after)] + [ones]
        out = lax.dot_general(
            weight, jnp.concatenate(stencil, axis=0), (((0,), (0,)), ((), ())), preferred_element_type=F32
        )
        o_ref[r] = out.astype(BF16)


def decode(refresh, me, level, gathered, base, up, down, weight, bias):
    return pl.pallas_call(
        decode_kernel,
        out_shape=jax.ShapeDtypeStruct((2, weight.shape[3], COLS), BF16),
        in_specs=[SMEM] * 3 + [VMEM] * 6,
        out_specs=VMEM,
        scratch_shapes=[pltpu.VMEM((16, VEC, 128), F32)],
        cost_estimate=cost(4 * 128 * 160 * 1024, 2 << 20),
        name="decode",
    )(refresh, me, level, gathered, base, up, down, weight, bias)


def on_device(
    fresh_qkv,
    kv_cache,
    hidden,
    refresh,
    out_weight,
    final_weight,
    final_bias,
    gate_scale,
    noise_level,
    noisy_latent,
    velocity_cache,
    conv_weight,
    conv_bias,
):
    me = lax.axis_index(PATCH).astype(jnp.int32)
    here = me.reshape(1)
    together = lax.optimization_barrier

    with jax.named_scope("queries"):
        own = fresh_qkv[:, 0].reshape(PATCHES, CHUNK, -1)
        own, fresh_qkv = together((own, fresh_qkv))
        got = exchange(own, PATCH)

    with jax.named_scope("keys_values"):
        refreshed = jnp.any(refresh == me)
        keys = jnp.where(refreshed, fresh_qkv[:, 1], kv_cache[:, 0])
        value_rows = jnp.where(refreshed, fresh_qkv[:, 2], kv_cache[:, 1])
        gated = final_weight.T.astype(F32) * gate_scale[None, :]
        high = lax.reduce_precision(gated, 8, 7)
        both = jnp.concatenate([high, gated - high], axis=0).astype(BF16)
        mixed = lax.dot_general(both, out_weight, (((1,), (1,)), ((), ())), preferred_element_type=F32)
        values = project_values(value_rows, mixed[:VEC] + mixed[VEC:])

    with jax.named_scope("latent_base"):
        plain = lax.dot_general(
            final_weight, hidden, (((0,), (1,)), ((), ())), preferred_element_type=F32
        )
        plain = plain + final_bias[:, None]
        base, edge_first, edge_last = latent_base(
            refresh, here, noise_level, plain, noisy_latent, velocity_cache
        )

    with jax.named_scope("queries"):
        got, keys, values, base, edge_first, edge_last = together(
            (got, keys, values, base, edge_first, edge_last)
        )
        held = exchange(select(refresh, got), ("yl", "xl", "z"))

    with jax.named_scope("keys_values"):
        keys_x, keys_y = mirror(keys, 0, 1), mirror(keys, 1, 0)
        values_x, values_y, values_far = mirror(values, 0, 1), mirror(values, 1, 0), mirror(values, 1, 1)

    with jax.named_scope("attention"):
        queries = held.reshape(16 * SLOTS * CHUNK, HEADS_HERE * HEAD_DIM)
        state = attend(queries, values, None, (keys,))
        keys_x, keys_y, state = together((keys_x, keys_y, state))
        far_a, far_b = halves(keys_x, keys_y)
        far_a, far_b = mirror(far_a, 1, 0), mirror(far_b, 0, 1)
        state = attend(queries, values_x, state, (keys_x,))
        values_y, state = together((values_y, state))
        state = attend(queries, values_y, state, (keys_y,))
        values_far, far_a, far_b, state = together((values_far, far_a, far_b, state))
        state = attend(queries, values_far, state, (far_a, far_b))
        part = merge_second(exchange(state, ("yl", "xl")))
        parts = exchange(part, "z")

    with jax.named_scope("velocity"):
        term = merge_last(parts)
        term = jnp.sum(lax.all_gather(term, HEAD), axis=0).astype(BF16)
        term, edge_first, edge_last = together((term, edge_first, edge_last))
        up = lax.ppermute(edge_last, PATCH, [(p, p + 1) for p in range(PATCHES - 1)])
        down = lax.ppermute(edge_first, PATCH, [(p + 1, p) for p in range(PATCHES - 1)])
        gathered = exchange(spread_out(term, 16), ("yh", "yl", "xh", "xl"))

    with jax.named_scope("decode"):
        weight = conv_weight.transpose(1, 2, 3, 0)
        return decode(
            refresh, here, noise_level, gathered, base, up, down, weight, conv_bias.reshape(1, -1)
        )


def solution(mesh):
    wide = Mesh(mesh.devices.reshape(2, 2, 2, 2, 4, 2, 2), PATCH + HEAD)
    return jax.shard_map(
        on_device,
        mesh=wide,
        in_specs=(
            P(PATCH, None, HEAD),
            P(PATCH, None, HEAD),
            P(PATCH, None),
            P(),
            P(HEAD, None),
            P(),
            P(),
            P(),
            P(),
            P(PATCH, None, None),
            P(PATCH, None, None),
            P(HEAD, None, None, None),
            P(HEAD),
        ),
        out_specs=P(PATCH, HEAD, None),
        check_vma=False,
    )
```

```python
import functools
import math

import jax
import jax.numpy as jnp
from jax import lax
from jax.experimental import pallas as pl
from jax.experimental.pallas import tpu as pltpu
from jax.sharding import Mesh
from jax.sharding import PartitionSpec as P

HEAD_DIM = 128
LAT_CH = 16
PATCHES = 64
SLOTS = 4
HEADS_HERE = 6
HALF = 3
VEC = 64
ROWS = HALF * VEC
PACK = ROWS + 16
KEYS = 512
COLS = 1024
CHUNK = 8
F32 = jnp.float32
BF16 = jnp.bfloat16
PATCH = ("yh", "yl", "xh", "xl", "z")
HEAD = ("w", "c")


def mirror(value, flip_y, flip_x):
    pairs = []
    for p in range(PATCHES):
        y, x, z = p // 16, (p // 4) % 4, p % 4
        pairs.append((p, (3 - y if flip_y else y) * 16 + (3 - x if flip_x else x) * 4 + z))
    return lax.ppermute(value, PATCH, pairs)


def spread_out(value, count):
    return jnp.broadcast_to(value[None], (count,) + value.shape)


def exchange(value, axis):
    return lax.all_to_all(value, axis, 0, 0)


def cost(flops, moved_bytes, exps=0):
    return pl.CostEstimate(flops=flops, bytes_accessed=moved_bytes, transcendentals=exps)


SMEM = pl.BlockSpec(memory_space=pltpu.SMEM)
VMEM = pl.BlockSpec(memory_space=pltpu.VMEM)


def split(value):
    high = value.astype(BF16)
    return high, (value - high.astype(F32)).astype(BF16)


def select_kernel(refresh_ref, got_ref, o_ref):
    for slot in range(SLOTS):
        rows = got_ref[refresh_ref[slot]]
        for k in range(o_ref.shape[0]):
            o_ref[k, slot * CHUNK : (slot + 1) * CHUNK, :] = rows


def select(refresh, got):
    width = got.shape[2]
    return pl.pallas_call(
        select_kernel,
        in_specs=[SMEM, VMEM],
        out_shape=jax.ShapeDtypeStruct((16, SLOTS * CHUNK, width), BF16),
        cost_estimate=cost(0, 17 * SLOTS * CHUNK * width * 2),
        name="select",
    )(refresh, got)


def values_kernel(v_ref, w_ref, o_ref):
    for h in range(HEADS_HERE):
        cols = slice(h * HEAD_DIM, (h + 1) * HEAD_DIM)
        left = jnp.concatenate(split(w_ref[:, cols]), axis=0)
        both = lax.dot_general(
            left, v_ref[:, cols], (((1,), (1,)), ((), ())), preferred_element_type=F32
        )
        o_ref[h * VEC : (h + 1) * VEC, :] = (both[:VEC] + both[VEC:]).astype(BF16)


def project_values(value_rows, mixed):
    return pl.pallas_call(
        values_kernel,
        out_shape=jax.ShapeDtypeStruct((HEADS_HERE * VEC, KEYS), BF16),
        cost_estimate=cost(4 * KEYS * VEC * HEAD_DIM * HEADS_HERE, 4 * KEYS * 768),
        name="values",
    )(value_rows, mixed)


def halves_kernel(x_ref, y_ref, a_ref, b_ref):
    a_ref[...] = x_ref[...]
    b_ref[...] = y_ref[...]


def halves(keys_x, keys_y):
    block = (KEYS // 2, keys_x.shape[1])
    whole = pl.BlockSpec(block, lambda i: (0, 0))
    return pl.pallas_call(
        halves_kernel,
        grid=(1,),
        in_specs=[whole, pl.BlockSpec(block, lambda i: (1, 0))],
        out_specs=(whole, whole),
        out_shape=(jax.ShapeDtypeStruct(block, BF16),) * 2,
        cost_estimate=cost(0, 2 * KEYS * keys_x.shape[1] * 2),
        name="halves",
    )(keys_x, keys_y)


def base_kernel(refresh_ref, me_ref, level_ref, plain_ref, noisy_ref, cache_ref, o_ref, *rest):
    first_ref, last_ref, block_ref = rest
    row = lax.broadcasted_iota(jnp.int32, (256, 256), 0)
    col = lax.broadcasted_iota(jnp.int32, (256, 256), 1)
    choose = ((row % 128) * 2 + row // 128 == col).astype(F32).astype(BF16)
    stacked = []
    for i in range(4):
        block_ref[i] = plain_ref[:, i * 128 : (i + 1) * 128]
        pieces = []
        for b in range(2):
            parts = [block_ref[i, pl.ds(a * 2 + b, LAT_CH, 4), :] for a in range(2)]
            pieces.append(jnp.concatenate(parts, axis=0))
        stacked.append(jnp.concatenate(pieces, axis=1))
    left = jnp.concatenate(stacked, axis=0)
    high, rest = left.astype(BF16), left - left.astype(BF16).astype(F32)
    mid, low = split(rest)
    field = sum(jnp.dot(part, choose, preferred_element_type=F32) for part in (high, mid, low))
    field = jnp.concatenate([field[i * 32 : (i + 1) * 32] for i in range(4)], axis=1)
    fresh = False
    for slot in range(SLOTS):
        fresh = fresh | (refresh_ref[slot] == me_ref[0])
    level = level_ref[0]
    for a in range(2):
        rows = slice(a * LAT_CH, (a + 1) * LAT_CH)
        velocity = jnp.where(fresh, field[rows], cache_ref[a].astype(F32))
        latent = noisy_ref[a].astype(F32) - level * velocity
        o_ref[rows, :] = latent
        (first_ref, last_ref)[a][...] = latent


def latent_base(refresh, me, level, plain, noisy, cache):
    edge = jax.ShapeDtypeStruct((LAT_CH, COLS), F32)
    return pl.pallas_call(
        base_kernel,
        in_specs=[SMEM] * 3 + [VMEM] * 3,
        out_shape=(jax.ShapeDtypeStruct((2 * LAT_CH, COLS), F32), edge, edge),
        scratch_shapes=[pltpu.VMEM((4, VEC, 128), F32)],
        cost_estimate=cost(6 * 128 * 256 * 256, 1 << 19),
        name="latent_base",
    )(refresh, me, level, plain, noisy, cache)


def pack_lse(entries, width):
    row = lax.broadcasted_iota(jnp.int32, (16, width), 0)
    block = jnp.zeros((16, width), F32)
    for h, lse in enumerate(entries):
        high = lse.astype(BF16).astype(F32)
        rest = lse - high
        mid = rest.astype(BF16).astype(F32)
        low = rest - mid
        for part, value in enumerate((high, mid, low)):
            block = jnp.where(row == part * HALF + h, jnp.broadcast_to(value, block.shape), block)
    return block.astype(BF16)


def attend_kernel(first, last, *refs):
    q_ref, v_ref, state_in, outs = refs[0], refs[1], None, refs[2:]
    if not first:
        state_in, outs = outs[:3], outs[3:]
    k_refs, outs = outs[: 2 if last else 1], outs[2 if last else 1 :]
    scale = math.log2(math.e) / math.sqrt(HEAD_DIM)

    def scores(head):
        cols = slice(head * HEAD_DIM, (head + 1) * HEAD_DIM)
        keys = [k[:, cols] for k in k_refs]
        keys = keys[0] if len(keys) == 1 else jnp.concatenate(keys, axis=0)
        return lax.dot_general(
            keys, q_ref[:, cols], (((1,), (1,)), ((), ())), preferred_element_type=F32
        )

    dots, lses = scores(0), []
    for head in range(HEADS_HERE):
        half, h = divmod(head, HALF)
        following = scores(head + 1) if head + 1 < HEADS_HERE else None
        rows = slice(head * VEC, (head + 1) * VEC)
        top = jnp.max(dots, axis=0, keepdims=True)
        if not first:
            old_top = state_in[1][head : head + 1, :]
            top = jnp.maximum(top, old_top)
        exps = jnp.exp2((dots - top) * scale)
        total = jnp.sum(exps, axis=0, keepdims=True)
        acc = jnp.dot(v_ref[rows, :], exps.astype(BF16), preferred_element_type=F32)
        if not first:
            shrink = jnp.exp2((old_top - top) * scale)
            total = total + state_in[2][head : head + 1, :] * shrink
            acc = acc + state_in[0][rows, :] * shrink
        if not last:
            outs[0][rows, :] = acc
            outs[1][head : head + 1, :] = top
            outs[2][head : head + 1, :] = total
        else:
            out = (acc * (1.0 / total)).astype(BF16)
            row = half * PACK + h * VEC
            for k in range(4):
                outs[0][k, row : row + VEC, :] = out[:, k * 128 : (k + 1) * 128]
            lses.append(top * (1.0 / math.sqrt(HEAD_DIM)) + jnp.log(total))
            if h == HALF - 1:
                packed = pack_lse(lses, out.shape[1])
                for k in range(4):
                    outs[0][k, half * PACK + ROWS : (half + 1) * PACK, :] = packed[:, k * 128 : (k + 1) * 128]
                lses = []
        dots = following


def attend(queries, values, state, keys):
    n = queries.shape[0]
    first, last = state is None, len(keys) == 2
    if last:
        out = jax.ShapeDtypeStruct((4, 2 * PACK, n // 4), BF16)
    else:
        rows = jax.ShapeDtypeStruct((8, n), F32)
        out = (jax.ShapeDtypeStruct((2 * ROWS, n), F32), rows, rows)
    return pl.pallas_call(
        functools.partial(attend_kernel, first, last),
        out_shape=out,
        cost_estimate=cost(
            4 * n * KEYS * HEAD_DIM * HEADS_HERE, 4 * n * 768 + 4 * KEYS * 768, n * KEYS * HEADS_HERE
        ),
        name="attend",
    )(queries, values, *(() if first else state), *keys)


def merge(parts_of):
    blocks = [p(ROWS, PACK).astype(F32) for p in parts_of]
    outs, lses = [], []
    for h in range(HALF):
        parts = [
            b[h : h + 1] + b[HALF + h : HALF + h + 1] + b[2 * HALF + h : 2 * HALF + h + 1] for b in blocks
        ]
        top = functools.reduce(jnp.maximum, parts)
        weights = [jnp.exp(p - top) for p in parts]
        total = sum(weights)
        inverse = 1.0 / total
        acc = 0.0
        for p, w in zip(parts_of, weights):
            acc = acc + p(h * VEC, (h + 1) * VEC).astype(F32) * (w * inverse)
        outs.append(acc)
        lses.append(top + jnp.log(total))
    return outs, lses


def merge_second_kernel(p_ref, o_ref):
    for base in (0, PACK):
        outs, lses = merge([lambda a, b, k=k: p_ref[k, base + a : base + b, :] for k in range(4)])
        packed = pack_lse(lses, 128)
        for k in range(4):
            for h in range(HALF):
                o_ref[k, base + h * VEC : base + (h + 1) * VEC, :] = outs[h].astype(BF16)
            o_ref[k, base + ROWS : base + PACK, :] = packed


def merge_second(parts):
    return pl.pallas_call(
        merge_second_kernel,
        out_shape=jax.ShapeDtypeStruct((4, 2 * PACK, 128), BF16),
        cost_estimate=cost(8 * PACK * 128 * 2, 16 * PACK * 128 * 2),
        name="merge_second",
    )(parts)


def merge_last_kernel(p_ref, o_ref):
    outs = []
    for base in (0, PACK):
        outs += merge([lambda a, b, k=k: p_ref[k, base + a : base + b, :] for k in range(4)])[0]
    o_ref[...] = sum(outs[1:], outs[0])


def merge_last(parts):
    return pl.pallas_call(
        merge_last_kernel,
        out_shape=jax.ShapeDtypeStruct((VEC, 128), F32),
        cost_estimate=cost(8 * PACK * 128 * 2, 10 * PACK * 128),
        name="merge_last",
    )(parts)


def decode_kernel(refresh_ref, me_ref, level_ref, v_ref, base_ref, up_ref, down_ref, w_ref, b_ref, o_ref, all_ref):
    level, me = level_ref[0], me_ref[0]
    all_ref[...] = v_ref[...].astype(F32)
    row = lax.broadcasted_iota(jnp.int32, (512, 128), 0)
    col = lax.broadcasted_iota(jnp.int32, (512, 128), 1)
    lane = row % 128
    target = (row // 256) * 64 + ((lane // 32) * 8 + lane % 8) * 2 + (row // 128) % 2

    def attention_rows(near, kinds):
        slot, on = 0, 0
        for s in range(SLOTS):
            hit = refresh_ref[s] == me + near
            slot = jnp.where(hit, s, slot)
            on = jnp.where(hit, 1, on)
        choose = (((lane // 8) % 4 == slot) & (target == col)).astype(F32).astype(BF16)
        count = LAT_CH * len(kinds)
        stacked = []
        for ys in range(4):
            for pair in range(2):
                pieces = []
                for xs in (pair * 2, pair * 2 + 1):
                    for b in range(2):
                        parts = [all_ref[ys * 4 + xs, pl.ds(kind * 2 + b, LAT_CH, 4), :] for kind in kinds]
                        pieces.append(jnp.concatenate(parts, axis=0))
                stacked.append(jnp.concatenate(pieces, axis=1))
        left = jnp.concatenate(stacked, axis=0).astype(BF16)
        field = jnp.dot(left, choose, preferred_element_type=F32)
        field = jnp.concatenate([field[i * count : (i + 1) * count] for i in range(8)], axis=1)
        return jnp.where(on > 0, field, 0.0)

    own = base_ref[...] - level * attention_rows(0, (0, 1))
    up = up_ref[...] - level * attention_rows(-1, (1,))
    down = down_ref[...] - level * attention_rows(1, (0,))
    latent = jnp.concatenate([up, own, down], axis=0) / 0.3611 + 0.1159
    line = lax.broadcasted_iota(jnp.int32, latent.shape, 0)
    column = lax.broadcasted_iota(jnp.int32, latent.shape, 1)
    inside = ((line >= 16) | (me > 0)) & ((line < 48) | (me < PATCHES - 1))
    latent = jnp.where(inside, latent, 0.0)
    before = jnp.where(column == 0, 0.0, pltpu.roll(latent, 1, 1)).astype(BF16)
    after = jnp.where(column == COLS - 1, 0.0, pltpu.roll(latent, COLS - 1, 1)).astype(BF16)
    middle = latent.astype(BF16)

    channels = w_ref.shape[3]
    line = lax.broadcasted_iota(jnp.int32, (16, channels), 0)
    bias = jnp.broadcast_to(b_ref[...], (16, channels))
    high = bias.astype(BF16).astype(F32)
    mid = (bias - high).astype(BF16).astype(F32)
    bias = jnp.where(line == 0, high, jnp.where(line == 1, mid, jnp.where(line == 2, bias - high - mid, 0.0)))
    weight = [w_ref[u, v] for v in range(3) for u in range(3)] + [bias.astype(BF16)]
    weight = jnp.concatenate(weight, axis=0)
    ones = jnp.ones((16, COLS), BF16)
    for r in range(2):
        stencil = [s[r * 16 : r * 16 + 48] for s in (before, middle, after)] + [ones]
        out = lax.dot_general(
            weight, jnp.concatenate(stencil, axis=0), (((0,), (0,)), ((), ())), preferred_element_type=F32
        )
        o_ref[r] = out.astype(BF16)


def decode(refresh, me, level, gathered, base, up, down, weight, bias):
    return pl.pallas_call(
        decode_kernel,
        out_shape=jax.ShapeDtypeStruct((2, weight.shape[3], COLS), BF16),
        in_specs=[SMEM] * 3 + [VMEM] * 6,
        out_specs=VMEM,
        scratch_shapes=[pltpu.VMEM((16, VEC, 128), F32)],
        cost_estimate=cost(4 * 128 * 160 * 1024, 2 << 20),
        name="decode",
    )(refresh, me, level, gathered, base, up, down, weight, bias)


def on_device(
    fresh_qkv,
    kv_cache,
    hidden,
    refresh,
    out_weight,
    final_weight,
    final_bias,
    gate_scale,
    noise_level,
    noisy_latent,
    velocity_cache,
    conv_weight,
    conv_bias,
):
    me = lax.axis_index(PATCH).astype(jnp.int32)
    here = me.reshape(1)
    together = lax.optimization_barrier

    with jax.named_scope("queries"):
        own = fresh_qkv[:, 0].reshape(PATCHES, CHUNK, -1)
        own, fresh_qkv = together((own, fresh_qkv))
        got = exchange(own, PATCH)

    with jax.named_scope("keys_values"):
        refreshed = jnp.any(refresh == me)
        keys = jnp.where(refreshed, fresh_qkv[:, 1], kv_cache[:, 0])
        value_rows = jnp.where(refreshed, fresh_qkv[:, 2], kv_cache[:, 1])

    with jax.named_scope("latent_base"):
        plain = lax.dot_general(
            final_weight, hidden, (((0,), (1,)), ((), ())), preferred_element_type=F32
        )
        plain = plain + final_bias[:, None]
        base, edge_first, edge_last = latent_base(
            refresh, here, noise_level, plain, noisy_latent, velocity_cache
        )
        up = lax.ppermute(edge_last, PATCH, [(p, p + 1) for p in range(PATCHES - 1)])
        down = lax.ppermute(edge_first, PATCH, [(p + 1, p) for p in range(PATCHES - 1)])

    with jax.named_scope("queries"):
        got, base, up, down, _, _ = together((got, base, up, down, keys, value_rows))
        held = exchange(select(refresh, got), ("yl", "xl", "z"))

    with jax.named_scope("keys_values"):
        keys_x, keys_y = mirror(keys, 0, 1), mirror(keys, 1, 0)
        gated = final_weight.T.astype(F32) * gate_scale[None, :]
        high = lax.reduce_precision(gated, 8, 7)
        both = jnp.concatenate([high, gated - high], axis=0).astype(BF16)
        mixed = lax.dot_general(both, out_weight, (((1,), (1,)), ((), ())), preferred_element_type=F32)
        values = project_values(value_rows, mixed[:VEC] + mixed[VEC:])
        values_x, values_y, values_far = mirror(values, 0, 1), mirror(values, 1, 0), mirror(values, 1, 1)

    with jax.named_scope("attention"):
        queries = held.reshape(16 * SLOTS * CHUNK, HEADS_HERE * HEAD_DIM)
        state = attend(queries, values, None, (keys,))
        keys_x, keys_y, state = together((keys_x, keys_y, state))
        far_a, far_b = halves(keys_x, keys_y)
        far_a, far_b = mirror(far_a, 1, 0), mirror(far_b, 0, 1)
        state = attend(queries, values_x, state, (keys_x,))
        values_y, state = together((values_y, state))
        state = attend(queries, values_y, state, (keys_y,))
        values_far, far_a, far_b, state = together((values_far, far_a, far_b, state))
        state = attend(queries, values_far, state, (far_a, far_b))
        part = merge_second(exchange(state, ("yl", "xl")))
        parts = exchange(part, "z")

    with jax.named_scope("velocity"):
        term = merge_last(parts)
        term = jnp.sum(lax.all_gather(term, HEAD), axis=0).astype(BF16)
        gathered = exchange(spread_out(term, 16), ("yh", "yl", "xh", "xl"))

    with jax.named_scope("decode"):
        weight = conv_weight.transpose(1, 2, 3, 0)
        return decode(
            refresh, here, noise_level, gathered, base, up, down, weight, conv_bias.reshape(1, -1)
        )


def solution(mesh):
    wide = Mesh(mesh.devices.reshape(2, 2, 2, 2, 4, 2, 2), PATCH + HEAD)
    return jax.shard_map(
        on_device,
        mesh=wide,
        in_specs=(
            P(PATCH, None, HEAD),
            P(PATCH, None, HEAD),
            P(PATCH, None),
            P(),
            P(HEAD, None),
            P(),
            P(),
            P(),
            P(),
            P(PATCH, None, None),
            P(PATCH, None, None),
            P(HEAD, None, None, None),
            P(HEAD),
        ),
        out_specs=P(PATCH, HEAD, None),
        check_vma=False,
    )
```

```python
import functools
import math

import jax
import jax.numpy as jnp
from jax import lax
from jax.experimental import pallas as pl
from jax.experimental.pallas import tpu as pltpu
from jax.sharding import Mesh
from jax.sharding import PartitionSpec as P

HEAD_DIM = 128
LAT_CH = 16
PATCHES = 64
SLOTS = 4
HEADS_HERE = 6
HALF = 3
VEC = 64
ROWS = HALF * VEC
PACK = ROWS + 16
KEYS = 512
COLS = 1024
CHUNK = 8
F32 = jnp.float32
BF16 = jnp.bfloat16
PATCH = ("yh", "yl", "xh", "xl", "z")
HEAD = ("w", "c")


def mirror(value, flip_y, flip_x):
    pairs = []
    for p in range(PATCHES):
        y, x, z = p // 16, (p // 4) % 4, p % 4
        pairs.append((p, (3 - y if flip_y else y) * 16 + (3 - x if flip_x else x) * 4 + z))
    return lax.ppermute(value, PATCH, pairs)


def spread_out(value, count):
    return jnp.broadcast_to(value[None], (count,) + value.shape)


def exchange(value, axis):
    return lax.all_to_all(value, axis, 0, 0)


def cost(flops, moved_bytes, exps=0):
    return pl.CostEstimate(flops=flops, bytes_accessed=moved_bytes, transcendentals=exps)


SMEM = pl.BlockSpec(memory_space=pltpu.SMEM)
VMEM = pl.BlockSpec(memory_space=pltpu.VMEM)


def split(value):
    high = value.astype(BF16)
    return high, (value - high.astype(F32)).astype(BF16)


def select_kernel(refresh_ref, got_ref, o_ref):
    for slot in range(SLOTS):
        rows = got_ref[refresh_ref[slot]]
        for k in range(o_ref.shape[0]):
            o_ref[k, slot * CHUNK : (slot + 1) * CHUNK, :] = rows


def select(refresh, got):
    width = got.shape[2]
    return pl.pallas_call(
        select_kernel,
        in_specs=[SMEM, VMEM],
        out_shape=jax.ShapeDtypeStruct((16, SLOTS * CHUNK, width), BF16),
        cost_estimate=cost(0, 17 * SLOTS * CHUNK * width * 2),
        name="select",
    )(refresh, got)


def values_kernel(v_ref, w_ref, o_ref):
    for h in range(HEADS_HERE):
        cols = slice(h * HEAD_DIM, (h + 1) * HEAD_DIM)
        left = jnp.concatenate(split(w_ref[:, cols]), axis=0)
        both = lax.dot_general(
            left, v_ref[:, cols], (((1,), (1,)), ((), ())), preferred_element_type=F32
        )
        o_ref[h * VEC : (h + 1) * VEC, :] = (both[:VEC] + both[VEC:]).astype(BF16)


def project_values(value_rows, mixed):
    return pl.pallas_call(
        values_kernel,
        out_shape=jax.ShapeDtypeStruct((HEADS_HERE * VEC, KEYS), BF16),
        cost_estimate=cost(4 * KEYS * VEC * HEAD_DIM * HEADS_HERE, 4 * KEYS * 768),
        name="values",
    )(value_rows, mixed)


def halves_kernel(x_ref, y_ref, a_ref, b_ref):
    a_ref[...] = x_ref[...]
    b_ref[...] = y_ref[...]


def halves(keys_x, keys_y):
    block = (KEYS // 2, keys_x.shape[1])
    whole = pl.BlockSpec(block, lambda i: (0, 0))
    return pl.pallas_call(
        halves_kernel,
        grid=(1,),
        in_specs=[whole, pl.BlockSpec(block, lambda i: (1, 0))],
        out_specs=(whole, whole),
        out_shape=(jax.ShapeDtypeStruct(block, BF16),) * 2,
        cost_estimate=cost(0, 2 * KEYS * keys_x.shape[1] * 2),
        name="halves",
    )(keys_x, keys_y)


def base_kernel(refresh_ref, me_ref, level_ref, plain_ref, noisy_ref, cache_ref, o_ref, *rest):
    first_ref, last_ref, block_ref = rest
    row = lax.broadcasted_iota(jnp.int32, (256, 256), 0)
    col = lax.broadcasted_iota(jnp.int32, (256, 256), 1)
    choose = ((row % 128) * 2 + row // 128 == col).astype(F32).astype(BF16)
    stacked = []
    for i in range(4):
        block_ref[i] = plain_ref[:, i * 128 : (i + 1) * 128]
        pieces = []
        for b in range(2):
            parts = [block_ref[i, pl.ds(a * 2 + b, LAT_CH, 4), :] for a in range(2)]
            pieces.append(jnp.concatenate(parts, axis=0))
        stacked.append(jnp.concatenate(pieces, axis=1))
    left = jnp.concatenate(stacked, axis=0)
    high, rest = left.astype(BF16), left - left.astype(BF16).astype(F32)
    mid, low = split(rest)
    field = sum(jnp.dot(part, choose, preferred_element_type=F32) for part in (high, mid, low))
    field = jnp.concatenate([field[i * 32 : (i + 1) * 32] for i in range(4)], axis=1)
    fresh = False
    for slot in range(SLOTS):
        fresh = fresh | (refresh_ref[slot] == me_ref[0])
    level = level_ref[0]
    for a in range(2):
        rows = slice(a * LAT_CH, (a + 1) * LAT_CH)
        velocity = jnp.where(fresh, field[rows], cache_ref[a].astype(F32))
        latent = noisy_ref[a].astype(F32) - level * velocity
        o_ref[rows, :] = latent
        (first_ref, last_ref)[a][...] = latent


def latent_base(refresh, me, level, plain, noisy, cache):
    edge = jax.ShapeDtypeStruct((LAT_CH, COLS), F32)
    return pl.pallas_call(
        base_kernel,
        in_specs=[SMEM] * 3 + [VMEM] * 3,
        out_shape=(jax.ShapeDtypeStruct((2 * LAT_CH, COLS), F32), edge, edge),
        scratch_shapes=[pltpu.VMEM((4, VEC, 128), F32)],
        cost_estimate=cost(6 * 128 * 256 * 256, 1 << 19),
        name="latent_base",
    )(refresh, me, level, plain, noisy, cache)


def pack_lse(entries, width):
    row = lax.broadcasted_iota(jnp.int32, (16, width), 0)
    block = jnp.zeros((16, width), F32)
    for h, lse in enumerate(entries):
        high = lse.astype(BF16).astype(F32)
        rest = lse - high
        mid = rest.astype(BF16).astype(F32)
        low = rest - mid
        for part, value in enumerate((high, mid, low)):
            block = jnp.where(row == part * HALF + h, jnp.broadcast_to(value, block.shape), block)
    return block.astype(BF16)


def attend_kernel(first, last, *refs):
    q_ref, v_ref, state_in, outs = refs[0], refs[1], None, refs[2:]
    if not first:
        state_in, outs = outs[:3], outs[3:]
    k_refs, outs = outs[: 2 if last else 1], outs[2 if last else 1 :]
    scale = math.log2(math.e) / math.sqrt(HEAD_DIM)

    def scores(head):
        cols = slice(head * HEAD_DIM, (head + 1) * HEAD_DIM)
        keys = [k[:, cols] for k in k_refs]
        keys = keys[0] if len(keys) == 1 else jnp.concatenate(keys, axis=0)
        return lax.dot_general(
            keys, q_ref[:, cols], (((1,), (1,)), ((), ())), preferred_element_type=F32
        )

    dots, lses = scores(0), []
    for head in range(HEADS_HERE):
        half, h = divmod(head, HALF)
        following = scores(head + 1) if head + 1 < HEADS_HERE else None
        rows = slice(head * VEC, (head + 1) * VEC)
        top = jnp.max(dots, axis=0, keepdims=True)
        if not first:
            old_top = state_in[1][head : head + 1, :]
            top = jnp.maximum(top, old_top)
        exps = jnp.exp2((dots - top) * scale)
        total = jnp.sum(exps, axis=0, keepdims=True)
        acc = jnp.dot(v_ref[rows, :], exps.astype(BF16), preferred_element_type=F32)
        if not first:
            shrink = jnp.exp2((old_top - top) * scale)
            total = total + state_in[2][head : head + 1, :] * shrink
            acc = acc + state_in[0][rows, :] * shrink
        if not last:
            outs[0][rows, :] = acc
            outs[1][head : head + 1, :] = top
            outs[2][head : head + 1, :] = total
        else:
            out = (acc * (1.0 / total)).astype(BF16)
            row = half * PACK + h * VEC
            for k in range(4):
                outs[0][k, row : row + VEC, :] = out[:, k * 128 : (k + 1) * 128]
            lses.append(top * (1.0 / math.sqrt(HEAD_DIM)) + jnp.log(total))
            if h == HALF - 1:
                packed = pack_lse(lses, out.shape[1])
                for k in range(4):
                    outs[0][k, half * PACK + ROWS : (half + 1) * PACK, :] = packed[:, k * 128 : (k + 1) * 128]
                lses = []
        dots = following


def attend(queries, values, state, keys):
    n = queries.shape[0]
    first, last = state is None, len(keys) == 2
    if last:
        out = jax.ShapeDtypeStruct((4, 2 * PACK, n // 4), BF16)
    else:
        rows = jax.ShapeDtypeStruct((8, n), F32)
        out = (jax.ShapeDtypeStruct((2 * ROWS, n), F32), rows, rows)
    return pl.pallas_call(
        functools.partial(attend_kernel, first, last),
        out_shape=out,
        cost_estimate=cost(
            4 * n * KEYS * HEAD_DIM * HEADS_HERE, 4 * n * 768 + 4 * KEYS * 768, n * KEYS * HEADS_HERE
        ),
        name="attend",
    )(queries, values, *(() if first else state), *keys)


def merge(parts_of):
    blocks = [p(ROWS, PACK).astype(F32) for p in parts_of]
    outs, lses = [], []
    for h in range(HALF):
        parts = [
            b[h : h + 1] + b[HALF + h : HALF + h + 1] + b[2 * HALF + h : 2 * HALF + h + 1] for b in blocks
        ]
        top = functools.reduce(jnp.maximum, parts)
        weights = [jnp.exp(p - top) for p in parts]
        total = sum(weights)
        inverse = 1.0 / total
        acc = 0.0
        for p, w in zip(parts_of, weights):
            acc = acc + p(h * VEC, (h + 1) * VEC).astype(F32) * (w * inverse)
        outs.append(acc)
        lses.append(top + jnp.log(total))
    return outs, lses


def merge_second_kernel(p_ref, o_ref):
    for base in (0, PACK):
        outs, lses = merge([lambda a, b, k=k: p_ref[k, base + a : base + b, :] for k in range(4)])
        packed = pack_lse(lses, 128)
        for h in range(HALF):
            o_ref[base + h * VEC : base + (h + 1) * VEC, :] = outs[h].astype(BF16)
        o_ref[base + ROWS : base + PACK, :] = packed


def merge_second(parts):
    return pl.pallas_call(
        merge_second_kernel,
        out_shape=jax.ShapeDtypeStruct((2 * PACK, 128), BF16),
        cost_estimate=cost(8 * PACK * 128 * 2, 10 * PACK * 128 * 2),
        name="merge_second",
    )(parts)


def merge_last_kernel(*refs):
    outs, o_ref = [], refs[4]
    for base in (0, PACK):
        outs += merge([lambda a, b, r=r: r[base + a : base + b, :] for r in refs[:4]])[0]
    o_ref[...] = sum(outs[1:], outs[0])


def merge_last(parts):
    return pl.pallas_call(
        merge_last_kernel,
        out_shape=jax.ShapeDtypeStruct((VEC, 128), F32),
        cost_estimate=cost(8 * PACK * 128 * 2, 10 * PACK * 128),
        name="merge_last",
    )(*parts)


def decode_kernel(refresh_ref, me_ref, level_ref, v_ref, base_ref, up_ref, down_ref, w_ref, b_ref, o_ref, all_ref):
    level, me = level_ref[0], me_ref[0]
    all_ref[...] = v_ref[...].astype(F32)
    row = lax.broadcasted_iota(jnp.int32, (512, 128), 0)
    col = lax.broadcasted_iota(jnp.int32, (512, 128), 1)
    lane = row % 128
    target = (row // 256) * 64 + ((lane // 32) * 8 + lane % 8) * 2 + (row // 128) % 2

    def attention_rows(near, kinds):
        slot, on = 0, 0
        for s in range(SLOTS):
            hit = refresh_ref[s] == me + near
            slot = jnp.where(hit, s, slot)
            on = jnp.where(hit, 1, on)
        choose = (((lane // 8) % 4 == slot) & (target == col)).astype(F32).astype(BF16)
        count = LAT_CH * len(kinds)
        stacked = []
        for ys in range(4):
            for pair in range(2):
                pieces = []
                for xs in (pair * 2, pair * 2 + 1):
                    for b in range(2):
                        parts = [all_ref[ys * 4 + xs, pl.ds(kind * 2 + b, LAT_CH, 4), :] for kind in kinds]
                        pieces.append(jnp.concatenate(parts, axis=0))
                stacked.append(jnp.concatenate(pieces, axis=1))
        left = jnp.concatenate(stacked, axis=0).astype(BF16)
        field = jnp.dot(left, choose, preferred_element_type=F32)
        field = jnp.concatenate([field[i * count : (i + 1) * count] for i in range(8)], axis=1)
        return jnp.where(on > 0, field, 0.0)

    own = base_ref[...] - level * attention_rows(0, (0, 1))
    up = up_ref[...] - level * attention_rows(-1, (1,))
    down = down_ref[...] - level * attention_rows(1, (0,))
    latent = jnp.concatenate([up, own, down], axis=0) / 0.3611 + 0.1159
    line = lax.broadcasted_iota(jnp.int32, latent.shape, 0)
    column = lax.broadcasted_iota(jnp.int32, latent.shape, 1)
    inside = ((line >= 16) | (me > 0)) & ((line < 48) | (me < PATCHES - 1))
    latent = jnp.where(inside, latent, 0.0)
    before = jnp.where(column == 0, 0.0, pltpu.roll(latent, 1, 1)).astype(BF16)
    after = jnp.where(column == COLS - 1, 0.0, pltpu.roll(latent, COLS - 1, 1)).astype(BF16)
    middle = latent.astype(BF16)

    channels = w_ref.shape[3]
    line = lax.broadcasted_iota(jnp.int32, (16, channels), 0)
    bias = jnp.broadcast_to(b_ref[...], (16, channels))
    high = bias.astype(BF16).astype(F32)
    mid = (bias - high).astype(BF16).astype(F32)
    bias = jnp.where(line == 0, high, jnp.where(line == 1, mid, jnp.where(line == 2, bias - high - mid, 0.0)))
    weight = [w_ref[u, v] for v in range(3) for u in range(3)] + [bias.astype(BF16)]
    weight = jnp.concatenate(weight, axis=0)
    ones = jnp.ones((16, COLS), BF16)
    for r in range(2):
        stencil = [s[r * 16 : r * 16 + 48] for s in (before, middle, after)] + [ones]
        out = lax.dot_general(
            weight, jnp.concatenate(stencil, axis=0), (((0,), (0,)), ((), ())), preferred_element_type=F32
        )
        o_ref[r] = out.astype(BF16)


def decode(refresh, me, level, gathered, base, up, down, weight, bias):
    return pl.pallas_call(
        decode_kernel,
        out_shape=jax.ShapeDtypeStruct((2, weight.shape[3], COLS), BF16),
        in_specs=[SMEM] * 3 + [VMEM] * 6,
        out_specs=VMEM,
        scratch_shapes=[pltpu.VMEM((16, VEC, 128), F32)],
        cost_estimate=cost(4 * 128 * 160 * 1024, 2 << 20),
        name="decode",
    )(refresh, me, level, gathered, base, up, down, weight, bias)


def on_device(
    fresh_qkv,
    kv_cache,
    hidden,
    refresh,
    out_weight,
    final_weight,
    final_bias,
    gate_scale,
    noise_level,
    noisy_latent,
    velocity_cache,
    conv_weight,
    conv_bias,
):
    me = lax.axis_index(PATCH).astype(jnp.int32)
    here = me.reshape(1)
    together = lax.optimization_barrier

    with jax.named_scope("queries"):
        own = fresh_qkv[:, 0].reshape(PATCHES, CHUNK, -1)
        own, fresh_qkv = together((own, fresh_qkv))
        got = exchange(own, PATCH)

    with jax.named_scope("keys_values"):
        refreshed = jnp.any(refresh == me)
        keys = jnp.where(refreshed, fresh_qkv[:, 1], kv_cache[:, 0])
        value_rows = jnp.where(refreshed, fresh_qkv[:, 2], kv_cache[:, 1])

    with jax.named_scope("latent_base"):
        plain = lax.dot_general(
            final_weight, hidden, (((0,), (1,)), ((), ())), preferred_element_type=F32
        )
        plain = plain + final_bias[:, None]
        base, edge_first, edge_last = latent_base(
            refresh, here, noise_level, plain, noisy_latent, velocity_cache
        )
        up = lax.ppermute(edge_last, PATCH, [(p, p + 1) for p in range(PATCHES - 1)])
        down = lax.ppermute(edge_first, PATCH, [(p + 1, p) for p in range(PATCHES - 1)])

    with jax.named_scope("queries"):
        got, base, up, down, _, _ = together((got, base, up, down, keys, value_rows))
        held = exchange(select(refresh, got), ("yl", "xl", "z"))

    with jax.named_scope("keys_values"):
        keys_x, keys_y = mirror(keys, 0, 1), mirror(keys, 1, 0)
        gated = final_weight.T.astype(F32) * gate_scale[None, :]
        high = lax.reduce_precision(gated, 8, 7)
        both = jnp.concatenate([high, gated - high], axis=0).astype(BF16)
        mixed = lax.dot_general(both, out_weight, (((1,), (1,)), ((), ())), preferred_element_type=F32)
        values = project_values(value_rows, mixed[:VEC] + mixed[VEC:])
        values_x, values_y, values_far = mirror(values, 0, 1), mirror(values, 1, 0), mirror(values, 1, 1)

    with jax.named_scope("attention"):
        queries = held.reshape(16 * SLOTS * CHUNK, HEADS_HERE * HEAD_DIM)
        state = attend(queries, values, None, (keys,))
        keys_x, keys_y, state = together((keys_x, keys_y, state))
        far_a, far_b = halves(keys_x, keys_y)
        far_a, far_b = mirror(far_a, 1, 0), mirror(far_b, 0, 1)
        state = attend(queries, values_x, state, (keys_x,))
        values_y, state = together((values_y, state))
        state = attend(queries, values_y, state, (keys_y,))
        values_far, far_a, far_b, state = together((values_far, far_a, far_b, state))
        state = attend(queries, values_far, state, (far_a, far_b))
        part = merge_second(exchange(state, ("yl", "xl")))
        parts = [part]
        for k in range(1, 4):
            parts.append(lax.ppermute(part, "z", [(i, (i + k) % 4) for i in range(4)]))

    with jax.named_scope("velocity"):
        term = merge_last(parts)
        term = jnp.sum(lax.all_gather(term, HEAD), axis=0).astype(BF16)
        gathered = exchange(spread_out(term, 16), ("yh", "yl", "xh", "xl"))

    with jax.named_scope("decode"):
        weight = conv_weight.transpose(1, 2, 3, 0)
        return decode(
            refresh, here, noise_level, gathered, base, up, down, weight, conv_bias.reshape(1, -1)
        )


def solution(mesh):
    wide = Mesh(mesh.devices.reshape(2, 2, 2, 2, 4, 2, 2), PATCH + HEAD)
    return jax.shard_map(
        on_device,
        mesh=wide,
        in_specs=(
            P(PATCH, None, HEAD),
            P(PATCH, None, HEAD),
            P(PATCH, None),
            P(),
            P(HEAD, None),
            P(),
            P(),
            P(),
            P(),
            P(PATCH, None, None),
            P(PATCH, None, None),
            P(HEAD, None, None, None),
            P(HEAD),
        ),
        out_specs=P(PATCH, HEAD, None),
        check_vma=False,
    )
```
